32 devices in a mesh: img: 8 (over z, y), seq: 4 (over x, core).
Axes of the slice: x: 2, y: 2, z: 4, core: 2. Of those that a mesh axis runs over, the one named last changes fastest.
Arguments:
- tokens: bfloat16 [8, 512, 1152], P('img', 'seq'), may hold values from -6 to 6
- counts: int32 [8, 4], P('img'), may hold values from 96 to 128, as said below
- w_qkv: bfloat16 [3981312], P(('img', 'seq')), may hold values from -1 to 1
- w_out: bfloat16 [1327104], P(('img', 'seq')), may hold values from -1.5 to 1.5
- w_fc1: bfloat16 [4958208], P(('img', 'seq')), may hold values from -0.1875 to 0.1875
- w_fc2: bfloat16 [4958208], P(('img', 'seq')), may hold values from -0.09375 to 0.09375
- vectors: bfloat16 [13536], P(('img', 'seq')), may hold values from -2 to 2
- cotangent: bfloat16 [8, 512, 1152], P('img', 'seq'), may hold values from -6 to 6
Outputs:
- output: bfloat16 [8, 512, 1152], P('img', 'seq')
- input_grad: float32 [8, 512, 1152], P('img', 'seq')
- grad_qkv: float32 [3981312], P(('img', 'seq'))
- grad_out: float32 [1327104], P(('img', 'seq'))
- grad_fc1: float32 [4958208], P(('img', 'seq'))
- grad_fc2: float32 [4958208], P(('img', 'seq'))
- grad_vectors: float32 [11232], P(('img', 'seq'))
- grad_front: float32 [2304], P(('img', 'seq'))
The draws below stay inside these ranges and needn't reach their ends.
Inputs may be any that keep to these rules, and one draw needn't show every extreme that they name: An image's counts come from one length L of 385 to 512 tokens: every slice gets L // 4 and the first L mod 4 slices one more; some image is full in every draw.
All inputs are finite; a program needn't handle non-finite values.
Results may differ from the reference program's by a relative error of at most 0.011.
Values may be sent and summed in bfloat16 or wider, within the bound.
A program may use at most 320 MiB of HBM per device.

```python
import jax
import jax.numpy as jnp
from jax import lax

D = 1152
HEADS = 16
HEAD_DIM = 72
FF = 4304
SLOT = 128
IMAGES = 8
VECS = 13536
N_SEQ = 4


def draw_counts(key, part):
    key_len = jax.random.fold_in(key, 11)
    key_full = jax.random.fold_in(key, 12)
    lengths = jax.random.randint(key_len, (IMAGES,), 3 * SLOT + 1, 4 * SLOT + 1)
    full_image = jax.random.randint(key_full, (), 0, IMAGES)
    lengths = jnp.where(jnp.arange(IMAGES) == full_image, 4 * SLOT, lengths)
    base = lengths // N_SEQ
    extra = lengths % N_SEQ
    result = base[:, None] + (jnp.arange(N_SEQ)[None, :] < extra[:, None]).astype(jnp.int32)
    return result.astype(jnp.int32)


def draw_w_qkv(key, part):
    key_base = jax.random.fold_in(key, 21)
    base = jnp.clip(jax.random.normal(key_base, (D, 3 * D), jnp.float32), -6.0, 6.0) / jnp.sqrt(jnp.float32(D))
    whole = base
    return jnp.clip(whole, -1.0, 1.0).reshape(-1).astype(jnp.bfloat16)


def draw_vectors(key, part):
    key_vals = jax.random.fold_in(key, 31)
    position = jnp.arange(VECS)
    block = position // D
    is_gain = (block == 2) | (block == 5)
    raw = jax.random.normal(key_vals, (VECS,), jnp.float32)
    values = jnp.where(is_gain, 1.0 + 0.1 * jnp.clip(raw, -3.0, 3.0), 0.5 * jnp.clip(raw, -4.0, 4.0))
    return values.astype(jnp.bfloat16)


def steps_of(stream_key, dims, cuts, least, largest):
    def one(dim, blocks):
        draws = jax.random.uniform(jax.random.fold_in(jax.random.fold_in(stream_key, 6), dim), (blocks,), jnp.float32, least / len(cuts), largest / len(cuts))
        return jnp.repeat(jnp.exp(draws), dims[dim] // blocks).reshape((-1,) + (1,) * (len(dims) - dim - 1))

    factor_of = one(*cuts[0])
    for cut in cuts[1:]:
        factor_of = factor_of * one(*cut)
    return factor_of


def noise(stream_key, extent, width, most, split=(), held_as=jnp.bfloat16):
    entries = width * jax.random.normal(stream_key, extent, jnp.float32)
    if split:
        entries = entries * steps_of(stream_key, extent, split, -0.22, 0.18)
    return jnp.clip(entries, -most, most).astype(held_as)


def setup_inputs(seed: int = 0) -> dict:
    streams_of = jax.random.split(jax.random.key(seed), 9)
    return {
        "tokens": noise(streams_of[0], (IMAGES, N_SEQ * SLOT, D), 1.0, 6.0, ((0, 8), (1, 4))),
        "counts": draw_counts(jax.random.fold_in(streams_of[8], 71), 0),
        "w_qkv": draw_w_qkv(jax.random.fold_in(streams_of[8], 71), 0),
        "w_out": noise(streams_of[3], (D * D,), (max(D * 8 // (N_SEQ * SLOT), 1)) ** -0.5, 1.5, ((0, 32),)),
        "w_fc1": noise(streams_of[4], (D * FF,), D ** -0.5, 0.1875, ((0, 32),)),
        "w_fc2": noise(streams_of[5], (FF * D,), FF ** -0.5, 0.09375, ((0, 32),)),
        "vectors": draw_vectors(jax.random.fold_in(streams_of[8], 71), 0),
        "cotangent": noise(streams_of[7], (IMAGES, N_SEQ * SLOT, D), 1.0, 6.0, ((0, 8), (1, 4))),
    }


EPS = 1e-06
GELU_C = 0.7978845608028654

def normalize(values):
    mean = lax.optimization_barrier(jnp.mean(values, axis=-1, keepdims=True))
    centred = values - mean
    rstd = lax.rsqrt(lax.optimization_barrier(jnp.mean(centred * centred, axis=-1, keepdims=True)) + EPS)
    return (centred * rstd, rstd)

def norm_back(grad_in, normed, rstd, gain):
    scaled = grad_in * gain
    return rstd * (scaled - lax.optimization_barrier(jnp.mean(scaled, axis=-1, keepdims=True)) - normed * lax.optimization_barrier(jnp.mean(scaled * normed, axis=-1, keepdims=True)))

def gelu_parts(pre):
    inner = GELU_C * (pre + 0.044715 * pre * pre * pre)
    tanh_v = jnp.tanh(inner)
    value = 0.5 * pre * (1.0 + tanh_v)
    slope = 0.5 * (1.0 + tanh_v) + 0.5 * pre * (1.0 - tanh_v * tanh_v) * GELU_C * (1.0 + 3.0 * 0.044715 * pre * pre)
    return (value, slope)

def split_heads(values):
    return values.astype(jnp.float32).reshape(values.shape[0], HEADS, HEAD_DIM)

def masked_scores(queries, keys, key_valid):
    scale = HEAD_DIM ** (-0.5)
    scores = jnp.einsum('shd,thd->hst', split_heads(queries), split_heads(keys)) * scale
    return jnp.where(key_valid[None, None, :], scores, -1e+30)

def reference(tokens, counts, w_qkv, w_out, w_fc1, w_fc2, vectors, cotangent):
    f32 = jnp.float32
    bf16 = jnp.bfloat16
    mat_qkv = w_qkv.reshape(D, 3 * D)
    mat_out = w_out.reshape(D, D)
    mat_fc1 = w_fc1.reshape(D, FF)
    mat_fc2 = w_fc2.reshape(FF, D)
    vec = vectors.astype(f32)
    bias1, v_bias, gain1, q_bias, out_bias, gain2, bias2, fc2_bias = [vec[i * D:(i + 1) * D] for i in range(8)]
    fc1_bias = vec[8 * D:8 * D + FF]
    scale = HEAD_DIM ** (-0.5)

    def one_image(carry, item):
        acc_qkv, acc_out, acc_fc1, acc_fc2, acc_vec = carry
        x_img, cnt, cot = item
        valid = (jnp.arange(SLOT)[None, :] < cnt[:, None]).reshape(-1)
        rowmask = valid.astype(f32)[:, None]
        x = x_img.astype(f32)
        normed1, rstd1 = normalize(x)
        ln1 = (normed1 * gain1 + bias1).astype(bf16)
        qkv = jnp.dot(ln1, mat_qkv, preferred_element_type=f32)
        queries = (qkv[:, :D] + q_bias).astype(bf16)
        keys = qkv[:, D:2 * D].astype(bf16)
        values = (qkv[:, 2 * D:] + v_bias).astype(bf16)
        scores = masked_scores(queries, keys, valid)
        top = lax.optimization_barrier(jnp.max(scores, axis=-1, keepdims=True))
        lse = top + jnp.log(lax.optimization_barrier(jnp.sum(jnp.exp(scores - top), axis=-1, keepdims=True)))
        probs = jnp.exp(scores - lse).astype(bf16)
        mixed = jnp.einsum('hst,thd->shd', probs.astype(f32), split_heads(values)).reshape(-1, D).astype(bf16)
        resid = x + jnp.dot(mixed, mat_out, preferred_element_type=f32) + out_bias
        normed2, rstd2 = normalize(resid)
        ln2 = (normed2 * gain2 + bias2).astype(bf16)
        pre = jnp.dot(ln2, mat_fc1, preferred_element_type=f32) + fc1_bias
        act_f, slope = gelu_parts(pre)
        act = act_f.astype(bf16)
        out_img = ((resid + jnp.dot(act, mat_fc2, preferred_element_type=f32) + fc2_bias) * rowmask).astype(bf16)
        grad_y = cot.astype(f32) * rowmask
        grad_y16 = grad_y.astype(bf16)
        g_fc2 = jnp.dot(act.T, grad_y16, preferred_element_type=f32)
        grad_act = jnp.dot(grad_y16, mat_fc2.T, preferred_element_type=f32)
        grad_pre = grad_act * slope
        grad_pre16 = grad_pre.astype(bf16)
        g_fc1 = jnp.dot(ln2.T, grad_pre16, preferred_element_type=f32)
        grad_ln2 = jnp.dot(grad_pre16, mat_fc1.T, preferred_element_type=f32)
        grad_resid = grad_y + norm_back(grad_ln2, normed2, rstd2, gain2)
        grad_resid16 = grad_resid.astype(bf16)
        g_out = jnp.dot(mixed.T, grad_resid16, preferred_element_type=f32)
        grad_mixed16 = jnp.dot(grad_resid16, mat_out.T, preferred_element_type=f32).astype(bf16)
        gm_heads = split_heads(grad_mixed16)
        delta = jnp.einsum('shd,shd->hs', gm_heads, split_heads(mixed))
        grad_values = jnp.einsum('hst,shd->thd', probs.astype(f32), gm_heads).reshape(-1, D)
        dots = jnp.einsum('shd,thd->hst', gm_heads, split_heads(values))
        grad_scores = (jnp.exp(scores - lse) * (dots - delta[:, :, None]) * scale).astype(bf16)
        grad_queries = jnp.einsum('hst,thd->shd', grad_scores.astype(f32), split_heads(keys)).reshape(-1, D)
        grad_keys = jnp.einsum('hst,shd->thd', grad_scores.astype(f32), split_heads(queries)).reshape(-1, D)
        grad_qkv16 = jnp.concatenate([grad_queries.astype(bf16), grad_keys.astype(bf16), grad_values.astype(bf16)], axis=1)
        g_qkv = jnp.dot(ln1.T, grad_qkv16, preferred_element_type=f32)
        grad_ln1 = jnp.dot(grad_qkv16, mat_qkv.T, preferred_element_type=f32)
        grad_in = grad_resid + norm_back(grad_ln1, normed1, rstd1, gain1)
        g_vec = jnp.concatenate([lax.optimization_barrier(jnp.sum(grad_ln1, axis=0)), lax.optimization_barrier(jnp.sum(grad_values, axis=0)), lax.optimization_barrier(jnp.sum(grad_ln1 * normed1, axis=0)), lax.optimization_barrier(jnp.sum(grad_queries, axis=0)), lax.optimization_barrier(jnp.sum(grad_resid, axis=0)), lax.optimization_barrier(jnp.sum(grad_ln2 * normed2, axis=0)), lax.optimization_barrier(jnp.sum(grad_ln2, axis=0)), lax.optimization_barrier(jnp.sum(grad_y, axis=0)), lax.optimization_barrier(jnp.sum(grad_pre, axis=0))])
        carry = (acc_qkv + g_qkv, acc_out + g_out, acc_fc1 + g_fc1, acc_fc2 + g_fc2, acc_vec + g_vec)
        return (carry, (out_img, grad_in))
    init = (jnp.zeros((D, 3 * D), f32), jnp.zeros((D, D), f32), jnp.zeros((D, FF), f32), jnp.zeros((FF, D), f32), jnp.zeros((8 * D + FF,), f32))
    carry, (outputs, input_grads) = lax.scan(one_image, init, (tokens, counts, cotangent))
    acc_qkv, acc_out, acc_fc1, acc_fc2, acc_vec = carry
    grad_front = acc_vec[:2 * D]
    grad_vectors = jnp.concatenate([acc_vec[2 * D:], jnp.zeros((VECS - 8 * D - FF,), f32)])
    return (outputs, input_grads, acc_qkv.reshape(-1), acc_out.reshape(-1), acc_fc1.reshape(-1), acc_fc2.reshape(-1), grad_vectors, grad_front)
```

```python
import functools

import jax
import jax.numpy as jnp
from jax import lax
from jax.experimental import pallas as pl
from jax.experimental.pallas import tpu as pltpu
from jax.sharding import PartitionSpec as P

HEADS = 16
HEAD_DIM = 72
EPS = 1e-06
GELU_C = 0.7978845608028654
LANES = 128
VMEM_LIMIT = 58 * 1024 * 1024
F32 = jnp.float32
BF16 = jnp.bfloat16


def round_up(value, step):
    return -(-value // step) * step


class Plan:
    def __init__(self, img, seq, width, shard_fc, shard_vec):
        self.img, self.seq, self.width = img, seq, width
        self.line = img // 2
        self.devices = img * seq
        self.hidden = shard_fc * self.devices // width
        self.cols = width // seq
        self.rows = width // img
        self.rows_pad = round_up(self.rows, 16)
        self.sub = self.rows // seq
        self.sub_pad = round_up(self.sub, 16)
        self.shard_fc, self.shard_vec = shard_fc, shard_vec
        self.first = [g * shard_fc // width for g in range(self.devices)]
        self.last = [-(-(g + 1) * shard_fc // width) for g in range(self.devices)]
        self.block = round_up(max(b - a for a, b in zip(self.first, self.last)), 16)
        self.units = img * self.block
        self.qkv_cols = round_up(3 * self.cols, LANES)
        self.mix_cols = round_up(4 * self.cols, LANES)


def coords(plan):
    index = lax.axis_index("img")
    return index // 2, lax.rem(index, 2), lax.axis_index("seq")


def remote(src, dst, send, recv, img, seq):
    return pltpu.make_async_remote_copy(
        src_ref=src,
        dst_ref=dst,
        send_sem=send,
        recv_sem=recv,
        device_id=(img, seq),
        device_id_type=pl.DeviceIdType.MESH,
    )


def entry_barrier(plan, z, y, s):
    barrier = pltpu.get_barrier_semaphore()

    def greet(img, seq):
        pl.semaphore_signal(
            barrier, inc=1, device_id=(img, seq), device_id_type=pl.DeviceIdType.MESH
        )

    @pl.when(z > 0)
    def _():
        greet((z - 1) * 2 + y, s)

    @pl.when(z < plan.line - 1)
    def _():
        greet((z + 1) * 2 + y, s)

    greet(z * 2 + 1 - y, s)
    for k in range(1, plan.seq):
        greet(z * 2 + y, lax.rem(s + k, plan.seq))
    peers = plan.seq + jnp.minimum(z, 1) + jnp.minimum(plan.line - 1 - z, 1)
    pl.semaphore_wait(barrier, peers)


def gather_kernel(
    plan,
    qkv_ref,
    fc1_ref,
    fc2_ref,
    ov_ref,
    x_ref,
    cot_ref,
    wq_ref,
    wf1_ref,
    wf2_ref,
    wo_ref,
    xs_ref,
    cots_ref,
    cq,
    cf,
    rq,
    rf,
    mq,
    mf,
    loc_sem,
    up_sem,
    down_sem,
    side_sem,
    got_sem,
    seq_send,
    seq_recv,
):
    z, y, s = coords(plan)
    me = z * 2 + y
    line, seq, sub = plan.line, plan.seq, plan.sub
    entry_barrier(plan, z, y, s)
    sources = [ov_ref, fc2_ref, mq, mf]
    targets = [wo_ref.at[s], wf2_ref, wq_ref, wf1_ref]

    def hop(q, piece, src, way):
        img = {"up": me + 2, "down": me - 2, "side": z * 2 + 1 - y}[way]
        sem = {"up": up_sem, "down": down_sem, "side": side_sem}[way]
        return remote(src, targets[q].at[piece], sem.at[q, piece], got_sem.at[q, piece], img, s)

    def own(q):
        pltpu.make_async_copy(sources[q], targets[q].at[me], loc_sem.at[q]).start()
        hop(q, me, sources[q], "side").start()

        @pl.when(z < line - 1)
        def _():
            hop(q, me, sources[q], "up").start()

        @pl.when(z > 0)
        def _():
            hop(q, me, sources[q], "down").start()

    def exchange(a, src, dst, k):
        peer = lax.rem(s + k, seq)
        return remote(src, dst, seq_send.at[a, k], seq_recv.at[a, k], me, peer)

    def came_from(k):
        return lax.rem(s + seq - k, seq)

    own(0)
    own(1)

    cq[...] = jnp.zeros_like(cq)
    cf[...] = jnp.zeros_like(cf)
    for t in range(seq):
        for j in range(3):
            at = j * plan.width + t * plan.cols
            cq[t, :sub, j * plan.cols : (j + 1) * plan.cols] = qkv_ref[:, at : at + plan.cols]
    for k in range(1, seq):
        exchange(0, cq.at[lax.rem(s + k, seq)], rq.at[s], k).start()
    for g in range(plan.devices):
        i, t = g // seq, g % seq
        a, b = plan.first[g], plan.last[g]
        cf[t, :sub, i * plan.block : i * plan.block + b - a] = fc1_ref[:, a:b]
    for k in range(1, seq):
        exchange(1, cf.at[lax.rem(s + k, seq)], rf.at[s], k).start()
    for a, src, dst in ((2, x_ref, xs_ref), (3, cot_ref, cots_ref)):
        pltpu.make_async_copy(src, dst.at[s], loc_sem.at[2 + a]).start()
        for k in range(1, seq):
            exchange(a, src, dst.at[s], k).start()

    for a, sent, got, merged in ((0, cq, rq, mq), (1, cf, rf, mf)):
        for k in range(1, seq):
            exchange(a, sent.at[lax.rem(s + k, seq)], got.at[came_from(k)], k).wait()
        got[s] = sent[s]
        for t in range(seq):
            merged[t * sub : (t + 1) * sub, :] = got[t, :sub, :]
        own(2 + a)

    for d in range(1, line):
        for q in range(4):
            low = (z - d) * 2 + y
            high = (z + d) * 2 + y

            @pl.when(z - d >= 0)
            def _():
                hop(q, low, targets[q].at[low], "side").wait_recv()
                hop(q, low, targets[q].at[low], "side").start()

                @pl.when(z < line - 1)
                def _():
                    hop(q, low, targets[q].at[low], "up").start()

            @pl.when(z + d < line)
            def _():
                hop(q, high, targets[q].at[high], "side").wait_recv()
                hop(q, high, targets[q].at[high], "side").start()

                @pl.when(z > 0)
                def _():
                    hop(q, high, targets[q].at[high], "down").start()

    def wait_side(q):
        for zs in range(line):
            piece = zs * 2 + 1 - y
            hop(q, piece, targets[q].at[piece], "side").wait_recv()
        pltpu.make_async_copy(sources[q], targets[q].at[me], loc_sem.at[q]).wait()

    wait_side(0)
    for k in range(1, seq):
        exchange(4, wo_ref.at[s], wo_ref.at[s], k).start()
    for q in range(1, 4):
        wait_side(q)

    for q in range(4):
        for zs in range(line):
            piece = zs * 2 + y
            hop(q, piece, targets[q].at[piece], "side").wait_send()

            @pl.when(jnp.logical_and(z < line - 1, zs <= z))
            def _():
                hop(q, piece, targets[q].at[piece], "up").wait_send()

            @pl.when(jnp.logical_and(z > 0, zs >= z))
            def _():
                hop(q, piece, targets[q].at[piece], "down").wait_send()

    for a, src, dst in ((2, x_ref, xs_ref), (3, cot_ref, cots_ref)):
        pltpu.make_async_copy(src, dst.at[s], loc_sem.at[2 + a]).wait()
        for k in range(1, seq):
            exchange(a, src, dst.at[came_from(k)], k).wait()
    for k in range(1, seq):
        exchange(4, wo_ref.at[s], wo_ref.at[came_from(k)], k).wait()


def gather_weights(plan, qkv, fc1, fc2, ov, x, cot):
    any_spec = pl.BlockSpec(memory_space=pl.ANY)
    vmem = pl.BlockSpec(memory_space=pltpu.VMEM)
    img, seq, width = plan.img, plan.seq, plan.width
    slot = x.shape[0]
    dma = pltpu.SemaphoreType.DMA
    shape = jax.ShapeDtypeStruct
    return pl.pallas_call(
        functools.partial(gather_kernel, plan),
        out_shape=(
            shape((img, plan.rows_pad, plan.qkv_cols), BF16),
            shape((img, plan.rows_pad, plan.units), BF16),
            shape((img, plan.block, width), BF16),
            shape((seq, img, plan.sub_pad, width), BF16),
            shape((seq, slot, width), BF16),
            shape((seq, slot, width), BF16),
        ),
        in_specs=[vmem, vmem, any_spec, any_spec, any_spec, any_spec],
        out_specs=(any_spec,) * 6,
        scratch_shapes=[
            pltpu.VMEM((seq, plan.sub_pad, plan.qkv_cols), BF16),
            pltpu.VMEM((seq, plan.sub_pad, plan.units), BF16),
            pltpu.VMEM((seq, plan.sub_pad, plan.qkv_cols), BF16),
            pltpu.VMEM((seq, plan.sub_pad, plan.units), BF16),
            pltpu.VMEM((plan.rows_pad, plan.qkv_cols), BF16),
            pltpu.VMEM((plan.rows_pad, plan.units), BF16),
            dma((6,)),
            dma((4, img)),
            dma((4, img)),
            dma((4, img)),
            dma((4, img)),
            dma((5, seq)),
            dma((5, seq)),
        ],
        compiler_params=pltpu.CompilerParams(
            collective_id=0, has_side_effects=True, vmem_limit_bytes=VMEM_LIMIT
        ),
        name="gather_weights",
    )(qkv, fc1, fc2, ov, x, cot)


def scatter_kernel(
    plan,
    parts,
    g2_ref,
    g1_ref,
    gm_ref,
    gv_ref,
    o2_ref,
    o1_ref,
    oq_ref,
    oo_ref,
    ov_ref,
    side2,
    side1,
    sidem,
    sidev,
    low2,
    low1,
    lowm,
    lowv,
    high2,
    high1,
    highm,
    highv,
    acc2,
    acc1,
    accm,
    accv,
    fin1,
    finm,
    cut1,
    cutm,
    cutv,
    got1,
    gotm,
    side_send,
    side_recv,
    low_send,
    low_recv,
    high_send,
    high_recv,
    seq_send,
    seq_recv,
):
    z, y, s = coords(plan)
    me = z * 2 + y
    line, seq, sub = plan.line, plan.seq, plan.sub
    entry_barrier(plan, z, y, s)
    grads = [g2_ref, g1_ref, gm_ref, gv_ref]
    sides = [side2, side1, sidem, sidev]
    lows = [low2, low1, lowm, lowv]
    highs = [high2, high1, highm, highv]
    accs = [acc2, acc1, accm, accv]

    def at(c):
        q, a, n = parts[c]
        return q, pl.ds(a, n)

    def to_side(c, dest):
        q, w = at(c)
        return remote(
            grads[q].at[dest * 2 + 1 - y, w],
            sides[q].at[dest, w],
            side_send.at[c, dest],
            side_recv.at[c, dest],
            z * 2 + 1 - y,
            s,
        )

    def to_up(c, dest):
        q, w = at(c)
        return remote(
            accs[q].at[dest, w],
            lows[q].at[dest, w],
            low_send.at[c, dest],
            low_recv.at[c, dest],
            me + 2,
            s,
        )

    def to_down(c, dest):
        q, w = at(c)
        return remote(
            accs[q].at[dest, w],
            highs[q].at[dest, w],
            high_send.at[c, dest],
            high_recv.at[c, dest],
            me - 2,
            s,
        )

    for c in range(len(parts)):
        for d in range(line - 1, -1, -1):

            @pl.when(z + d < line)
            def _():
                to_side(c, z + d).start()

            if d:

                @pl.when(z - d >= 0)
                def _():
                    to_side(c, z - d).start()

    def both(c, dest):
        q, w = at(c)
        to_side(c, dest).wait_recv()
        return grads[q][dest * 2 + y, w, :].astype(F32) + sides[q][dest, w, :].astype(F32)

    def pass_on(c):
        q, w = at(c)
        for d in range(line - 1, 0, -1):

            @pl.when(z + d < line)
            def _():
                dest = z + d
                total = both(c, dest)

                @pl.when(z > 0)
                def _():
                    to_up(c, dest).wait_recv()
                    accs[q][dest, w, :] = (total + lows[q][dest, w, :].astype(F32)).astype(BF16)

                @pl.when(z == 0)
                def _():
                    accs[q][dest, w, :] = total.astype(BF16)

                to_up(c, dest).start()

            @pl.when(z - d >= 0)
            def _():
                dest = z - d
                total = both(c, dest)

                @pl.when(z < line - 1)
                def _():
                    to_down(c, dest).wait_recv()
                    accs[q][dest, w, :] = (total + highs[q][dest, w, :].astype(F32)).astype(BF16)

                @pl.when(z == line - 1)
                def _():
                    accs[q][dest, w, :] = total.astype(BF16)

                to_down(c, dest).start()

    outs = [o2_ref, fin1, finm, None]

    def finish(c):
        q, w = at(c)
        total = both(c, z)

        def store(value):
            if q == 3:
                cutv[s, w, :] = value.astype(BF16)
            else:
                outs[q][w, :] = value.astype(outs[q].dtype)


        @pl.when(z == 0)
        def _():
            to_down(c, z).wait_recv()
            store(total + highs[q][z, w, :].astype(F32))

        @pl.when(z == line - 1)
        def _():
            to_up(c, z).wait_recv()
            store(total + lows[q][z, w, :].astype(F32))

        @pl.when(jnp.logical_and(z > 0, z < line - 1))
        def _():
            to_down(c, z).wait_recv()
            to_up(c, z).wait_recv()
            store(total + lows[q][z, w, :].astype(F32) + highs[q][z, w, :].astype(F32))

    def exchange(a, src, dst, k):
        peer = lax.rem(s + k, seq)
        return remote(src, dst, seq_send.at[a, k], seq_recv.at[a, k], me, peer)

    def came_from(k):
        return lax.rem(s + seq - k, seq)

    ends = {max(c for c in range(len(parts)) if parts[c][0] == q): q for q in (1, 2, 3)}

    def after(c):
        if c not in ends:
            return
        q = ends[c]
        if q == 3:
            for k in range(1, seq):
                exchange(2, cutv.at[s], ov_ref.at[s], k).start()
            return
        fin, cut, got = ((fin1, cut1, got1), (finm, cutm, gotm))[q - 1]
        for t in range(seq):
            cut[t, :sub, :] = fin[t * sub : (t + 1) * sub, :].astype(BF16)
        for k in range(1, seq):
            exchange(q - 1, cut.at[lax.rem(s + k, seq)], got.at[s], k).start()

    lag = 1
    for c in range(len(parts) + lag):
        if c < len(parts):
            pass_on(c)
        if c >= lag:
            finish(c - lag)
            after(c - lag)

    got1[s] = cut1[s]
    gotm[s] = cutm[s]
    ov_ref[s] = cutv[s]
    for k in range(1, seq):
        exchange(1, cutm.at[lax.rem(s + k, seq)], gotm.at[came_from(k)], k).wait()
    for t in range(seq):
        for j in range(3):
            to = j * plan.width + t * plan.cols
            oq_ref[:, to : to + plan.cols] = gotm[
                t, :sub, j * plan.cols : (j + 1) * plan.cols
            ].astype(F32)
        oo_ref[:, t * plan.cols : (t + 1) * plan.cols] = gotm[
            t, :sub, 3 * plan.cols : 4 * plan.cols
        ].astype(F32)
    for k in range(1, seq):
        exchange(0, cut1.at[lax.rem(s + k, seq)], got1.at[came_from(k)], k).wait()
    o1_ref[...] = jnp.zeros_like(o1_ref)
    for g in range(plan.devices):
        i, t = g // seq, g % seq
        a, b = plan.first[g], plan.last[g]
        o1_ref[:, a:b] += got1[t, :sub, i * plan.block : i * plan.block + b - a].astype(F32)
    for k in range(1, seq):
        exchange(2, cutv.at[s], ov_ref.at[came_from(k)], k).wait()

    for c in range(len(parts)):
        for dest in range(line):
            to_side(c, dest).wait_send()

            @pl.when(dest > z)
            def _():
                to_up(c, dest).wait_send()

            @pl.when(dest < z)
            def _():
                to_down(c, dest).wait_send()


def scatter_grads(plan, g2, g1, gm, gv):
    vmem = pl.BlockSpec(memory_space=pltpu.VMEM)
    seq, width, line = plan.seq, plan.width, plan.line
    dma = pltpu.SemaphoreType.DMA
    shape = jax.ShapeDtypeStruct
    parts = []
    step = 48
    for q, rows in ((0, plan.block), (1, plan.rows_pad), (2, plan.rows_pad)):
        parts += [(q, a, min(step, rows - a)) for a in range(0, rows, step)]
    parts.append((3, 0, 16))
    inner = [ref.shape[1:] for ref in (g2, g1, gm, gv)]
    buffers = [pltpu.VMEM((line, *dims), BF16) for _ in range(4) for dims in inner]
    n = len(parts)
    return pl.pallas_call(
        functools.partial(scatter_kernel, plan, parts),
        out_shape=(
            shape((plan.block, width), F32),
            shape((plan.sub, plan.hidden), F32),
            shape((plan.sub, 3 * width), F32),
            shape((plan.sub, width), F32),
            shape((seq, *gv.shape[1:]), BF16),
        ),
        in_specs=[vmem] * 4,
        out_specs=(vmem,) * 5,
        scratch_shapes=buffers
        + [
            pltpu.VMEM(g1.shape[1:], F32),
            pltpu.VMEM(gm.shape[1:], F32),
            pltpu.VMEM((seq, plan.sub_pad, g1.shape[2]), BF16),
            pltpu.VMEM((seq, plan.sub_pad, gm.shape[2]), BF16),
            pltpu.VMEM((seq, *gv.shape[1:]), BF16),
            pltpu.VMEM((seq, plan.sub_pad, g1.shape[2]), BF16),
            pltpu.VMEM((seq, plan.sub_pad, gm.shape[2]), BF16),
        ]
        + [dma((n, line))] * 6
        + [dma((3, seq))] * 2,
        compiler_params=pltpu.CompilerParams(
            collective_id=1, has_side_effects=True, vmem_limit_bytes=VMEM_LIMIT
        ),
        name="scatter_grads",
    )(g2, g1, gm, gv)


def normalize(values):
    mean = jnp.mean(values, axis=-1, keepdims=True)
    centred = values - mean
    rstd = lax.rsqrt(jnp.mean(centred * centred, axis=-1, keepdims=True) + EPS)
    return (centred * rstd, rstd)


def norm_back(grad_in, normed, rstd, gain):
    scaled = grad_in * gain
    return rstd * (
        scaled
        - jnp.mean(scaled, axis=-1, keepdims=True)
        - normed * jnp.mean(scaled * normed, axis=-1, keepdims=True)
    )


def gelu_parts(pre):
    inner = GELU_C * (pre + 0.044715 * pre * pre * pre)
    tanh_v = jnp.tanh(inner)
    value = 0.5 * pre * (1.0 + tanh_v)
    slope = 0.5 * (1.0 + tanh_v) + 0.5 * pre * (1.0 - tanh_v * tanh_v) * GELU_C * (
        1.0 + 3.0 * 0.044715 * pre * pre
    )
    return (value, slope)


def gather(value, axes):
    return lax.all_gather(value, axes, axis=0, tiled=True)


def scatter_sum(value, axes):
    return lax.psum_scatter(value, axes, scatter_dimension=0, tiled=True)


def weight_grad(left, right):
    return lax.dot_general(
        left, right, (((0,), (0,)), ((), ())), preferred_element_type=F32
    ).astype(BF16)


def dot_t(left, right):
    return lax.dot_general(left, right, (((1,), (1,)), ((), ())), preferred_element_type=F32)


def batched(left, right, over_left, over_right):
    return lax.dot_general(
        left,
        right,
        (((over_left,), (over_right,)), ((0,), (0,))),
        preferred_element_type=F32,
    )


TILE = 2048


def pack(flat):
    padded = round_up(flat.shape[0], TILE)
    return jnp.pad(flat, (0, padded - flat.shape[0])).reshape(-1, LANES)


def unpack_blocks(packed, blocks, length):
    return packed.reshape(blocks, -1)[:, :length].reshape(-1)


def pack_blocks(flat, blocks):
    block = flat.reshape(blocks, -1)
    padded = round_up(block.shape[1], TILE)
    return jnp.pad(block, ((0, 0), (0, padded - block.shape[1]))).reshape(-1, LANES)


def shards_by_rows(tokens, counts, w_qkv, w_out, w_fc1, w_fc2, vectors, cotangent):
    f32 = jnp.float32
    bf16 = jnp.bfloat16
    width = tokens.shape[2]
    slot = tokens.shape[1]
    scale = HEAD_DIM ** (-0.5)
    position = lax.axis_index("seq")
    seq_count = lax.axis_size("seq")
    img_count = lax.axis_size("img")
    device_count = img_count * seq_count
    both = ("img", "seq")
    shard_qkv, shard_out, shard_fc1, shard_fc2, shard_vec = (
        w.shape[0] for w in (w_qkv, w_out, w_fc1, w_fc2, vectors)
    )
    hidden = shard_fc1 * device_count // width
    heads = HEADS // seq_count
    cols = width // seq_count
    units = hidden // seq_count
    rows = width // img_count
    pad_cols = round_up(3 * cols, LANES) - 3 * cols
    pad_units = round_up(units, LANES) - units
    to_quarter = [(c, (c % img_count) * seq_count + c // img_count) for c in range(device_count)]
    to_owner = [(b, a) for a, b in to_quarter]

    slice_counts = counts[0]
    key_valid = (jnp.arange(slot)[None, :] < slice_counts[:, None]).reshape(-1)
    row_valid = lax.dynamic_slice_in_dim(key_valid, position * slot, slot)
    rowmask = row_valid.astype(f32)[:, None]

    def mine(values):
        return lax.dynamic_slice_in_dim(values, position * slot, slot)

    shard_ov = shard_out + shard_vec
    local = gather(pack(jnp.concatenate([w_qkv, w_fc1, w_out, vectors])), "seq")
    local = local.reshape(seq_count, -1)
    x_all16 = gather(tokens[0], "seq")
    qkv_rows = local[:, :shard_qkv].reshape(rows, 3 * width)
    fc1_rows = local[:, shard_qkv : shard_qkv + shard_fc1].reshape(rows, hidden)
    ov_flat = local[:, shard_qkv + shard_fc1 : shard_qkv + shard_fc1 + shard_ov].reshape(-1)
    ov_cols = round_up(-(-ov_flat.shape[0] // rows), LANES)
    ov_part = jnp.pad(ov_flat, (0, rows * ov_cols - ov_flat.shape[0])).reshape(rows, ov_cols)
    qkv_part = jnp.concatenate(
        [
            lax.dynamic_slice_in_dim(qkv_rows, j * width + position * cols, cols, axis=1)
            for j in range(3)
        ]
        + [jnp.zeros((rows, pad_cols), bf16)],
        axis=1,
    )
    fc1_part = jnp.pad(
        lax.dynamic_slice_in_dim(fc1_rows, position * units, units, axis=1),
        ((0, 0), (0, pad_units)),
    )
    fc2_chunk = lax.ppermute(pack(w_fc2), both, to_quarter).reshape(-1)[:shard_fc2]
    fc2_part = jnp.pad(fc2_chunk.reshape(rows, units), ((0, 0), (0, pad_units)))
    weights = gather(jnp.concatenate([qkv_part, fc1_part, fc2_part, ov_part], axis=1), "img")
    end_qkv = 3 * cols + pad_cols
    end_fc1 = end_qkv + units + pad_units
    end_fc2 = end_fc1 + units + pad_units
    mat_qkv = weights[:, :end_qkv]
    mat_fc1 = weights[:, end_qkv:end_fc1]
    mat_fc2 = jnp.pad(
        weights[:, end_fc1 : end_fc1 + units].reshape(units, width), ((0, pad_units), (0, 0))
    )
    out_vec = weights[:, end_fc2:].reshape(img_count, -1)[:, : seq_count * shard_ov]
    cot_all = gather(cotangent[0], "seq")

    blocks_ov = out_vec.reshape(device_count, -1)
    mat_out = blocks_ov[:, :shard_out].reshape(width, width)
    vec = blocks_ov[:, shard_out : shard_out + shard_vec].reshape(-1).astype(f32)
    bias1, v_bias, gain1, q_bias, out_bias, gain2, bias2, fc2_bias = (
        vec[i * width : (i + 1) * width] for i in range(8)
    )
    fc1_bias = vec[8 * width : 8 * width + hidden]

    def my_cols(values):
        return lax.dynamic_slice_in_dim(values, position * cols, cols)

    fc1_bias_mine = jnp.pad(
        lax.dynamic_slice_in_dim(fc1_bias, position * units, units), (0, pad_units)
    )

    x = x_all16.astype(f32)
    normed1, _ = normalize(x)
    ln1 = (normed1 * gain1 + bias1).astype(bf16)
    qkv = jnp.dot(ln1, mat_qkv, preferred_element_type=f32)

    def by_head(values):
        return values.reshape(-1, heads, HEAD_DIM).transpose(1, 0, 2)

    def by_slot(values):
        return values.transpose(1, 0, 2).reshape(-1, cols)

    queries = by_head((qkv[:, :cols] + my_cols(q_bias)).astype(bf16))
    keys = by_head(qkv[:, cols : 2 * cols].astype(bf16))
    values = by_head((qkv[:, 2 * cols : 3 * cols] + my_cols(v_bias)).astype(bf16))
    scores = batched(queries, keys, 2, 2) * scale
    scores = jnp.where(key_valid[None, None, :], scores, -1e30)
    top = jnp.max(scores, axis=-1, keepdims=True)
    lse = top + jnp.log(jnp.sum(jnp.exp(scores - top), axis=-1, keepdims=True))
    probs = jnp.exp(scores - lse).astype(bf16)
    mixed_heads = batched(probs, values, 2, 1)
    mixed_mine = by_slot(mixed_heads).astype(bf16)
    mixed = lax.all_gather(mixed_mine, "seq", axis=0, tiled=True)
    mixed = (
        mixed.reshape(seq_count, -1, cols).transpose(1, 0, 2).reshape(-1, width)
    )
    resid = x + jnp.dot(mixed, mat_out, preferred_element_type=f32) + out_bias
    normed2, rstd2 = normalize(resid)
    ln2 = (normed2 * gain2 + bias2).astype(bf16)
    pre = jnp.dot(ln2, mat_fc1, preferred_element_type=f32) + fc1_bias_mine
    act_f, slope = gelu_parts(pre)
    act = act_f.astype(bf16)

    grad_y16 = jnp.where(key_valid[:, None], cot_all, jnp.zeros((), bf16))
    grad_pre = dot_t(grad_y16, mat_fc2) * slope
    grad_pre16 = grad_pre.astype(bf16)
    grad_ln2 = scatter_sum(dot_t(grad_pre16, mat_fc1).astype(bf16), "seq").astype(f32)
    grad_y = cotangent[0].astype(f32) * rowmask
    normed2_mine = mine(normed2)
    grad_resid = grad_y + norm_back(grad_ln2, normed2_mine, mine(rstd2), gain2)
    grad_resid16 = gather(grad_resid.astype(bf16), "seq")

    part_fc1 = weight_grad(ln2, grad_pre16)
    part_fc2 = pack_blocks(weight_grad(act, grad_y16)[:units].reshape(-1), img_count)
    out_terms = scatter_sum(
        jnp.dot(act, mat_fc2, preferred_element_type=f32).astype(bf16), "seq"
    ).astype(f32)
    output = ((mine(resid) + out_terms + fc2_bias) * rowmask).astype(bf16)

    out_mine = lax.dynamic_slice_in_dim(mat_out, position * cols, cols)
    gm = by_head(dot_t(grad_resid16, out_mine).astype(bf16))
    mixed_back = by_head(mixed_mine)
    delta = jnp.sum(gm.astype(f32) * mixed_back.astype(f32), axis=-1, keepdims=True)
    grad_values = by_slot(batched(probs, gm, 1, 1))
    dots = batched(gm, values, 2, 2)
    grad_scores = (jnp.exp(scores - lse) * (dots - delta) * scale).astype(bf16)
    grad_queries = by_slot(batched(grad_scores, keys, 2, 1))
    grad_keys = by_slot(batched(grad_scores, queries, 1, 1))
    grad_qkv16 = jnp.concatenate(
        [grad_queries.astype(bf16), grad_keys.astype(bf16), grad_values.astype(bf16)]
        + [jnp.zeros((seq_count * slot, pad_cols), bf16)],
        axis=1,
    )
    grad_ln1 = scatter_sum(dot_t(grad_qkv16, mat_qkv).astype(bf16), "seq").astype(f32)
    part_qkv = weight_grad(ln1, grad_qkv16)
    part_out = pack_blocks(weight_grad(mixed_mine, grad_resid16).reshape(-1), img_count)
    normed1_mine, rstd1_mine = normalize(tokens[0].astype(f32))
    input_grad = grad_resid + norm_back(grad_ln1, normed1_mine, rstd1_mine, gain1)

    def spread(part, full):
        return lax.dynamic_update_slice_in_dim(
            jnp.zeros((full,), f32), part, position * part.shape[0], 0
        )

    shard_front = 2 * width // device_count
    unused = shard_vec * device_count - 8 * width - hidden
    g_front = jnp.concatenate(
        [jnp.sum(grad_ln1, axis=0), spread(jnp.sum(grad_values, axis=0), width)]
    )
    g_rest = jnp.concatenate(
        [
            jnp.sum(grad_ln1 * normed1_mine, axis=0),
            spread(jnp.sum(grad_queries, axis=0), width),
            jnp.sum(grad_resid, axis=0),
            jnp.sum(grad_ln2 * normed2_mine, axis=0),
            jnp.sum(grad_ln2, axis=0),
            jnp.sum(grad_y, axis=0),
            spread(jnp.sum(grad_pre, axis=0)[:units], hidden),
            jnp.zeros((unused,), f32),
        ]
    )
    g_vec = jnp.concatenate(
        [g_front.reshape(device_count, -1), g_rest.reshape(device_count, -1)], axis=1
    )
    vec_pad = round_up(shard_vec, 4 * LANES)
    part_vec = jnp.pad(g_vec, ((0, 0), (0, vec_pad - shard_vec))).astype(bf16)

    parts = [
        part.reshape(img_count, -1, LANES)
        for part in (part_qkv, part_fc1, part_vec, part_fc2, part_out)
    ]
    sizes = [part.shape[1] for part in parts]
    summed = scatter_sum(jnp.concatenate(parts, axis=1).reshape(-1, LANES), "img")
    ends = [sum(sizes[: i + 1]) for i in range(5)]
    chunks = lax.ppermute(summed[ends[2] :], both, to_owner)
    grad_fc2 = chunks[: sizes[3]].reshape(-1)[:shard_fc2].astype(f32)
    grad_out = chunks[sizes[3] :].reshape(-1)[:shard_out].astype(f32)
    shared = gather(summed[: ends[2]], "seq").reshape(seq_count, ends[2], LANES)

    def own_block(packed, thirds, used, size):
        blocks = packed.reshape(seq_count, rows, -1)[:, :, : thirds * used]
        whole = blocks.reshape(seq_count, rows, thirds, used).transpose(1, 2, 0, 3)
        return lax.dynamic_slice_in_dim(whole.reshape(-1), position * size, size).astype(f32)

    grad_qkv = own_block(shared[:, : ends[0]], 3, cols, shard_qkv)
    grad_fc1 = own_block(shared[:, ends[0] : ends[1]], 1, units, shard_fc1)
    vec_sums = jnp.sum(shared[:, ends[1] :].astype(f32), axis=0).reshape(seq_count, vec_pad)
    vec_mine = lax.dynamic_slice_in_dim(vec_sums, position, 1).reshape(-1)
    return (
        output[None],
        input_grad[None],
        grad_qkv,
        grad_out,
        grad_fc1,
        grad_fc2,
        vec_mine[shard_front:shard_vec],
        vec_mine[:shard_front],
    )


def shards(tokens, counts, w_qkv, w_out, w_fc1, w_fc2, vectors, cotangent):
    width = tokens.shape[2]
    slot = tokens.shape[1]
    scale = HEAD_DIM ** (-0.5)
    position = lax.axis_index("seq")
    seq_count = lax.axis_size("seq")
    img_count = lax.axis_size("img")
    device_count = img_count * seq_count
    chunk = lax.axis_index("img") * seq_count + position
    shard_vec = vectors.shape[0]
    plan = Plan(img_count, seq_count, width, w_fc1.shape[0], shard_vec)
    hidden, cols, rows, units = plan.hidden, plan.cols, plan.rows, plan.units
    heads = HEADS // seq_count
    shard_fc = plan.shard_fc

    slice_counts = counts[0]
    key_valid = (jnp.arange(slot)[None, :] < slice_counts[:, None]).reshape(-1)
    row_valid = lax.dynamic_slice_in_dim(key_valid, position * slot, slot)
    rowmask = row_valid.astype(F32)[:, None]

    def mine(values):
        return lax.dynamic_slice_in_dim(values, position * slot, slot)

    shift = lax.rem(chunk * shard_fc, width)
    fc2_flat = lax.dynamic_update_slice_in_dim(
        jnp.zeros((plan.block * width,), BF16), w_fc2, shift, 0
    )
    ov = jnp.concatenate(
        [
            w_out.reshape(plan.sub, width),
            jnp.pad(vectors, (0, width - shard_vec))[None],
            jnp.zeros((plan.sub_pad - plan.sub - 1, width), BF16),
        ]
    )
    wq, wf1, wf2, wo, xs, cots = gather_weights(
        plan,
        w_qkv.reshape(plan.sub, 3 * width),
        w_fc1.reshape(plan.sub, hidden),
        fc2_flat.reshape(plan.block, width),
        ov,
        tokens[0],
        cotangent[0],
    )
    mat_qkv = wq[:, :rows].reshape(width, -1)
    mat_fc1 = wf1[:, :rows].reshape(width, -1)
    mat_fc2 = wf2.reshape(units, width)
    wo_t = wo.transpose(1, 0, 2, 3)
    mat_out = wo_t[:, :, : plan.sub].reshape(width, width)
    vec = wo_t[:, :, plan.sub, :shard_vec].reshape(-1).astype(F32)
    x_all16 = xs.reshape(seq_count * slot, width)
    cot_all = cots.reshape(seq_count * slot, width)

    bias1, v_bias, gain1, q_bias, out_bias, gain2, bias2, fc2_bias = (
        vec[i * width : (i + 1) * width] for i in range(8)
    )
    fc1_bias = vec[8 * width : 8 * width + hidden]

    def my_cols(values):
        return lax.dynamic_slice_in_dim(values, position * cols, cols)

    fc1_bias_mine = lax.dynamic_slice_in_dim(
        jnp.stack(
            [
                jnp.pad(fc1_bias[a:b], (0, plan.block - (b - a)))
                for a, b in zip(plan.first, plan.last)
            ]
        ).reshape(img_count, seq_count, plan.block),
        position,
        1,
        axis=1,
    ).reshape(-1)

    x = x_all16.astype(F32)
    normed1, _ = normalize(x)
    ln1 = (normed1 * gain1 + bias1).astype(BF16)
    qkv = jnp.dot(ln1, mat_qkv, preferred_element_type=F32)

    def by_head(values):
        return values.reshape(-1, heads, HEAD_DIM).transpose(1, 0, 2)

    def by_slot(values):
        return values.transpose(1, 0, 2).reshape(-1, cols)

    queries = by_head((qkv[:, :cols] + my_cols(q_bias)).astype(BF16))
    keys = by_head(qkv[:, cols : 2 * cols].astype(BF16))
    values = by_head((qkv[:, 2 * cols : 3 * cols] + my_cols(v_bias)).astype(BF16))
    scores = batched(queries, keys, 2, 2) * scale
    scores = jnp.where(key_valid[None, None, :], scores, -1e30)
    top = jnp.max(scores, axis=-1, keepdims=True)
    lse = top + jnp.log(jnp.sum(jnp.exp(scores - top), axis=-1, keepdims=True))
    probs = jnp.exp(scores - lse).astype(BF16)
    mixed_heads = batched(probs, values, 2, 1)
    mixed_mine = by_slot(mixed_heads).astype(BF16)
    mixed = lax.all_gather(mixed_mine, "seq", axis=0, tiled=True)
    mixed = mixed.reshape(seq_count, -1, cols).transpose(1, 0, 2).reshape(-1, width)
    resid = x + jnp.dot(mixed, mat_out, preferred_element_type=F32) + out_bias
    normed2, rstd2 = normalize(resid)
    ln2 = (normed2 * gain2 + bias2).astype(BF16)
    pre = jnp.dot(ln2, mat_fc1, preferred_element_type=F32) + fc1_bias_mine
    act_f, slope = gelu_parts(pre)
    act = act_f.astype(BF16)

    grad_y16 = jnp.where(key_valid[:, None], cot_all, jnp.zeros((), BF16))
    grad_pre = dot_t(grad_y16, mat_fc2) * slope
    grad_pre16 = grad_pre.astype(BF16)
    grad_ln2 = scatter_sum(dot_t(grad_pre16, mat_fc1).astype(BF16), "seq").astype(F32)
    grad_y = cotangent[0].astype(F32) * rowmask
    normed2_mine = mine(normed2)
    grad_resid = grad_y + norm_back(grad_ln2, normed2_mine, mine(rstd2), gain2)
    grad_resid16 = gather(grad_resid.astype(BF16), "seq")

    part_fc1 = weight_grad(ln2, grad_pre16)
    part_fc2 = weight_grad(act, grad_y16)
    out_terms = scatter_sum(
        jnp.dot(act, mat_fc2, preferred_element_type=F32).astype(BF16), "seq"
    ).astype(F32)
    output = ((mine(resid) + out_terms + fc2_bias) * rowmask).astype(BF16)

    out_mine = lax.dynamic_slice_in_dim(mat_out, position * cols, cols)
    gm = by_head(dot_t(grad_resid16, out_mine).astype(BF16))
    mixed_back = by_head(mixed_mine)
    delta = jnp.sum(gm.astype(F32) * mixed_back.astype(F32), axis=-1, keepdims=True)
    grad_values = by_slot(batched(probs, gm, 1, 1))
    dots = batched(gm, values, 2, 2)
    grad_scores = (jnp.exp(scores - lse) * (dots - delta) * scale).astype(BF16)
    grad_queries = by_slot(batched(grad_scores, keys, 2, 1))
    grad_keys = by_slot(batched(grad_scores, queries, 1, 1))
    grad_qkv16 = jnp.concatenate(
        [grad_queries.astype(BF16), grad_keys.astype(BF16), grad_values.astype(BF16)]
        + [jnp.zeros((seq_count * slot, plan.qkv_cols - 3 * cols), BF16)],
        axis=1,
    )
    grad_ln1 = scatter_sum(dot_t(grad_qkv16, mat_qkv).astype(BF16), "seq").astype(F32)
    part_qkv = weight_grad(ln1, grad_qkv16[:, : 3 * cols])
    part_out = weight_grad(
        mixed, lax.dynamic_slice_in_dim(grad_resid16, position * cols, cols, axis=1)
    )
    part_mix = jnp.concatenate([part_qkv, part_out], axis=1)
    normed1_mine, rstd1_mine = normalize(tokens[0].astype(F32))
    input_grad = grad_resid + norm_back(grad_ln1, normed1_mine, rstd1_mine, gain1)

    def spread(part, full):
        return lax.dynamic_update_slice_in_dim(
            jnp.zeros((full,), F32), part, position * part.shape[0], 0
        )

    pre_sums = jnp.sum(grad_pre, axis=0).reshape(img_count, 1, plan.block)
    pre_blocks = lax.dynamic_update_slice(
        jnp.zeros((img_count, seq_count, plan.block), F32), pre_sums, (0, position, 0)
    ).reshape(device_count, plan.block)
    pieces = []
    for g in range(device_count):
        a, b = plan.first[g], plan.last[g]
        start = 1 if g and plan.last[g - 1] > a else 0
        piece = pre_blocks[g, start : b - a]
        if g + 1 < device_count and plan.first[g + 1] < b:
            piece = jnp.concatenate([piece[:-1], piece[-1:] + pre_blocks[g + 1, :1]])
        pieces.append(piece)
    g_fc1_bias = jnp.concatenate(pieces)

    shard_front = 2 * width // device_count
    unused = shard_vec * device_count - 8 * width - hidden
    g_front = jnp.concatenate(
        [jnp.sum(grad_ln1, axis=0), spread(jnp.sum(grad_values, axis=0), width)]
    )
    g_rest = jnp.concatenate(
        [
            jnp.sum(grad_ln1 * normed1_mine, axis=0),
            spread(jnp.sum(grad_queries, axis=0), width),
            jnp.sum(grad_resid, axis=0),
            jnp.sum(grad_ln2 * normed2_mine, axis=0),
            jnp.sum(grad_ln2, axis=0),
            jnp.sum(grad_y, axis=0),
            g_fc1_bias,
            jnp.zeros((unused,), F32),
        ]
    )
    g_vec = jnp.concatenate(
        [g_front.reshape(device_count, -1), g_rest.reshape(device_count, -1)], axis=1
    )
    vec_pad = round_up(shard_vec, LANES)
    part_vec = jnp.pad(
        g_vec.reshape(img_count, seq_count, shard_vec),
        ((0, 0), (0, 16 - seq_count), (0, vec_pad - shard_vec)),
    ).astype(BF16)

    pad_rows = ((0, 0), (0, plan.rows_pad - rows), (0, 0))
    grad2, grad1, gradq, grado, gradv = scatter_grads(
        plan,
        part_fc2.reshape(img_count, plan.block, width),
        jnp.pad(part_fc1.reshape(img_count, rows, -1), pad_rows),
        jnp.pad(part_mix.reshape(img_count, rows, -1), pad_rows),
        part_vec,
    )
    grad_fc2 = lax.dynamic_slice_in_dim(grad2.reshape(-1), shift, shard_fc)
    vec_sums = jnp.sum(gradv.astype(F32), axis=0)
    vec_mine = lax.dynamic_slice_in_dim(vec_sums, position, 1).reshape(-1)
    return (
        output[None],
        input_grad[None],
        gradq.reshape(-1),
        grado.reshape(-1),
        grad1.reshape(-1),
        grad_fc2,
        vec_mine[shard_front:shard_vec],
        vec_mine[:shard_front],
    )


def solution(mesh):
    def layer(*arrays):
        width = arrays[0].shape[2]
        whole_rows = width % mesh.size == 0 and mesh.shape["img"] % 2 == 0
        return (shards if whole_rows else shards_by_rows)(*arrays)

    return jax.shard_map(
        layer,
        mesh=mesh,
        in_specs=(
            P("img", "seq", None),
            P("img", None),
            P(("img", "seq")),
            P(("img", "seq")),
            P(("img", "seq")),
            P(("img", "seq")),
            P(("img", "seq")),
            P("img", "seq", None),
        ),
        out_specs=(
            P("img", "seq", None),
            P("img", "seq", None),
            P(("img", "seq")),
            P(("img", "seq")),
            P(("img", "seq")),
            P(("img", "seq")),
            P(("img", "seq")),
            P(("img", "seq")),
        ),
        check_vma=False,
    )
```

```python
import functools
from typing import NamedTuple

import jax
import jax.numpy as jnp
from jax import lax
from jax.experimental import pallas as pl
from jax.experimental.pallas import tpu as pltpu
from jax.sharding import PartitionSpec as P

HEADS = 16
HEAD_DIM = 72
EPS = 1e-06
GELU_C = 0.7978845608028654
LANES = 128
VMEM_LIMIT = 58 * 1024 * 1024
ACROSS = 1
F32 = jnp.float32
BF16 = jnp.bfloat16


def round_up(value, step):
    return -(-value // step) * step


class Plan:
    def __init__(self, img, seq, width, shard_fc, shard_vec):
        self.img, self.seq, self.width = img, seq, width
        self.line = img // 2
        self.devices = img * seq
        self.hidden = shard_fc * self.devices // width
        self.cols = width // seq
        self.rows = width // img
        self.rows_pad = round_up(self.rows, 16)
        self.sub = self.rows // seq
        self.sub_pad = round_up(self.sub, 16)
        self.shard_fc, self.shard_vec = shard_fc, shard_vec
        self.first = [g * shard_fc // width for g in range(self.devices)]
        self.last = [-(-(g + 1) * shard_fc // width) for g in range(self.devices)]
        self.block = round_up(max(b - a for a, b in zip(self.first, self.last)), 16)
        self.units = img * self.block
        self.qkv_cols = round_up(3 * self.cols, LANES)
        self.mix_cols = round_up(4 * self.cols, LANES)


def coords(plan):
    index = lax.axis_index("img")
    return index // 2, lax.rem(index, 2), lax.axis_index("seq")


def remote(src, dst, send, recv, img, seq):
    return pltpu.make_async_remote_copy(
        src_ref=src,
        dst_ref=dst,
        send_sem=send,
        recv_sem=recv,
        device_id=(img, seq),
        device_id_type=pl.DeviceIdType.MESH,
    )


def entry_barrier(plan, z, y, s):
    barrier = pltpu.get_barrier_semaphore()

    def greet(img, seq):
        pl.semaphore_signal(
            barrier, inc=1, device_id=(img, seq), device_id_type=pl.DeviceIdType.MESH
        )

    @pl.when(z > 0)
    def _():
        greet((z - 1) * 2 + y, s)

    @pl.when(z < plan.line - 1)
    def _():
        greet((z + 1) * 2 + y, s)

    greet(z * 2 + 1 - y, s)
    for k in range(1, plan.seq):
        greet(z * 2 + y, lax.rem(s + k, plan.seq))
    peers = plan.seq + jnp.minimum(z, 1) + jnp.minimum(plan.line - 1 - z, 1)
    pl.semaphore_wait(barrier, peers)


class ForwardIn(NamedTuple):
    qkv: jax.Array
    fc1: jax.Array
    fc2: jax.Array
    ov: jax.Array
    x: jax.Array
    cot: jax.Array
    key_ok: jax.Array


class ForwardOut(NamedTuple):
    wf1: jax.Array
    wf2: jax.Array
    cots: jax.Array
    mat_qkv: jax.Array
    queries: jax.Array
    keys: jax.Array
    values: jax.Array
    lse: jax.Array
    mixed_mine: jax.Array
    mixed: jax.Array
    ln1: jax.Array
    ln2: jax.Array
    base: jax.Array
    normed2: jax.Array
    rstd2: jax.Array
    normed1: jax.Array
    rstd1: jax.Array
    out_mine: jax.Array
    gain1: jax.Array
    gain2: jax.Array
    fc1_bias: jax.Array


class ForwardScratch(NamedTuple):
    cq: jax.Array
    cf: jax.Array
    rq: jax.Array
    rf: jax.Array
    mq: jax.Array
    mf: jax.Array
    wo: jax.Array
    mat_out: jax.Array
    xs: jax.Array
    vec: jax.Array
    qkv_all: jax.Array
    others: jax.Array
    loc_sem: jax.Array
    up_sem: jax.Array
    down_sem: jax.Array
    side_sem: jax.Array
    got_sem: jax.Array
    seq_send: jax.Array
    seq_recv: jax.Array
    ag_send: jax.Array
    ag_recv: jax.Array


FORWARD = ForwardIn._fields + ForwardOut._fields + ForwardScratch._fields


class Refs:
    def __init__(self, names, refs):
        self.__dict__.update(zip(names, refs))


def forward_kernel(plan, items, heads, *refs):
    r = Refs(FORWARD, refs)
    z, y, s = coords(plan)
    me = z * 2 + y
    line, seq, sub, cols, width = plan.line, plan.seq, plan.sub, plan.cols, plan.width
    slot = r.x.shape[0]
    scale = HEAD_DIM ** (-0.5)
    entry_barrier(plan, z, y, s)
    sources = dict(ov=r.ov, fc2=r.fc2, wq=r.mq, wf1=r.mf)

    def source(q):
        name, a, n = items[q]
        return sources[name].at[pl.ds(a, n)]

    def target(q, piece):
        name, a, n = items[q]
        if name == "ov":
            return r.wo.at[s, piece]
        if name == "wq":
            return r.mat_qkv.at[pl.ds(pl.multiple_of(piece * plan.rows_pad + a, 16), n)]
        return {"fc2": r.wf2, "wf1": r.wf1}[name].at[piece, pl.ds(a, n)]

    def hop(q, piece, src, way):
        img = {"up": me + 2, "down": me - 2, "side": z * 2 + 1 - y}[way]
        sem = {"up": r.up_sem, "down": r.down_sem, "side": r.side_sem}[way]
        return remote(src, target(q, piece), sem.at[q, piece], r.got_sem.at[q, piece], img, s)

    def own_copy(q):
        return pltpu.make_async_copy(source(q), target(q, me), r.loc_sem.at[q])

    def own(q):
        own_copy(q).start()
        hop(q, me, source(q), "side").start()

        @pl.when(z < line - 1)
        def _():
            hop(q, me, source(q), "up").start()

        @pl.when(z > 0)
        def _():
            hop(q, me, source(q), "down").start()

    def line_only(q, d):
        for yy in (y, 1 - y):
            low, high = (z - d) * 2 + yy, (z + d) * 2 + yy

            @pl.when(z - d >= 0)
            def _():
                hop(q, low, target(q, low), "up").wait_recv()

                @pl.when(z < line - 1)
                def _():
                    hop(q, low, target(q, low), "up").start()

            @pl.when(z + d < line)
            def _():
                hop(q, high, target(q, high), "down").wait_recv()

                @pl.when(z > 0)
                def _():
                    hop(q, high, target(q, high), "down").start()

    def from_side(q):
        other = z * 2 + 1 - y
        hop(q, other, target(q, other), "side").wait_recv()

        @pl.when(z < line - 1)
        def _():
            hop(q, other, target(q, other), "up").start()

        @pl.when(z > 0)
        def _():
            hop(q, other, target(q, other), "down").start()

    def pass_on(q, d):
        if q in across_first:
            if d == 1:
                from_side(q)
            line_only(q, d)
            return
        low = (z - d) * 2 + y
        high = (z + d) * 2 + y

        @pl.when(z - d >= 0)
        def _():
            hop(q, low, target(q, low), "side").wait_recv()
            hop(q, low, target(q, low), "side").start()

            @pl.when(z < line - 1)
            def _():
                hop(q, low, target(q, low), "up").start()

        @pl.when(z + d < line)
        def _():
            hop(q, high, target(q, high), "side").wait_recv()
            hop(q, high, target(q, high), "side").start()

            @pl.when(z > 0)
            def _():
                hop(q, high, target(q, high), "down").start()

    def wait_side(q):
        for zs in range(line):
            piece = zs * 2 + 1 - y
            if q not in across_first:
                hop(q, piece, target(q, piece), "side").wait_recv()
        own_copy(q).wait()

    def exchange(a, src, dst, k):
        peer = lax.rem(s + k, seq)
        return remote(src, dst, r.seq_send.at[a, k], r.seq_recv.at[a, k], me, peer)

    def came_from(k):
        return lax.rem(s + seq - k, seq)

    def item(name):
        return [q for q in range(len(items)) if items[q][0] == name]

    def rows_of(t):
        return pl.ds(pl.multiple_of(t * slot, slot), slot)

    across_first = item("fc2")[-ACROSS:] if ACROSS else []

    own(item("ov")[0])
    early = item("fc2")[:1]
    for q in early:
        own(q)
    x_copy = pltpu.make_async_copy(r.x, r.xs.at[rows_of(s)], r.loc_sem.at[len(items)])
    cot_copy = pltpu.make_async_copy(r.cot, r.cots.at[s], r.loc_sem.at[len(items) + 1])
    r.cq[...] = jnp.zeros_like(r.cq)
    for t in range(seq):
        for j in range(3):
            at = j * width + t * cols
            r.cq[t, :sub, j * cols : (j + 1) * cols] = r.qkv[:, at : at + cols]
    for k in range(1, seq):
        exchange(0, r.cq.at[lax.rem(s + k, seq)], r.rq.at[s], k).start()
    x_copy.start()
    for k in range(1, seq):
        exchange(2, r.x, r.xs.at[rows_of(s)], k).start()
    r.cf[...] = jnp.zeros_like(r.cf)
    for g in range(plan.devices):
        i, t = g // seq, g % seq
        a, b = plan.first[g], plan.last[g]
        r.cf[t, :sub, i * plan.block : i * plan.block + b - a] = r.fc1[:, a:b]
    for k in range(1, seq):
        exchange(1, r.cf.at[lax.rem(s + k, seq)], r.rf.at[s], k).start()
    wq, late = item("wq"), [q for q in item("fc2") if q not in early]

    def merge(a, sent, got, merged):
        for k in range(1, seq):
            exchange(a, sent.at[lax.rem(s + k, seq)], got.at[came_from(k)], k).wait()
        got[s] = sent[s]
        for t in range(seq):
            merged[t * sub : (t + 1) * sub, :] = got[t, :sub, :]

    def all_on(queue, d):
        for q in queue:
            pass_on(q, d)

    merge(0, r.cq, r.rq, r.mq)
    own(wq[0])
    all_on(item("ov"), 1)
    for q in late:
        own(q)
    merge(1, r.cf, r.rf, r.mf)
    all_on(wq, 1)
    for d in range(2, line):
        all_on(item("ov"), d)
    for q in item("wf1"):
        own(q)
    for d in range(2, line):
        all_on(wq, d)
    all_on(early, 1)
    wait_side(item("ov")[0])
    for k in range(1, seq):
        exchange(4, r.wo.at[s], r.wo.at[s], k).start()
    cot_copy.start()
    for k in range(1, seq):
        exchange(3, r.cot, r.cots.at[s], k).start()
    all_on(late, 1)
    for d in range(2, line):
        all_on(early, d)

    rest = [(q, 1) for q in item("wf1")]
    rest += [(q, d) for d in range(2, line) for q in late + item("wf1")]

    def service(n=1):
        for _ in range(n):
            if rest:
                pass_on(*rest.pop(0))

    x_copy.wait()
    for k in range(1, seq):
        exchange(2, r.x, r.xs.at[rows_of(came_from(k))], k).wait()
    for k in range(1, seq):
        exchange(4, r.wo.at[s], r.wo.at[came_from(k)], k).wait()
    count = plan.shard_vec
    for g in range(plan.devices):
        i, t = g // seq, g % seq
        r.vec[:, g * count : (g + 1) * count] = r.wo[t, i, sub : sub + 1, :count].astype(F32)
        r.mat_out[g * sub : (g + 1) * sub, :] = r.wo[t, i, :sub, :]
    service()
    bias1, v_bias, gain1, q_bias, out_bias, gain2, bias2, fc2_bias = (
        r.vec[:, n * width : (n + 1) * width] for n in range(8)
    )
    r.gain1[...] = gain1
    r.gain2[...] = gain2
    r.fc1_bias[...] = jnp.zeros_like(r.fc1_bias)
    for t in range(seq):

        @pl.when(s == t)
        def _():
            for i in range(plan.img):
                a, b = plan.first[i * seq + t], plan.last[i * seq + t]
                to = i * plan.block
                r.fc1_bias[:, to : to + b - a] = r.vec[:, 8 * width + a : 8 * width + b]
            r.out_mine[...] = r.mat_out[t * cols : (t + 1) * cols, :]

    for t in range(seq):
        rows = slice(t * slot, (t + 1) * slot)
        normed, rstd = normalize(r.xs[rows, :].astype(F32))
        r.ln1[rows, :] = (normed * gain1 + bias1).astype(BF16)

        @pl.when(s == t)
        def _():
            r.normed1[...] = normed
            r.rstd1[...] = rstd

        service()

    for q in item("wq"):
        wait_side(q)
    for t in range(seq):
        rows = slice(t * slot, (t + 1) * slot)
        r.qkv_all[rows, :] = jnp.dot(
            r.ln1[rows, :], r.mat_qkv[...], preferred_element_type=F32
        )
        service()
    for t in range(seq):

        @pl.when(s == t)
        def _():
            lanes = slice(t * cols, (t + 1) * cols)
            r.qkv_all[:, :cols] += q_bias[:, lanes]
            r.qkv_all[:, 2 * cols : 3 * cols] += v_bias[:, lanes]

    for h in range(heads):
        for j, out in enumerate((r.queries, r.keys, r.values)):
            at = j * cols + h * HEAD_DIM
            out[h] = r.qkv_all[:, at : at + HEAD_DIM].astype(BF16)
    tile = 2 * slot
    for h in range(heads):
        lanes = slice(h * HEAD_DIM, (h + 1) * HEAD_DIM)
        key, value = r.keys[h], r.values[h]
        for at in range(0, seq * slot, tile):
            rows = slice(at, at + tile)
            scores = dot_t(r.queries[h, rows, :], key) * scale
            scores = jnp.where(r.key_ok[...] > 0, scores, -1e30)
            top = jnp.max(scores, axis=-1, keepdims=True)
            terms = jnp.exp(scores - top)
            total = jnp.sum(terms, axis=-1, keepdims=True)
            r.lse[h, rows, :] = top + jnp.log(total)
            probs = (terms * (1.0 / total)).astype(BF16)
            r.mixed_mine[rows, lanes] = jnp.dot(
                probs, value, preferred_element_type=F32
            ).astype(BF16)
            service()

    core = lax.rem(s, 2)
    mate, cross = s + 1 - 2 * core, lax.rem(s + 2, seq)

    def share(part, to, n):
        src = r.mixed_mine if n < 2 else r.others.at[part]
        return remote(src, r.others.at[part], r.ag_send.at[n], r.ag_recv.at[n], me, to)

    share(s, cross, 0).start()
    share(s, mate, 1).start()
    r.others[s] = r.mixed_mine[...]
    service()
    share(cross, cross, 0).wait_recv()
    share(cross, mate, 2).start()
    service()
    share(mate, mate, 1).wait_recv()
    share(lax.rem(mate + 2, seq), mate, 2).wait_recv()
    for t in range(seq):
        r.mixed[:, t * cols : (t + 1) * cols] = r.others[t]
    for t in range(seq):
        rows = slice(t * slot, (t + 1) * slot)
        resid = (
            r.xs[rows, :].astype(F32)
            + jnp.dot(r.mixed[rows, :], r.mat_out[...], preferred_element_type=F32)
            + out_bias
        )
        normed, rstd = normalize(resid)
        r.ln2[rows, :] = (normed * gain2 + bias2).astype(BF16)

        @pl.when(s == t)
        def _():
            r.base[...] = resid + fc2_bias
            r.normed2[...] = normed
            r.rstd2[...] = rstd

        service()
    service(len(rest))
    for q in item("fc2") + item("wf1"):
        wait_side(q)

    def wait_sends(q, piece, zs):
        @pl.when(jnp.logical_and(z < line - 1, zs <= z))
        def _():
            hop(q, piece, target(q, piece), "up").wait_send()

        @pl.when(jnp.logical_and(z > 0, zs >= z))
        def _():
            hop(q, piece, target(q, piece), "down").wait_send()

    for q in range(len(items)):
        if q in across_first:
            hop(q, me, target(q, me), "side").wait_send()
        for zs in range(line):
            wait_sends(q, zs * 2 + y, zs)
            if q in across_first:
                wait_sends(q, zs * 2 + 1 - y, zs)
            else:
                hop(q, zs * 2 + y, target(q, zs * 2 + y), "side").wait_send()

    cot_copy.wait()
    for k in range(1, seq):
        exchange(3, r.cot, r.cots.at[came_from(k)], k).wait()
    share(s, cross, 0).wait_send()
    share(s, mate, 1).wait_send()
    share(cross, mate, 2).wait_send()


def forward(plan, slot, heads, args):
    any_spec = pl.BlockSpec(memory_space=pl.ANY)
    vmem = pl.BlockSpec(memory_space=pltpu.VMEM)
    img, seq, width, cols = plan.img, plan.seq, plan.width, plan.cols
    tokens = seq * slot
    dma = pltpu.SemaphoreType.DMA
    shape = jax.ShapeDtypeStruct
    items = [("ov", 0, plan.sub_pad)]
    step = 48
    for name, rows, by in (
        ("fc2", plan.block, step),
        ("wq", plan.rows_pad, plan.rows_pad),
        ("wf1", plan.rows_pad, step),
    ):
        items += [(name, a, min(by, rows - a)) for a in range(0, rows, by)]
    n = len(items)
    head = shape((heads, tokens, HEAD_DIM), BF16)
    all16 = shape((tokens, width), BF16)
    own32 = shape((slot, width), F32)
    column = shape((slot, 1), F32)
    row = shape((1, width), F32)
    outs = (
        shape((img, plan.rows_pad, plan.units), BF16),
        shape((img, plan.block, width), BF16),
        shape((seq, slot, width), BF16),
        shape((img * plan.rows_pad, plan.qkv_cols), BF16),
        head,
        head,
        head,
        shape((heads, tokens, 1), F32),
        shape((tokens, cols), BF16),
        all16,
        all16,
        all16,
        own32,
        own32,
        column,
        own32,
        column,
        shape((cols, width), BF16),
        row,
        row,
        shape((1, plan.units), F32),
    )
    result = pl.pallas_call(
        functools.partial(forward_kernel, plan, items, heads),
        out_shape=outs,
        in_specs=[vmem, vmem, any_spec, any_spec, vmem, any_spec, vmem],
        out_specs=(any_spec,) * 3 + (vmem,) * (len(outs) - 3),
        scratch_shapes=[
            pltpu.VMEM((seq, plan.sub_pad, plan.qkv_cols), BF16),
            pltpu.VMEM((seq, plan.sub_pad, plan.units), BF16),
            pltpu.VMEM((seq, plan.sub_pad, plan.qkv_cols), BF16),
            pltpu.VMEM((seq, plan.sub_pad, plan.units), BF16),
            pltpu.VMEM((plan.rows_pad, plan.qkv_cols), BF16),
            pltpu.VMEM((plan.rows_pad, plan.units), BF16),
            pltpu.VMEM((seq, img, plan.sub_pad, width), BF16),
            pltpu.VMEM((width, width), BF16),
            pltpu.VMEM((tokens, width), BF16),
            pltpu.VMEM((1, plan.shard_vec * plan.devices), F32),
            pltpu.VMEM((tokens, plan.qkv_cols), F32),
            pltpu.VMEM((seq, tokens, cols), BF16),
            dma((n + 2,)),
            *[dma((n, img))] * 4,
            *[dma((5, seq))] * 2,
            *[dma((3,))] * 2,
        ],
        compiler_params=pltpu.CompilerParams(
            collective_id=0, has_side_effects=True, vmem_limit_bytes=VMEM_LIMIT
        ),
        name="forward",
    )(*[args[name] for name in ForwardIn._fields])
    return Refs(ForwardOut._fields, result)


def dot_00(left, right):
    return lax.dot_general(left, right, (((0,), (0,)), ((), ())), preferred_element_type=F32)


def dot_t(left, right):
    return lax.dot_general(left, right, (((1,), (1,)), ((), ())), preferred_element_type=F32)


def norm_back(grad_in, normed, rstd, gain):
    scaled = grad_in * gain
    return rstd * (
        scaled
        - jnp.mean(scaled, axis=-1, keepdims=True)
        - normed * jnp.mean(scaled * normed, axis=-1, keepdims=True)
    )


class BackwardIn(NamedTuple):
    g2: jax.Array
    g1: jax.Array
    ln2_part: jax.Array
    out_part: jax.Array
    normed2: jax.Array
    rstd2: jax.Array
    gain2: jax.Array
    grad_y: jax.Array
    base: jax.Array
    rowmask: jax.Array
    queries: jax.Array
    keys: jax.Array
    values: jax.Array
    lse: jax.Array
    key_ok: jax.Array
    mixed_mine: jax.Array
    mixed: jax.Array
    ln1: jax.Array
    mat_qkv: jax.Array
    out_mine: jax.Array
    normed1: jax.Array
    rstd1: jax.Array
    gain1: jax.Array
    pre_sums: jax.Array


class BackwardOut(NamedTuple):
    output: jax.Array
    input_grad: jax.Array
    o2: jax.Array
    o1: jax.Array
    oq: jax.Array
    oo: jax.Array
    ov: jax.Array


class BackwardScratch(NamedTuple):
    side2: jax.Array
    side1: jax.Array
    sidem: jax.Array
    sidev: jax.Array
    low2: jax.Array
    low1: jax.Array
    lowm: jax.Array
    lowv: jax.Array
    high2: jax.Array
    high1: jax.Array
    highm: jax.Array
    highv: jax.Array
    acc2: jax.Array
    acc1: jax.Array
    accm: jax.Array
    accv: jax.Array
    fin1: jax.Array
    finm: jax.Array
    cut1: jax.Array
    cutm: jax.Array
    cutv: jax.Array
    got1: jax.Array
    gotm: jax.Array
    gmix: jax.Array
    gvec: jax.Array
    gvec32: jax.Array
    front: jax.Array
    rest: jax.Array
    qsum: jax.Array
    vsum: jax.Array
    pair_ln2: jax.Array
    cross_ln2: jax.Array
    sum_ln2: jax.Array
    pair_out: jax.Array
    cross_out: jax.Array
    sum_out: jax.Array
    pair_ln1: jax.Array
    cross_ln1: jax.Array
    sum_ln1: jax.Array
    own_resid: jax.Array
    all_resid: jax.Array
    resid32: jax.Array
    gm: jax.Array
    gqkv: jax.Array
    part_ln1: jax.Array
    cols_resid: jax.Array
    side_send: jax.Array
    side_recv: jax.Array
    low_send: jax.Array
    low_recv: jax.Array
    high_send: jax.Array
    high_recv: jax.Array
    seq_send: jax.Array
    seq_recv: jax.Array
    rs_send: jax.Array
    rs_recv: jax.Array
    ag_send: jax.Array
    ag_recv: jax.Array


BACKWARD = BackwardIn._fields + BackwardOut._fields + BackwardScratch._fields


def backward_kernel(plan, parts, heads, *refs):
    r = Refs(BACKWARD, refs)
    z, y, s = coords(plan)
    me = z * 2 + y
    line, seq, sub, cols = plan.line, plan.seq, plan.sub, plan.cols
    width = plan.width
    slot = r.output.shape[0]
    scale = HEAD_DIM ** (-0.5)
    entry_barrier(plan, z, y, s)
    grads = [r.g2, r.g1, r.gmix, r.gvec]
    tall = [plan.block, plan.rows_pad, plan.rows_pad, 16]
    sides = [r.side2, r.side1, r.sidem, r.sidev]
    lows = [r.low2, r.low1, r.lowm, r.lowv]
    highs = [r.high2, r.high1, r.highm, r.highv]
    accs = [r.acc2, r.acc1, r.accm, r.accv]

    def at(c):
        q, a, n = parts[c]
        return q, pl.ds(a, n)

    def piece(c, img):
        q, a, n = parts[c]
        return grads[q].at[pl.ds(pl.multiple_of(img * tall[q] + a, 16), n)]

    def to_side(c, dest):
        q, w = at(c)
        return remote(
            piece(c, dest * 2 + 1 - y),
            sides[q].at[dest, w],
            r.side_send.at[c, dest],
            r.side_recv.at[c, dest],
            z * 2 + 1 - y,
            s,
        )

    def to_up(c, dest):
        q, w = at(c)
        return remote(
            accs[q].at[dest, w],
            lows[q].at[dest, w],
            r.low_send.at[c, dest],
            r.low_recv.at[c, dest],
            me + 2,
            s,
        )

    def to_down(c, dest):
        q, w = at(c)
        return remote(
            accs[q].at[dest, w],
            highs[q].at[dest, w],
            r.high_send.at[c, dest],
            r.high_recv.at[c, dest],
            me - 2,
            s,
        )

    def send_side(c):
        for d in range(line - 1, -1, -1):

            @pl.when(z + d < line)
            def _():
                to_side(c, z + d).start()

            if d:

                @pl.when(z - d >= 0)
                def _():
                    to_side(c, z - d).start()

    def both(c, dest):
        q, w = at(c)
        to_side(c, dest).wait_recv()
        return piece(c, dest * 2 + y)[...].astype(F32) + sides[q][dest, w, :].astype(F32)

    def pass_on(c):
        q, w = at(c)
        for d in range(line - 1, 0, -1):

            @pl.when(z + d < line)
            def _():
                dest = z + d
                total = both(c, dest)

                @pl.when(z > 0)
                def _():
                    to_up(c, dest).wait_recv()
                    accs[q][dest, w, :] = (total + lows[q][dest, w, :].astype(F32)).astype(BF16)

                @pl.when(z == 0)
                def _():
                    accs[q][dest, w, :] = total.astype(BF16)

                to_up(c, dest).start()

            @pl.when(z - d >= 0)
            def _():
                dest = z - d
                total = both(c, dest)

                @pl.when(z < line - 1)
                def _():
                    to_down(c, dest).wait_recv()
                    accs[q][dest, w, :] = (total + highs[q][dest, w, :].astype(F32)).astype(BF16)

                @pl.when(z == line - 1)
                def _():
                    accs[q][dest, w, :] = total.astype(BF16)

                to_down(c, dest).start()

    outs = [r.o2, r.fin1, r.finm, None]

    def finish(c):
        q, w = at(c)
        total = both(c, z)

        def store(value):
            if q == 3:
                r.cutv[s, w, :] = value.astype(BF16)
            else:
                outs[q][w, :] = value

        @pl.when(z == 0)
        def _():
            to_down(c, z).wait_recv()
            store(total + highs[q][z, w, :].astype(F32))

        @pl.when(z == line - 1)
        def _():
            to_up(c, z).wait_recv()
            store(total + lows[q][z, w, :].astype(F32))

        @pl.when(jnp.logical_and(z > 0, z < line - 1))
        def _():
            to_down(c, z).wait_recv()
            to_up(c, z).wait_recv()
            store(total + lows[q][z, w, :].astype(F32) + highs[q][z, w, :].astype(F32))

    def exchange(a, src, dst, k):
        peer = lax.rem(s + k, seq)
        return remote(src, dst, r.seq_send.at[a, k], r.seq_recv.at[a, k], me, peer)

    def came_from(k):
        return lax.rem(s + seq - k, seq)

    ends = {max(c for c in range(len(parts)) if parts[c][0] == q): q for q in (1, 2, 3)}

    def after(c):
        if c not in ends:
            return
        q = ends[c]
        if q == 3:
            for k in range(1, seq):
                exchange(2, r.cutv.at[s], r.ov.at[s], k).start()
            return
        fin, cut, got = ((r.fin1, r.cut1, r.got1), (r.finm, r.cutm, r.gotm))[q - 1]
        for t in range(seq):
            cut[t, :sub, :] = fin[t * sub : (t + 1) * sub, :].astype(BF16)
        for k in range(1, seq):
            exchange(q - 1, cut.at[lax.rem(s + k, seq)], got.at[s], k).start()

    def service(c):
        if c < len(parts):
            pass_on(c)
        if c >= 1:
            finish(c - 1)
            after(c - 1)

    core, far = lax.rem(s, 2), s // 2
    mate, cross = s + 1 - 2 * core, lax.rem(s + 2, seq)

    def rows_of(t):
        return pl.ds(pl.multiple_of(t * slot, slot), slot)

    def to_mate(n, part, pair, h):
        return remote(
            part.at[rows_of(h * 2 + 1 - core)],
            pair.at[h],
            r.rs_send.at[n, h],
            r.rs_recv.at[n, h],
            me,
            mate,
        )

    def to_cross(n, summed, got):
        return remote(summed, got, r.rs_send.at[n, 2], r.rs_recv.at[n, 2], me, cross)

    def sum_start(n, part, pair):
        to_mate(n, part, pair, 1 - far).start()
        to_mate(n, part, pair, far).start()

    def sum_across(n, part, pair, summed, got):
        to_mate(n, part, pair, 1 - far).wait_recv()
        summed[...] = (
            part[rows_of(cross), :].astype(F32) + pair[1 - far].astype(F32)
        ).astype(BF16)
        to_cross(n, summed, got).start()

    def sum_end(n, part, pair, summed, got):
        to_mate(n, part, pair, far).wait_recv()
        to_cross(n, summed, got).wait_recv()
        to_mate(n, part, pair, far).wait_send()
        to_mate(n, part, pair, 1 - far).wait_send()
        to_cross(n, summed, got).wait_send()
        return part[rows_of(s), :].astype(F32) + pair[far].astype(F32) + got[...].astype(F32)

    ln2_args = (0, r.ln2_part, r.pair_ln2)
    out_args = (1, r.out_part, r.pair_out)
    ln1_args = (2, r.part_ln1, r.pair_ln1)

    sum_start(*ln2_args)
    first_mix = min(c for c in range(len(parts)) if parts[c][0] == 2)
    for c in range(first_mix):
        send_side(c)
    r.rest[...] = jnp.zeros_like(r.rest)
    r.rest[:, 5 * width : 6 * width] = jnp.sum(r.grad_y[...], axis=0, keepdims=True)
    for t in range(seq):

        @pl.when(s == t)
        def _():
            for i in range(plan.img):
                a, b = plan.first[i * seq + t], plan.last[i * seq + t]
                at = i * plan.block
                r.rest[:, 6 * width + a : 6 * width + b] += r.pre_sums[:, at : at + b - a]

    r.gqkv[...] = jnp.zeros_like(r.gqkv)
    r.gvec32[...] = jnp.zeros_like(r.gvec32)
    sum_across(*ln2_args, r.sum_ln2, r.cross_ln2)
    sum_start(*out_args)
    grad_ln2 = sum_end(*ln2_args, r.sum_ln2, r.cross_ln2)
    grad_resid = r.grad_y[...] + norm_back(grad_ln2, r.normed2[...], r.rstd2[...], r.gain2[...])
    r.own_resid[...] = grad_resid.astype(BF16)
    r.resid32[...] = grad_resid

    def gather_resid(part, to, n):
        rows = r.all_resid.at[rows_of(part)]
        src = r.own_resid if n < 2 else rows
        return remote(src, rows, r.ag_send.at[n], r.ag_recv.at[n], me, to)

    gather_resid(s, cross, 0).start()
    gather_resid(s, mate, 1).start()
    r.all_resid[rows_of(s), :] = r.own_resid[...]
    r.rest[:, 2 * width : 3 * width] = jnp.sum(grad_resid, axis=0, keepdims=True)
    r.rest[:, 3 * width : 4 * width] = jnp.sum(grad_ln2 * r.normed2[...], axis=0, keepdims=True)
    r.rest[:, 4 * width : 5 * width] = jnp.sum(grad_ln2, axis=0, keepdims=True)
    service(0)
    gather_resid(cross, cross, 0).wait_recv()
    gather_resid(cross, mate, 2).start()
    sum_across(*out_args, r.sum_out, r.cross_out)
    gather_resid(mate, mate, 1).wait_recv()
    gather_resid(lax.rem(mate + 2, seq), mate, 2).wait_recv()

    for t in range(seq):
        rows = slice(t * slot, (t + 1) * slot)
        r.gm[rows, :] = dot_t(r.all_resid[rows, :], r.out_mine[...]).astype(BF16)

        @pl.when(s == t)
        def _():
            r.cols_resid[...] = r.all_resid[:, t * cols : (t + 1) * cols]

    tile = 2 * slot
    for h in range(heads):
        lanes = slice(h * HEAD_DIM, (h + 1) * HEAD_DIM)
        key, value = r.keys[h], r.values[h]
        grad_value = jnp.zeros((seq * slot, HEAD_DIM), F32)
        grad_key = jnp.zeros((seq * slot, HEAD_DIM), F32)
        query_sum = jnp.zeros((1, HEAD_DIM), F32)
        for at_row in range(0, seq * slot, tile):
            rows = slice(at_row, at_row + tile)
            query, gm = r.queries[h, rows, :], r.gm[rows, lanes]
            scores = dot_t(query, key) * scale
            scores = jnp.where(r.key_ok[...] > 0, scores, -1e30)
            probs = jnp.exp(scores - r.lse[h, rows, :])
            grad_value += dot_00(probs.astype(BF16), gm)
            delta = jnp.sum(
                gm.astype(F32) * r.mixed_mine[rows, lanes].astype(F32), axis=-1, keepdims=True
            )
            grad_scores = (probs * (dot_t(gm, value) - delta) * scale).astype(BF16)
            grad_query = jnp.dot(grad_scores, key, preferred_element_type=F32)
            grad_key += dot_00(grad_scores, query)
            r.gqkv[rows, lanes] = grad_query.astype(BF16)
            query_sum += jnp.sum(grad_query, axis=0, keepdims=True)
        r.qsum[:, lanes] = query_sum
        r.vsum[:, lanes] = jnp.sum(grad_value, axis=0, keepdims=True)
        for j, grad in ((1, grad_key), (2, grad_value)):
            to = j * cols + h * HEAD_DIM
            r.gqkv[:, to : to + HEAD_DIM] = grad.astype(BF16)
        if h % 2 == 1:
            service(1 + h // 2)

    for t in range(seq):
        rows = slice(t * slot, (t + 1) * slot)
        r.part_ln1[rows, :] = dot_t(r.gqkv[rows, :], r.mat_qkv[...]).astype(BF16)
    sum_start(*ln1_args)
    for m in range(0, width, LANES):
        grad = jnp.concatenate(
            [
                dot_00(r.ln1[:, m : m + LANES], r.gqkv[...])[:, : 3 * cols],
                dot_00(r.mixed[:, m : m + LANES], r.cols_resid[...]),
            ],
            axis=1,
        )
        r.gmix[m : m + LANES, :] = grad.astype(BF16)
    for c in range(first_mix, len(parts) - 1):
        send_side(c)
    sum_across(*ln1_args, r.sum_ln1, r.cross_ln1)
    out_terms = sum_end(*out_args, r.sum_out, r.cross_out)
    r.output[...] = ((r.base[...] + out_terms) * r.rowmask[...]).astype(BF16)
    service(3)
    grad_ln1 = sum_end(*ln1_args, r.sum_ln1, r.cross_ln1)
    normed1 = r.normed1[...]
    r.input_grad[...] = r.resid32[...] + norm_back(grad_ln1, normed1, r.rstd1[...], r.gain1[...])

    r.front[...] = jnp.zeros_like(r.front)
    r.front[:, :width] = jnp.sum(grad_ln1, axis=0, keepdims=True)
    r.rest[:, :width] = jnp.sum(grad_ln1 * normed1, axis=0, keepdims=True)
    for t in range(seq):

        @pl.when(s == t)
        def _():
            lanes = slice(width + t * cols, width + (t + 1) * cols)
            r.front[:, lanes] = r.vsum[...]
            r.rest[:, lanes] = r.qsum[...]

    own_front = 2 * width // plan.devices
    own_rest = plan.shard_vec - own_front
    for g in range(plan.devices):
        row = g // seq * 16 + g % seq
        r.gvec32[row : row + 1, :own_front] = r.front[:, g * own_front : (g + 1) * own_front]
        r.gvec32[row : row + 1, own_front : own_front + own_rest] = r.rest[
            :, g * own_rest : (g + 1) * own_rest
        ]
    r.gvec[...] = r.gvec32[...].astype(BF16)
    send_side(len(parts) - 1)

    for c in range(4, first_mix + 1):
        service(c)
    service(first_mix + 1)
    r.got1[s] = r.cut1[s]
    for k in range(1, seq):
        exchange(0, r.cut1.at[lax.rem(s + k, seq)], r.got1.at[came_from(k)], k).wait()
    r.o1[...] = jnp.zeros_like(r.o1)
    for g in range(plan.devices):
        i, t = g // seq, g % seq
        a, b = plan.first[g], plan.last[g]
        r.o1[:, a:b] += r.got1[t, :sub, i * plan.block : i * plan.block + b - a].astype(F32)
    for c in range(first_mix + 2, len(parts) + 1):
        service(c)
    r.gotm[s] = r.cutm[s]
    r.ov[s] = r.cutv[s]
    for k in range(1, seq):
        exchange(1, r.cutm.at[lax.rem(s + k, seq)], r.gotm.at[came_from(k)], k).wait()
    for t in range(seq):
        for j in range(3):
            to = j * width + t * cols
            r.oq[:, to : to + cols] = r.gotm[t, :sub, j * cols : (j + 1) * cols].astype(F32)
        r.oo[:, t * cols : (t + 1) * cols] = r.gotm[t, :sub, 3 * cols : 4 * cols].astype(F32)
    for k in range(1, seq):
        exchange(2, r.cutv.at[s], r.ov.at[came_from(k)], k).wait()

    gather_resid(s, cross, 0).wait_send()
    gather_resid(s, mate, 1).wait_send()
    gather_resid(cross, mate, 2).wait_send()
    for c in range(len(parts)):
        for dest in range(line):
            to_side(c, dest).wait_send()

            @pl.when(dest > z)
            def _():
                to_up(c, dest).wait_send()

            @pl.when(dest < z)
            def _():
                to_down(c, dest).wait_send()


def backward(plan, slot, heads, args):
    vmem = pl.BlockSpec(memory_space=pltpu.VMEM)
    img, seq, width, line, cols = plan.img, plan.seq, plan.width, plan.line, plan.cols
    dma = pltpu.SemaphoreType.DMA
    shape = jax.ShapeDtypeStruct
    vec_pad = round_up(plan.shard_vec, LANES)
    parts = []
    step = 48
    for q, rows in ((0, plan.block), (1, plan.rows_pad), (2, plan.rows_pad)):
        parts += [(q, a, min(step, rows - a)) for a in range(0, rows, step)]
    parts.append((3, 0, 16))
    n = len(parts)
    mix = 4 * cols
    inner = [
        (plan.block, width),
        (plan.rows_pad, plan.units),
        (plan.rows_pad, mix),
        (16, vec_pad),
    ]
    buffers = [pltpu.VMEM((line, *dims), BF16) for _ in range(4) for dims in inner]
    own16 = pltpu.VMEM((slot, width), BF16)
    all16 = pltpu.VMEM((seq * slot, width), BF16)
    sums = [pltpu.VMEM((2, slot, width), BF16), own16, own16]
    scratch = buffers + [
        pltpu.VMEM(inner[1], F32),
        pltpu.VMEM(inner[2], F32),
        pltpu.VMEM((seq, plan.sub_pad, plan.units), BF16),
        pltpu.VMEM((seq, plan.sub_pad, mix), BF16),
        pltpu.VMEM((seq, 16, vec_pad), BF16),
        pltpu.VMEM((seq, plan.sub_pad, plan.units), BF16),
        pltpu.VMEM((seq, plan.sub_pad, mix), BF16),
        pltpu.VMEM((img * plan.rows_pad, mix), BF16),
        pltpu.VMEM((img * 16, vec_pad), BF16),
        pltpu.VMEM((img * 16, vec_pad), F32),
        pltpu.VMEM((1, 2 * width), F32),
        pltpu.VMEM((1, plan.shard_vec * plan.devices - 2 * width), F32),
        pltpu.VMEM((1, cols), F32),
        pltpu.VMEM((1, cols), F32),
        *sums,
        *sums,
        *sums,
        own16,
        all16,
        pltpu.VMEM((slot, width), F32),
        pltpu.VMEM((seq * slot, cols), BF16),
        pltpu.VMEM((seq * slot, plan.qkv_cols), BF16),
        all16,
        pltpu.VMEM((seq * slot, cols), BF16),
        *[dma((n, line))] * 6,
        *[dma((3, seq))] * 2,
        *[dma((3, 3))] * 2,
        *[dma((3,))] * 2,
    ]
    return pl.pallas_call(
        functools.partial(backward_kernel, plan, parts, heads),
        out_shape=(
            shape((slot, width), BF16),
            shape((slot, width), F32),
            shape((plan.block, width), F32),
            shape((plan.sub, plan.hidden), F32),
            shape((plan.sub, 3 * width), F32),
            shape((plan.sub, width), F32),
            shape((seq, 16, vec_pad), BF16),
        ),
        in_specs=[vmem] * len(BackwardIn._fields),
        out_specs=(vmem,) * len(BackwardOut._fields),
        scratch_shapes=scratch,
        compiler_params=pltpu.CompilerParams(
            collective_id=1, has_side_effects=True, vmem_limit_bytes=VMEM_LIMIT
        ),
        name="backward",
    )(*[args[name] for name in BackwardIn._fields])


def normalize(values):
    mean = jnp.mean(values, axis=-1, keepdims=True)
    centred = values - mean
    rstd = lax.rsqrt(jnp.mean(centred * centred, axis=-1, keepdims=True) + EPS)
    return (centred * rstd, rstd)


def gelu_parts(pre):
    inner = GELU_C * (pre + 0.044715 * pre * pre * pre)
    tanh_v = jnp.tanh(inner)
    value = 0.5 * pre * (1.0 + tanh_v)
    slope = 0.5 * (1.0 + tanh_v) + 0.5 * pre * (1.0 - tanh_v * tanh_v) * GELU_C * (
        1.0 + 3.0 * 0.044715 * pre * pre
    )
    return (value, slope)


def gather(value, axes):
    return lax.all_gather(value, axes, axis=0, tiled=True)


def scatter_sum(value, axes):
    return lax.psum_scatter(value, axes, scatter_dimension=0, tiled=True)


def weight_grad(left, right):
    return lax.dot_general(
        left, right, (((0,), (0,)), ((), ())), preferred_element_type=F32
    ).astype(BF16)


def batched(left, right, over_left, over_right):
    return lax.dot_general(
        left,
        right,
        (((over_left,), (over_right,)), ((0,), (0,))),
        preferred_element_type=F32,
    )


TILE = 2048


def pack(flat):
    padded = round_up(flat.shape[0], TILE)
    return jnp.pad(flat, (0, padded - flat.shape[0])).reshape(-1, LANES)


def unpack_blocks(packed, blocks, length):
    return packed.reshape(blocks, -1)[:, :length].reshape(-1)


def pack_blocks(flat, blocks):
    block = flat.reshape(blocks, -1)
    padded = round_up(block.shape[1], TILE)
    return jnp.pad(block, ((0, 0), (0, padded - block.shape[1]))).reshape(-1, LANES)


def shards_by_rows(tokens, counts, w_qkv, w_out, w_fc1, w_fc2, vectors, cotangent):
    f32 = jnp.float32
    bf16 = jnp.bfloat16
    width = tokens.shape[2]
    slot = tokens.shape[1]
    scale = HEAD_DIM ** (-0.5)
    position = lax.axis_index("seq")
    seq_count = lax.axis_size("seq")
    img_count = lax.axis_size("img")
    device_count = img_count * seq_count
    both = ("img", "seq")
    shard_qkv, shard_out, shard_fc1, shard_fc2, shard_vec = (
        w.shape[0] for w in (w_qkv, w_out, w_fc1, w_fc2, vectors)
    )
    hidden = shard_fc1 * device_count // width
    heads = HEADS // seq_count
    cols = width // seq_count
    units = hidden // seq_count
    rows = width // img_count
    pad_cols = round_up(3 * cols, LANES) - 3 * cols
    pad_units = round_up(units, LANES) - units
    to_quarter = [(c, (c % img_count) * seq_count + c // img_count) for c in range(device_count)]
    to_owner = [(b, a) for a, b in to_quarter]

    slice_counts = counts[0]
    key_valid = (jnp.arange(slot)[None, :] < slice_counts[:, None]).reshape(-1)
    row_valid = lax.dynamic_slice_in_dim(key_valid, position * slot, slot)
    rowmask = row_valid.astype(f32)[:, None]

    def mine(values):
        return lax.dynamic_slice_in_dim(values, position * slot, slot)

    shard_ov = shard_out + shard_vec
    local = gather(pack(jnp.concatenate([w_qkv, w_fc1, w_out, vectors])), "seq")
    local = local.reshape(seq_count, -1)
    x_all16 = gather(tokens[0], "seq")
    qkv_rows = local[:, :shard_qkv].reshape(rows, 3 * width)
    fc1_rows = local[:, shard_qkv : shard_qkv + shard_fc1].reshape(rows, hidden)
    ov_flat = local[:, shard_qkv + shard_fc1 : shard_qkv + shard_fc1 + shard_ov].reshape(-1)
    ov_cols = round_up(-(-ov_flat.shape[0] // rows), LANES)
    ov_part = jnp.pad(ov_flat, (0, rows * ov_cols - ov_flat.shape[0])).reshape(rows, ov_cols)
    qkv_part = jnp.concatenate(
        [
            lax.dynamic_slice_in_dim(qkv_rows, j * width + position * cols, cols, axis=1)
            for j in range(3)
        ]
        + [jnp.zeros((rows, pad_cols), bf16)],
        axis=1,
    )
    fc1_part = jnp.pad(
        lax.dynamic_slice_in_dim(fc1_rows, position * units, units, axis=1),
        ((0, 0), (0, pad_units)),
    )
    fc2_chunk = lax.ppermute(pack(w_fc2), both, to_quarter).reshape(-1)[:shard_fc2]
    fc2_part = jnp.pad(fc2_chunk.reshape(rows, units), ((0, 0), (0, pad_units)))
    weights = gather(jnp.concatenate([qkv_part, fc1_part, fc2_part, ov_part], axis=1), "img")
    end_qkv = 3 * cols + pad_cols
    end_fc1 = end_qkv + units + pad_units
    end_fc2 = end_fc1 + units + pad_units
    mat_qkv = weights[:, :end_qkv]
    mat_fc1 = weights[:, end_qkv:end_fc1]
    mat_fc2 = jnp.pad(
        weights[:, end_fc1 : end_fc1 + units].reshape(units, width), ((0, pad_units), (0, 0))
    )
    out_vec = weights[:, end_fc2:].reshape(img_count, -1)[:, : seq_count * shard_ov]
    cot_all = gather(cotangent[0], "seq")

    blocks_ov = out_vec.reshape(device_count, -1)
    mat_out = blocks_ov[:, :shard_out].reshape(width, width)
    vec = blocks_ov[:, shard_out : shard_out + shard_vec].reshape(-1).astype(f32)
    bias1, v_bias, gain1, q_bias, out_bias, gain2, bias2, fc2_bias = (
        vec[i * width : (i + 1) * width] for i in range(8)
    )
    fc1_bias = vec[8 * width : 8 * width + hidden]

    def my_cols(values):
        return lax.dynamic_slice_in_dim(values, position * cols, cols)

    fc1_bias_mine = jnp.pad(
        lax.dynamic_slice_in_dim(fc1_bias, position * units, units), (0, pad_units)
    )

    x = x_all16.astype(f32)
    normed1, _ = normalize(x)
    ln1 = (normed1 * gain1 + bias1).astype(bf16)
    qkv = jnp.dot(ln1, mat_qkv, preferred_element_type=f32)

    def by_head(values):
        return values.reshape(-1, heads, HEAD_DIM).transpose(1, 0, 2)

    def by_slot(values):
        return values.transpose(1, 0, 2).reshape(-1, cols)

    queries = by_head((qkv[:, :cols] + my_cols(q_bias)).astype(bf16))
    keys = by_head(qkv[:, cols : 2 * cols].astype(bf16))
    values = by_head((qkv[:, 2 * cols : 3 * cols] + my_cols(v_bias)).astype(bf16))
    scores = batched(queries, keys, 2, 2) * scale
    scores = jnp.where(key_valid[None, None, :], scores, -1e30)
    top = jnp.max(scores, axis=-1, keepdims=True)
    lse = top + jnp.log(jnp.sum(jnp.exp(scores - top), axis=-1, keepdims=True))
    probs = jnp.exp(scores - lse).astype(bf16)
    mixed_heads = batched(probs, values, 2, 1)
    mixed_mine = by_slot(mixed_heads).astype(bf16)
    mixed = lax.all_gather(mixed_mine, "seq", axis=0, tiled=True)
    mixed = (
        mixed.reshape(seq_count, -1, cols).transpose(1, 0, 2).reshape(-1, width)
    )
    resid = x + jnp.dot(mixed, mat_out, preferred_element_type=f32) + out_bias
    normed2, rstd2 = normalize(resid)
    ln2 = (normed2 * gain2 + bias2).astype(bf16)
    pre = jnp.dot(ln2, mat_fc1, preferred_element_type=f32) + fc1_bias_mine
    act_f, slope = gelu_parts(pre)
    act = act_f.astype(bf16)

    grad_y16 = jnp.where(key_valid[:, None], cot_all, jnp.zeros((), bf16))
    grad_pre = dot_t(grad_y16, mat_fc2) * slope
    grad_pre16 = grad_pre.astype(bf16)
    grad_ln2 = scatter_sum(dot_t(grad_pre16, mat_fc1).astype(bf16), "seq").astype(f32)
    grad_y = cotangent[0].astype(f32) * rowmask
    normed2_mine = mine(normed2)
    grad_resid = grad_y + norm_back(grad_ln2, normed2_mine, mine(rstd2), gain2)
    grad_resid16 = gather(grad_resid.astype(bf16), "seq")

    part_fc1 = weight_grad(ln2, grad_pre16)
    part_fc2 = pack_blocks(weight_grad(act, grad_y16)[:units].reshape(-1), img_count)
    out_terms = scatter_sum(
        jnp.dot(act, mat_fc2, preferred_element_type=f32).astype(bf16), "seq"
    ).astype(f32)
    output = ((mine(resid) + out_terms + fc2_bias) * rowmask).astype(bf16)

    out_mine = lax.dynamic_slice_in_dim(mat_out, position * cols, cols)
    gm = by_head(dot_t(grad_resid16, out_mine).astype(bf16))
    mixed_back = by_head(mixed_mine)
    delta = jnp.sum(gm.astype(f32) * mixed_back.astype(f32), axis=-1, keepdims=True)
    grad_values = by_slot(batched(probs, gm, 1, 1))
    dots = batched(gm, values, 2, 2)
    grad_scores = (jnp.exp(scores - lse) * (dots - delta) * scale).astype(bf16)
    grad_queries = by_slot(batched(grad_scores, keys, 2, 1))
    grad_keys = by_slot(batched(grad_scores, queries, 1, 1))
    grad_qkv16 = jnp.concatenate(
        [grad_queries.astype(bf16), grad_keys.astype(bf16), grad_values.astype(bf16)]
        + [jnp.zeros((seq_count * slot, pad_cols), bf16)],
        axis=1,
    )
    grad_ln1 = scatter_sum(dot_t(grad_qkv16, mat_qkv).astype(bf16), "seq").astype(f32)
    part_qkv = weight_grad(ln1, grad_qkv16)
    part_out = pack_blocks(weight_grad(mixed_mine, grad_resid16).reshape(-1), img_count)
    normed1_mine, rstd1_mine = normalize(tokens[0].astype(f32))
    input_grad = grad_resid + norm_back(grad_ln1, normed1_mine, rstd1_mine, gain1)

    def spread(part, full):
        return lax.dynamic_update_slice_in_dim(
            jnp.zeros((full,), f32), part, position * part.shape[0], 0
        )

    shard_front = 2 * width // device_count
    unused = shard_vec * device_count - 8 * width - hidden
    g_front = jnp.concatenate(
        [jnp.sum(grad_ln1, axis=0), spread(jnp.sum(grad_values, axis=0), width)]
    )
    g_rest = jnp.concatenate(
        [
            jnp.sum(grad_ln1 * normed1_mine, axis=0),
            spread(jnp.sum(grad_queries, axis=0), width),
            jnp.sum(grad_resid, axis=0),
            jnp.sum(grad_ln2 * normed2_mine, axis=0),
            jnp.sum(grad_ln2, axis=0),
            jnp.sum(grad_y, axis=0),
            spread(jnp.sum(grad_pre, axis=0)[:units], hidden),
            jnp.zeros((unused,), f32),
        ]
    )
    g_vec = jnp.concatenate(
        [g_front.reshape(device_count, -1), g_rest.reshape(device_count, -1)], axis=1
    )
    vec_pad = round_up(shard_vec, 4 * LANES)
    part_vec = jnp.pad(g_vec, ((0, 0), (0, vec_pad - shard_vec))).astype(bf16)

    parts = [
        part.reshape(img_count, -1, LANES)
        for part in (part_qkv, part_fc1, part_vec, part_fc2, part_out)
    ]
    sizes = [part.shape[1] for part in parts]
    summed = scatter_sum(jnp.concatenate(parts, axis=1).reshape(-1, LANES), "img")
    ends = [sum(sizes[: i + 1]) for i in range(5)]
    chunks = lax.ppermute(summed[ends[2] :], both, to_owner)
    grad_fc2 = chunks[: sizes[3]].reshape(-1)[:shard_fc2].astype(f32)
    grad_out = chunks[sizes[3] :].reshape(-1)[:shard_out].astype(f32)
    shared = gather(summed[: ends[2]], "seq").reshape(seq_count, ends[2], LANES)

    def own_block(packed, thirds, used, size):
        blocks = packed.reshape(seq_count, rows, -1)[:, :, : thirds * used]
        whole = blocks.reshape(seq_count, rows, thirds, used).transpose(1, 2, 0, 3)
        return lax.dynamic_slice_in_dim(whole.reshape(-1), position * size, size).astype(f32)

    grad_qkv = own_block(shared[:, : ends[0]], 3, cols, shard_qkv)
    grad_fc1 = own_block(shared[:, ends[0] : ends[1]], 1, units, shard_fc1)
    vec_sums = jnp.sum(shared[:, ends[1] :].astype(f32), axis=0).reshape(seq_count, vec_pad)
    vec_mine = lax.dynamic_slice_in_dim(vec_sums, position, 1).reshape(-1)
    return (
        output[None],
        input_grad[None],
        grad_qkv,
        grad_out,
        grad_fc1,
        grad_fc2,
        vec_mine[shard_front:shard_vec],
        vec_mine[:shard_front],
    )


def shards(tokens, counts, w_qkv, w_out, w_fc1, w_fc2, vectors, cotangent):
    width = tokens.shape[2]
    slot = tokens.shape[1]
    scale = HEAD_DIM ** (-0.5)
    position = lax.axis_index("seq")
    seq_count = lax.axis_size("seq")
    img_count = lax.axis_size("img")
    device_count = img_count * seq_count
    chunk = lax.axis_index("img") * seq_count + position
    shard_vec = vectors.shape[0]
    plan = Plan(img_count, seq_count, width, w_fc1.shape[0], shard_vec)
    hidden, cols, rows, units = plan.hidden, plan.cols, plan.rows, plan.units
    heads = HEADS // seq_count
    shard_fc = plan.shard_fc

    slice_counts = counts[0]
    key_valid = (jnp.arange(slot)[None, :] < slice_counts[:, None]).reshape(-1)
    row_valid = lax.dynamic_slice_in_dim(key_valid, position * slot, slot)
    rowmask = row_valid.astype(F32)[:, None]
    key_ok = key_valid.astype(F32)[None]

    shifts = sorted({g * shard_fc % width for g in range(device_count)})
    shift = lax.rem(chunk * shard_fc, width)
    fc2_flat = jnp.zeros((), BF16)
    for by in shifts:
        placed = jnp.pad(w_fc2, (by, plan.block * width - by - shard_fc))
        fc2_flat = jnp.where(shift == by, placed, fc2_flat)
    ov = jnp.concatenate(
        [
            w_out.reshape(plan.sub, width),
            jnp.pad(vectors, (0, width - shard_vec))[None],
            jnp.zeros((plan.sub_pad - plan.sub - 1, width), BF16),
        ]
    )
    f = forward(
        plan,
        slot,
        heads,
        dict(
            qkv=w_qkv.reshape(plan.sub, 3 * width),
            fc1=w_fc1.reshape(plan.sub, hidden),
            fc2=fc2_flat.reshape(plan.block, width),
            ov=ov,
            x=tokens[0],
            cot=cotangent[0],
            key_ok=key_ok,
        ),
    )
    mat_fc1 = f.wf1.reshape(width, units)
    mat_fc2 = f.wf2.reshape(units, width)
    cot_all = f.cots.reshape(seq_count * slot, width)
    pre = jnp.dot(f.ln2, mat_fc1, preferred_element_type=F32) + f.fc1_bias
    act_f, slope = gelu_parts(pre)
    act = act_f.astype(BF16)
    grad_y16 = jnp.where(key_valid[:, None], cot_all, jnp.zeros((), BF16))
    grad_pre = dot_t(grad_y16, mat_fc2) * slope
    grad_pre16 = grad_pre.astype(BF16)
    ln2_part = dot_t(grad_pre16, mat_fc1).astype(BF16)
    out_part = jnp.dot(act, mat_fc2, preferred_element_type=F32).astype(BF16)
    part_fc1 = weight_grad(f.ln2, grad_pre16)
    part_fc2 = weight_grad(act, grad_y16)

    output, input_grad, grad2, grad1, gradq, grado, gradv = backward(
        plan,
        slot,
        heads,
        dict(
            g2=part_fc2,
            g1=part_fc1,
            ln2_part=ln2_part,
            out_part=out_part,
            grad_y=cotangent[0].astype(F32) * rowmask,
            rowmask=rowmask,
            key_ok=key_ok,
            pre_sums=jnp.sum(grad_pre, axis=0, keepdims=True),
            **{name: getattr(f, name) for name in BackwardIn._fields if name in ForwardOut._fields},
        ),
    )
    grad_fc2 = lax.dynamic_slice_in_dim(grad2.reshape(-1), shift, shard_fc)
    shard_front = 2 * width // device_count
    vec_sums = jnp.sum(gradv.astype(F32), axis=0)
    vec_mine = lax.dynamic_slice_in_dim(vec_sums, position, 1).reshape(-1)
    return (
        output[None],
        input_grad[None],
        gradq.reshape(-1),
        grado.reshape(-1),
        grad1.reshape(-1),
        grad_fc2,
        vec_mine[shard_front:shard_vec],
        vec_mine[:shard_front],
    )


def solution(mesh):
    def layer(*arrays):
        width = arrays[0].shape[2]
        whole_rows = (
            width % mesh.size == 0
            and mesh.shape["seq"] == 4
            and width // mesh.shape["img"] % 16 == 0
        )
        return (shards if whole_rows else shards_by_rows)(*arrays)

    return jax.shard_map(
        layer,
        mesh=mesh,
        in_specs=(
            P("img", "seq", None),
            P("img", None),
            P(("img", "seq")),
            P(("img", "seq")),
            P(("img", "seq")),
            P(("img", "seq")),
            P(("img", "seq")),
            P("img", "seq", None),
        ),
        out_specs=(
            P("img", "seq", None),
            P("img", "seq", None),
            P(("img", "seq")),
            P(("img", "seq")),
            P(("img", "seq")),
            P(("img", "seq")),
            P(("img", "seq")),
            P(("img", "seq")),
        ),
        check_vma=False,
    )
```

```python
import functools
from typing import NamedTuple

import jax
import jax.numpy as jnp
from jax import lax
from jax.experimental import pallas as pl
from jax.experimental.pallas import tpu as pltpu
from jax.sharding import PartitionSpec as P

HEADS = 16
HEAD_DIM = 72
EPS = 1e-06
GELU_C = 0.7978845608028654
LANES = 128
VMEM_LIMIT = 58 * 1024 * 1024
ACROSS = 1
PACE = ((1, 1, 1, 0), (1, 1, 1, 1), (1, 1, 1, 1), (0, 0), (0, 0, 0, 0))
F32 = jnp.float32
BF16 = jnp.bfloat16


def round_up(value, step):
    return -(-value // step) * step


class Plan:
    def __init__(self, img, seq, width, shard_fc, shard_vec):
        self.img, self.seq, self.width = img, seq, width
        self.line = img // 2
        self.devices = img * seq
        self.hidden = shard_fc * self.devices // width
        self.cols = width // seq
        self.rows = width // img
        self.rows_pad = round_up(self.rows, 16)
        self.sub = self.rows // seq
        self.sub_pad = round_up(self.sub, 16)
        self.shard_fc, self.shard_vec = shard_fc, shard_vec
        self.first = [g * shard_fc // width for g in range(self.devices)]
        self.last = [-(-(g + 1) * shard_fc // width) for g in range(self.devices)]
        self.block = round_up(max(b - a for a, b in zip(self.first, self.last)), 16)
        self.units = img * self.block
        self.qkv_cols = round_up(3 * self.cols, LANES)
        self.mix_cols = round_up(4 * self.cols, LANES)


def coords(plan):
    index = lax.axis_index("img")
    return index // 2, lax.rem(index, 2), lax.axis_index("seq")


def remote(src, dst, send, recv, img, seq):
    return pltpu.make_async_remote_copy(
        src_ref=src,
        dst_ref=dst,
        send_sem=send,
        recv_sem=recv,
        device_id=(img, seq),
        device_id_type=pl.DeviceIdType.MESH,
    )


def entry_barrier(plan, z, y, s):
    barrier = pltpu.get_barrier_semaphore()

    def greet(img, seq):
        pl.semaphore_signal(
            barrier, inc=1, device_id=(img, seq), device_id_type=pl.DeviceIdType.MESH
        )

    @pl.when(z > 0)
    def _():
        greet((z - 1) * 2 + y, s)

    @pl.when(z < plan.line - 1)
    def _():
        greet((z + 1) * 2 + y, s)

    greet(z * 2 + 1 - y, s)
    for k in range(1, plan.seq):
        greet(z * 2 + y, lax.rem(s + k, plan.seq))
    peers = plan.seq + jnp.minimum(z, 1) + jnp.minimum(plan.line - 1 - z, 1)
    pl.semaphore_wait(barrier, peers)


class ForwardIn(NamedTuple):
    qkv: jax.Array
    fc1: jax.Array
    fc2: jax.Array
    ov: jax.Array
    vec_in: jax.Array
    x: jax.Array
    cot: jax.Array
    key_ok: jax.Array


class ForwardOut(NamedTuple):
    wf1: jax.Array
    wf2: jax.Array
    cots: jax.Array
    mat_qkv: jax.Array
    queries: jax.Array
    keys: jax.Array
    values: jax.Array
    lse: jax.Array
    mixed_mine: jax.Array
    mixed: jax.Array
    ln1: jax.Array
    ln2: jax.Array
    base: jax.Array
    normed2: jax.Array
    rstd2: jax.Array
    normed1: jax.Array
    rstd1: jax.Array
    out_mine: jax.Array
    gain1: jax.Array
    gain2: jax.Array
    fc1_bias: jax.Array


class ForwardScratch(NamedTuple):
    cq: jax.Array
    cf: jax.Array
    rq: jax.Array
    rf: jax.Array
    mq: jax.Array
    mf: jax.Array
    wo: jax.Array
    vecs: jax.Array
    mat_out: jax.Array
    xs: jax.Array
    vec: jax.Array
    qkv_all: jax.Array
    others: jax.Array
    loc_sem: jax.Array
    up_sem: jax.Array
    down_sem: jax.Array
    side_sem: jax.Array
    got_sem: jax.Array
    seq_send: jax.Array
    seq_recv: jax.Array
    ag_send: jax.Array
    ag_recv: jax.Array


FORWARD = ForwardIn._fields + ForwardOut._fields + ForwardScratch._fields


class Refs:
    def __init__(self, names, refs):
        self.__dict__.update(zip(names, refs))


def forward_kernel(plan, items, heads, *refs):
    r = Refs(FORWARD, refs)
    z, y, s = coords(plan)
    me = z * 2 + y
    line, seq, sub, cols, width = plan.line, plan.seq, plan.sub, plan.cols, plan.width
    slot = r.x.shape[0]
    scale = HEAD_DIM ** (-0.5)
    entry_barrier(plan, z, y, s)
    sources = dict(vec=r.vec_in, ov=r.ov, fc2=r.fc2, wq=r.mq, wf1=r.mf)

    def source(q):
        name, a, n = items[q]
        return sources[name].at[pl.ds(a, n)]

    def target(q, piece):
        name, a, n = items[q]
        if name == "vec":
            return r.vecs.at[s, piece]
        if name == "ov":
            return r.wo.at[s, piece]
        if name == "wq":
            return r.mat_qkv.at[pl.ds(pl.multiple_of(piece * plan.rows_pad + a, 16), n)]
        return {"fc2": r.wf2, "wf1": r.wf1}[name].at[piece, pl.ds(a, n)]

    def hop(q, piece, src, way):
        img = {"up": me + 2, "down": me - 2, "side": z * 2 + 1 - y}[way]
        sem = {"up": r.up_sem, "down": r.down_sem, "side": r.side_sem}[way]
        return remote(src, target(q, piece), sem.at[q, piece], r.got_sem.at[q, piece], img, s)

    def own_copy(q):
        return pltpu.make_async_copy(source(q), target(q, me), r.loc_sem.at[q])

    def own(q):
        own_copy(q).start()
        hop(q, me, source(q), "side").start()

        @pl.when(z < line - 1)
        def _():
            hop(q, me, source(q), "up").start()

        @pl.when(z > 0)
        def _():
            hop(q, me, source(q), "down").start()

    def line_only(q, d):
        for yy in (y, 1 - y):
            low, high = (z - d) * 2 + yy, (z + d) * 2 + yy

            @pl.when(z - d >= 0)
            def _():
                hop(q, low, target(q, low), "up").wait_recv()

                @pl.when(z < line - 1)
                def _():
                    hop(q, low, target(q, low), "up").start()

            @pl.when(z + d < line)
            def _():
                hop(q, high, target(q, high), "down").wait_recv()

                @pl.when(z > 0)
                def _():
                    hop(q, high, target(q, high), "down").start()

    def from_side(q):
        other = z * 2 + 1 - y
        hop(q, other, target(q, other), "side").wait_recv()

        @pl.when(z < line - 1)
        def _():
            hop(q, other, target(q, other), "up").start()

        @pl.when(z > 0)
        def _():
            hop(q, other, target(q, other), "down").start()

    def pass_on(q, d):
        if q in across_first:
            if d == 1:
                from_side(q)
            line_only(q, d)
            return
        low = (z - d) * 2 + y
        high = (z + d) * 2 + y

        @pl.when(z - d >= 0)
        def _():
            hop(q, low, target(q, low), "side").wait_recv()
            hop(q, low, target(q, low), "side").start()

            @pl.when(z < line - 1)
            def _():
                hop(q, low, target(q, low), "up").start()

        @pl.when(z + d < line)
        def _():
            hop(q, high, target(q, high), "side").wait_recv()
            hop(q, high, target(q, high), "side").start()

            @pl.when(z > 0)
            def _():
                hop(q, high, target(q, high), "down").start()

    def wait_side(q):
        for zs in range(line):
            piece = zs * 2 + 1 - y
            if q not in across_first:
                hop(q, piece, target(q, piece), "side").wait_recv()
        own_copy(q).wait()

    def exchange(a, src, dst, k):
        peer = lax.rem(s + k, seq)
        return remote(src, dst, r.seq_send.at[a, k], r.seq_recv.at[a, k], me, peer)

    def came_from(k):
        return lax.rem(s + seq - k, seq)

    core = lax.rem(s, 2)
    mate, cross = s + 1 - 2 * core, lax.rem(s + 2, seq)

    def spread(n, own, part, owner, to, k):
        src = part(owner) if own is None else own
        return remote(src, part(owner), r.ag_send.at[n, k], r.ag_recv.at[n, k], me, to)

    def spread_start(n, own, part):
        spread(n, own, part, s, cross, 0).start()
        spread(n, own, part, s, mate, 1).start()

    def spread_on(n, own, part):
        spread(n, None, part, cross, cross, 0).wait_recv()
        spread(n, None, part, cross, mate, 2).start()

    def spread_end(n, own, part):
        spread(n, None, part, mate, mate, 1).wait_recv()
        spread(n, None, part, lax.rem(mate + 2, seq), mate, 2).wait_recv()

    def spread_sent(n, own, part):
        spread(n, own, part, s, cross, 0).wait_send()
        spread(n, own, part, s, mate, 1).wait_send()
        spread(n, None, part, cross, mate, 2).wait_send()

    def item(name):
        return [q for q in range(len(items)) if items[q][0] == name]

    def rows_of(t):
        return pl.ds(pl.multiple_of(t * slot, slot), slot)

    across_first = item("fc2")[-ACROSS:] if ACROSS else []

    xs = (0, r.x, lambda t: r.xs.at[rows_of(t)])
    cots = (1, r.cot, lambda t: r.cots.at[t])
    vecs = (2, None, lambda t: r.vecs.at[t])
    wos = (3, None, lambda t: r.wo.at[t])
    mixes = (4, r.mixed_mine, lambda t: r.others.at[t])
    own(item("vec")[0])
    own(item("ov")[0])
    early = item("fc2")[:1]
    for q in early:
        own(q)
    x_copy = pltpu.make_async_copy(r.x, r.xs.at[rows_of(s)], r.loc_sem.at[len(items)])
    cot_copy = pltpu.make_async_copy(r.cot, r.cots.at[s], r.loc_sem.at[len(items) + 1])
    r.cq[...] = jnp.zeros_like(r.cq)
    for t in range(seq):
        for j in range(3):
            at = j * width + t * cols
            r.cq[t, :sub, j * cols : (j + 1) * cols] = r.qkv[:, at : at + cols]
    for k in range(1, seq):
        exchange(0, r.cq.at[lax.rem(s + k, seq)], r.rq.at[s], k).start()
    x_copy.start()
    spread_start(*xs)
    r.cf[...] = jnp.zeros_like(r.cf)
    for g in range(plan.devices):
        i, t = g // seq, g % seq
        a, b = plan.first[g], plan.last[g]
        r.cf[t, :sub, i * plan.block : i * plan.block + b - a] = r.fc1[:, a:b]
    for k in range(1, seq):
        exchange(1, r.cf.at[lax.rem(s + k, seq)], r.rf.at[s], k).start()
    wq, late = item("wq"), [q for q in item("fc2") if q not in early]

    def merge(a, sent, got, merged):
        for k in range(1, seq):
            exchange(a, sent.at[lax.rem(s + k, seq)], got.at[came_from(k)], k).wait()
        got[s] = sent[s]
        for t in range(seq):
            merged[t * sub : (t + 1) * sub, :] = got[t, :sub, :]

    def all_on(queue, d):
        for q in queue:
            pass_on(q, d)

    all_on(item("vec"), 1)
    merge(0, r.cq, r.rq, r.mq)
    own(wq[0])
    all_on(item("ov"), 1)
    all_on(item("vec"), 2)
    spread_on(*xs)
    for q in late:
        own(q)
    merge(1, r.cf, r.rf, r.mf)
    all_on(wq, 1)
    for d in range(3, line):
        all_on(item("vec"), d)
    for d in range(2, line):
        all_on(item("ov"), d)
    wait_side(item("vec")[0])
    spread_start(*vecs)
    for q in item("wf1"):
        own(q)
    for d in range(2, line):
        all_on(wq, d)
    all_on(early, 1)
    spread_on(*vecs)
    wait_side(item("ov")[0])
    spread_start(*wos)
    cot_copy.start()
    spread_start(*cots)
    all_on(late, 1)
    for d in range(2, line):
        all_on(early, d)

    rest = [(q, 1) for q in item("wf1")]
    rest += [(q, d) for d in range(2, line) for q in late + item("wf1")]

    def service(n=1):
        for _ in range(n):
            if rest:
                pass_on(*rest.pop(0))

    x_copy.wait()
    spread_end(*xs)
    spread_end(*vecs)
    count = plan.shard_vec
    for g in range(plan.devices):
        i, t = g // seq, g % seq
        r.vec[:, g * count : (g + 1) * count] = r.vecs[t, i, :1, :count].astype(F32)
    bias1, v_bias, gain1, q_bias, out_bias, gain2, bias2, fc2_bias = (
        r.vec[:, n * width : (n + 1) * width] for n in range(8)
    )
    r.gain1[...] = gain1
    r.gain2[...] = gain2
    r.fc1_bias[...] = jnp.zeros_like(r.fc1_bias)
    for t in range(seq):

        @pl.when(s == t)
        def _():
            for i in range(plan.img):
                a, b = plan.first[i * seq + t], plan.last[i * seq + t]
                to = i * plan.block
                r.fc1_bias[:, to : to + b - a] = r.vec[:, 8 * width + a : 8 * width + b]

    for t in range(seq):
        rows = slice(t * slot, (t + 1) * slot)
        normed, rstd = normalize(r.xs[rows, :].astype(F32))
        r.ln1[rows, :] = (normed * gain1 + bias1).astype(BF16)

        @pl.when(s == t)
        def _():
            r.normed1[...] = normed
            r.rstd1[...] = rstd

        service(PACE[0][t])

    for q in item("wq"):
        wait_side(q)
    for t in range(seq):
        rows = slice(t * slot, (t + 1) * slot)
        r.qkv_all[rows, :] = jnp.dot(
            r.ln1[rows, :], r.mat_qkv[...], preferred_element_type=F32
        )
        service(PACE[1][t])
    for t in range(seq):

        @pl.when(s == t)
        def _():
            lanes = slice(t * cols, (t + 1) * cols)
            r.qkv_all[:, :cols] += q_bias[:, lanes]
            r.qkv_all[:, 2 * cols : 3 * cols] += v_bias[:, lanes]

    for h in range(heads):
        for j, out in enumerate((r.queries, r.keys, r.values)):
            at = j * cols + h * HEAD_DIM
            out[h] = r.qkv_all[:, at : at + HEAD_DIM].astype(BF16)
    tile = 2 * slot
    for h in range(heads):
        lanes = slice(h * HEAD_DIM, (h + 1) * HEAD_DIM)
        key, value = r.keys[h], r.values[h]
        for at in range(0, seq * slot, tile):
            rows = slice(at, at + tile)
            scores = dot_t(r.queries[h, rows, :], key) * scale
            scores = jnp.where(r.key_ok[...] > 0, scores, -1e30)
            top = jnp.max(scores, axis=-1, keepdims=True)
            terms = jnp.exp(scores - top)
            total = jnp.sum(terms, axis=-1, keepdims=True)
            r.lse[h, rows, :] = top + jnp.log(total)
            probs = (terms * (1.0 / total)).astype(BF16)
            r.mixed_mine[rows, lanes] = jnp.dot(
                probs, value, preferred_element_type=F32
            ).astype(BF16)
        service(PACE[2][h])
        if h == 0:
            spread_on(*wos)
        if h == heads - 1:
            spread_on(*cots)

    spread_start(*mixes)
    r.others[s] = r.mixed_mine[...]
    spread_end(*wos)
    for g in range(plan.devices):
        i, t = g // seq, g % seq
        r.mat_out[g * sub : (g + 1) * sub, :] = r.wo[t, i, :sub, :]
    for t in range(seq):

        @pl.when(s == t)
        def _():
            r.out_mine[...] = r.mat_out[t * cols : (t + 1) * cols, :]

    service(PACE[3][0])
    spread_on(*mixes)
    service(PACE[3][1])
    spread_end(*mixes)
    for t in range(seq):
        r.mixed[:, t * cols : (t + 1) * cols] = r.others[t]
    for t in range(seq):
        rows = slice(t * slot, (t + 1) * slot)
        resid = (
            r.xs[rows, :].astype(F32)
            + jnp.dot(r.mixed[rows, :], r.mat_out[...], preferred_element_type=F32)
            + out_bias
        )
        normed, rstd = normalize(resid)
        r.ln2[rows, :] = (normed * gain2 + bias2).astype(BF16)

        @pl.when(s == t)
        def _():
            r.base[...] = resid + fc2_bias
            r.normed2[...] = normed
            r.rstd2[...] = rstd

        service(PACE[4][t])
    service(len(rest))
    for q in item("fc2") + item("wf1"):
        wait_side(q)

    def wait_sends(q, piece, zs):
        @pl.when(jnp.logical_and(z < line - 1, zs <= z))
        def _():
            hop(q, piece, target(q, piece), "up").wait_send()

        @pl.when(jnp.logical_and(z > 0, zs >= z))
        def _():
            hop(q, piece, target(q, piece), "down").wait_send()

    for q in range(len(items)):
        if q in across_first:
            hop(q, me, target(q, me), "side").wait_send()
        for zs in range(line):
            wait_sends(q, zs * 2 + y, zs)
            if q in across_first:
                wait_sends(q, zs * 2 + 1 - y, zs)
            else:
                hop(q, zs * 2 + y, target(q, zs * 2 + y), "side").wait_send()

    cot_copy.wait()
    spread_end(*cots)
    for each in (xs, cots, vecs, wos, mixes):
        spread_sent(*each)


def forward(plan, slot, heads, args):
    any_spec = pl.BlockSpec(memory_space=pl.ANY)
    vmem = pl.BlockSpec(memory_space=pltpu.VMEM)
    img, seq, width, cols = plan.img, plan.seq, plan.width, plan.cols
    tokens = seq * slot
    dma = pltpu.SemaphoreType.DMA
    shape = jax.ShapeDtypeStruct
    items = [("vec", 0, 16), ("ov", 0, plan.sub_pad)]
    step = 48
    for name, rows, by in (
        ("fc2", plan.block, step),
        ("wq", plan.rows_pad, plan.rows_pad),
        ("wf1", plan.rows_pad, step),
    ):
        items += [(name, a, min(by, rows - a)) for a in range(0, rows, by)]
    n = len(items)
    head = shape((heads, tokens, HEAD_DIM), BF16)
    all16 = shape((tokens, width), BF16)
    own32 = shape((slot, width), F32)
    column = shape((slot, 1), F32)
    row = shape((1, width), F32)
    outs = (
        shape((img, plan.rows_pad, plan.units), BF16),
        shape((img, plan.block, width), BF16),
        shape((seq, slot, width), BF16),
        shape((img * plan.rows_pad, plan.qkv_cols), BF16),
        head,
        head,
        head,
        shape((heads, tokens, 1), F32),
        shape((tokens, cols), BF16),
        all16,
        all16,
        all16,
        own32,
        own32,
        column,
        own32,
        column,
        shape((cols, width), BF16),
        row,
        row,
        shape((1, plan.units), F32),
    )
    result = pl.pallas_call(
        functools.partial(forward_kernel, plan, items, heads),
        out_shape=outs,
        in_specs=[vmem, vmem, any_spec, any_spec, vmem, vmem, any_spec, vmem],
        out_specs=(any_spec,) * 3 + (vmem,) * (len(outs) - 3),
        scratch_shapes=[
            pltpu.VMEM((seq, plan.sub_pad, plan.qkv_cols), BF16),
            pltpu.VMEM((seq, plan.sub_pad, plan.units), BF16),
            pltpu.VMEM((seq, plan.sub_pad, plan.qkv_cols), BF16),
            pltpu.VMEM((seq, plan.sub_pad, plan.units), BF16),
            pltpu.VMEM((plan.rows_pad, plan.qkv_cols), BF16),
            pltpu.VMEM((plan.rows_pad, plan.units), BF16),
            pltpu.VMEM((seq, img, plan.sub_pad, width), BF16),
            pltpu.VMEM((seq, img, *args["vec_in"].shape), BF16),
            pltpu.VMEM((width, width), BF16),
            pltpu.VMEM((tokens, width), BF16),
            pltpu.VMEM((1, plan.shard_vec * plan.devices), F32),
            pltpu.VMEM((tokens, plan.qkv_cols), F32),
            pltpu.VMEM((seq, tokens, cols), BF16),
            dma((n + 2,)),
            *[dma((n, img))] * 4,
            *[dma((2, seq))] * 2,
            *[dma((5, 3))] * 2,
        ],
        compiler_params=pltpu.CompilerParams(
            collective_id=0, has_side_effects=True, vmem_limit_bytes=VMEM_LIMIT
        ),
        name="forward",
    )(*[args[name] for name in ForwardIn._fields])
    return Refs(ForwardOut._fields, result)


def dot_00(left, right):
    return lax.dot_general(left, right, (((0,), (0,)), ((), ())), preferred_element_type=F32)


def dot_t(left, right):
    return lax.dot_general(left, right, (((1,), (1,)), ((), ())), preferred_element_type=F32)


def norm_back(grad_in, normed, rstd, gain):
    scaled = grad_in * gain
    return rstd * (
        scaled
        - jnp.mean(scaled, axis=-1, keepdims=True)
        - normed * jnp.mean(scaled * normed, axis=-1, keepdims=True)
    )


class BackwardIn(NamedTuple):
    g2: jax.Array
    g1: jax.Array
    ln2_part: jax.Array
    out_part: jax.Array
    normed2: jax.Array
    rstd2: jax.Array
    gain2: jax.Array
    grad_y: jax.Array
    base: jax.Array
    rowmask: jax.Array
    queries: jax.Array
    keys: jax.Array
    values: jax.Array
    lse: jax.Array
    key_ok: jax.Array
    mixed_mine: jax.Array
    mixed: jax.Array
    ln1: jax.Array
    mat_qkv: jax.Array
    out_mine: jax.Array
    normed1: jax.Array
    rstd1: jax.Array
    gain1: jax.Array
    pre_sums: jax.Array


class BackwardOut(NamedTuple):
    output: jax.Array
    input_grad: jax.Array
    o2: jax.Array
    o1: jax.Array
    oq: jax.Array
    oo: jax.Array
    ov: jax.Array


class BackwardScratch(NamedTuple):
    side2: jax.Array
    side1: jax.Array
    sidem: jax.Array
    sidev: jax.Array
    low2: jax.Array
    low1: jax.Array
    lowm: jax.Array
    lowv: jax.Array
    high2: jax.Array
    high1: jax.Array
    highm: jax.Array
    highv: jax.Array
    acc2: jax.Array
    acc1: jax.Array
    accm: jax.Array
    accv: jax.Array
    fin1: jax.Array
    finm: jax.Array
    cut1: jax.Array
    cutm: jax.Array
    cutv: jax.Array
    got1: jax.Array
    gotm: jax.Array
    gmix: jax.Array
    gvec: jax.Array
    gvec32: jax.Array
    front: jax.Array
    rest: jax.Array
    qsum: jax.Array
    vsum: jax.Array
    pair_ln2: jax.Array
    cross_ln2: jax.Array
    sum_ln2: jax.Array
    pair_out: jax.Array
    cross_out: jax.Array
    sum_out: jax.Array
    pair_ln1: jax.Array
    cross_ln1: jax.Array
    sum_ln1: jax.Array
    own_resid: jax.Array
    all_resid: jax.Array
    resid32: jax.Array
    gm: jax.Array
    gqkv: jax.Array
    part_ln1: jax.Array
    cols_resid: jax.Array
    side_send: jax.Array
    side_recv: jax.Array
    low_send: jax.Array
    low_recv: jax.Array
    high_send: jax.Array
    high_recv: jax.Array
    seq_send: jax.Array
    seq_recv: jax.Array
    rs_send: jax.Array
    rs_recv: jax.Array
    ag_send: jax.Array
    ag_recv: jax.Array


BACKWARD = BackwardIn._fields + BackwardOut._fields + BackwardScratch._fields


def backward_kernel(plan, parts, heads, *refs):
    r = Refs(BACKWARD, refs)
    z, y, s = coords(plan)
    me = z * 2 + y
    line, seq, sub, cols = plan.line, plan.seq, plan.sub, plan.cols
    width = plan.width
    slot = r.output.shape[0]
    scale = HEAD_DIM ** (-0.5)
    entry_barrier(plan, z, y, s)
    grads = [r.g2, r.g1, r.gmix, r.gvec]
    tall = [plan.block, plan.rows_pad, plan.rows_pad, 16]
    sides = [r.side2, r.side1, r.sidem, r.sidev]
    lows = [r.low2, r.low1, r.lowm, r.lowv]
    highs = [r.high2, r.high1, r.highm, r.highv]
    accs = [r.acc2, r.acc1, r.accm, r.accv]

    def at(c):
        q, a, n = parts[c]
        return q, pl.ds(a, n)

    def piece(c, img):
        q, a, n = parts[c]
        return grads[q].at[pl.ds(pl.multiple_of(img * tall[q] + a, 16), n)]

    def to_side(c, dest):
        q, w = at(c)
        return remote(
            piece(c, dest * 2 + 1 - y),
            sides[q].at[dest, w],
            r.side_send.at[c, dest],
            r.side_recv.at[c, dest],
            z * 2 + 1 - y,
            s,
        )

    def to_up(c, dest):
        q, w = at(c)
        return remote(
            accs[q].at[dest, w],
            lows[q].at[dest, w],
            r.low_send.at[c, dest],
            r.low_recv.at[c, dest],
            me + 2,
            s,
        )

    def to_down(c, dest):
        q, w = at(c)
        return remote(
            accs[q].at[dest, w],
            highs[q].at[dest, w],
            r.high_send.at[c, dest],
            r.high_recv.at[c, dest],
            me - 2,
            s,
        )

    def send_side(c):
        for d in range(line - 1, -1, -1):

            @pl.when(z + d < line)
            def _():
                to_side(c, z + d).start()

            if d:

                @pl.when(z - d >= 0)
                def _():
                    to_side(c, z - d).start()

    def both(c, dest):
        q, w = at(c)
        to_side(c, dest).wait_recv()
        return piece(c, dest * 2 + y)[...].astype(F32) + sides[q][dest, w, :].astype(F32)

    def pass_on(c):
        q, w = at(c)
        for d in range(line - 1, 0, -1):

            @pl.when(z + d < line)
            def _():
                dest = z + d
                total = both(c, dest)

                @pl.when(z > 0)
                def _():
                    to_up(c, dest).wait_recv()
                    accs[q][dest, w, :] = (total + lows[q][dest, w, :].astype(F32)).astype(BF16)

                @pl.when(z == 0)
                def _():
                    accs[q][dest, w, :] = total.astype(BF16)

                to_up(c, dest).start()

            @pl.when(z - d >= 0)
            def _():
                dest = z - d
                total = both(c, dest)

                @pl.when(z < line - 1)
                def _():
                    to_down(c, dest).wait_recv()
                    accs[q][dest, w, :] = (total + highs[q][dest, w, :].astype(F32)).astype(BF16)

                @pl.when(z == line - 1)
                def _():
                    accs[q][dest, w, :] = total.astype(BF16)

                to_down(c, dest).start()

    outs = [r.o2, r.fin1, r.finm, None]

    def finish(c):
        q, w = at(c)
        total = both(c, z)

        def store(value):
            if q == 3:
                r.cutv[s, w, :] = value.astype(BF16)
            else:
                outs[q][w, :] = value

        @pl.when(z == 0)
        def _():
            to_down(c, z).wait_recv()
            store(total + highs[q][z, w, :].astype(F32))

        @pl.when(z == line - 1)
        def _():
            to_up(c, z).wait_recv()
            store(total + lows[q][z, w, :].astype(F32))

        @pl.when(jnp.logical_and(z > 0, z < line - 1))
        def _():
            to_down(c, z).wait_recv()
            to_up(c, z).wait_recv()
            store(total + lows[q][z, w, :].astype(F32) + highs[q][z, w, :].astype(F32))

    def exchange(a, src, dst, k):
        peer = lax.rem(s + k, seq)
        return remote(src, dst, r.seq_send.at[a, k], r.seq_recv.at[a, k], me, peer)

    def came_from(k):
        return lax.rem(s + seq - k, seq)

    ends = {max(c for c in range(len(parts)) if parts[c][0] == q): q for q in (1, 2, 3)}

    def after(c):
        if c not in ends:
            return
        q = ends[c]
        if q == 3:
            for k in range(1, seq):
                exchange(2, r.cutv.at[s], r.ov.at[s], k).start()
            return
        fin, cut, got = ((r.fin1, r.cut1, r.got1), (r.finm, r.cutm, r.gotm))[q - 1]
        for t in range(seq):
            cut[t, :sub, :] = fin[t * sub : (t + 1) * sub, :].astype(BF16)
        for k in range(1, seq):
            exchange(q - 1, cut.at[lax.rem(s + k, seq)], got.at[s], k).start()

    def service(c):
        if c < len(parts):
            pass_on(c)
        if c >= 1:
            finish(c - 1)
            after(c - 1)

    core, far = lax.rem(s, 2), s // 2
    mate, cross = s + 1 - 2 * core, lax.rem(s + 2, seq)

    def rows_of(t):
        return pl.ds(pl.multiple_of(t * slot, slot), slot)

    def to_mate(n, part, pair, h):
        return remote(
            part.at[rows_of(h * 2 + 1 - core)],
            pair.at[h],
            r.rs_send.at[n, h],
            r.rs_recv.at[n, h],
            me,
            mate,
        )

    def to_cross(n, summed, got):
        return remote(summed, got, r.rs_send.at[n, 2], r.rs_recv.at[n, 2], me, cross)

    def sum_start(n, part, pair):
        to_mate(n, part, pair, 1 - far).start()
        to_mate(n, part, pair, far).start()

    def sum_across(n, part, pair, summed, got):
        to_mate(n, part, pair, 1 - far).wait_recv()
        summed[...] = (
            part[rows_of(cross), :].astype(F32) + pair[1 - far].astype(F32)
        ).astype(BF16)
        to_cross(n, summed, got).start()

    def sum_end(n, part, pair, summed, got):
        to_mate(n, part, pair, far).wait_recv()
        to_cross(n, summed, got).wait_recv()
        to_mate(n, part, pair, far).wait_send()
        to_mate(n, part, pair, 1 - far).wait_send()
        to_cross(n, summed, got).wait_send()
        return part[rows_of(s), :].astype(F32) + pair[far].astype(F32) + got[...].astype(F32)

    ln2_args = (0, r.ln2_part, r.pair_ln2)
    out_args = (1, r.out_part, r.pair_out)
    ln1_args = (2, r.part_ln1, r.pair_ln1)

    sum_start(*ln2_args)
    first_mix = min(c for c in range(len(parts)) if parts[c][0] == 2)
    for c in range(first_mix):
        send_side(c)
    r.rest[...] = jnp.zeros_like(r.rest)
    r.rest[:, 5 * width : 6 * width] = jnp.sum(r.grad_y[...], axis=0, keepdims=True)
    for t in range(seq):

        @pl.when(s == t)
        def _():
            for i in range(plan.img):
                a, b = plan.first[i * seq + t], plan.last[i * seq + t]
                at = i * plan.block
                r.rest[:, 6 * width + a : 6 * width + b] += r.pre_sums[:, at : at + b - a]

    r.gqkv[...] = jnp.zeros_like(r.gqkv)
    r.gvec32[...] = jnp.zeros_like(r.gvec32)
    sum_across(*ln2_args, r.sum_ln2, r.cross_ln2)
    sum_start(*out_args)
    grad_ln2 = sum_end(*ln2_args, r.sum_ln2, r.cross_ln2)
    grad_resid = r.grad_y[...] + norm_back(grad_ln2, r.normed2[...], r.rstd2[...], r.gain2[...])
    r.own_resid[...] = grad_resid.astype(BF16)
    r.resid32[...] = grad_resid

    def gather_resid(part, to, n):
        rows = r.all_resid.at[rows_of(part)]
        src = r.own_resid if n < 2 else rows
        return remote(src, rows, r.ag_send.at[n], r.ag_recv.at[n], me, to)

    gather_resid(s, cross, 0).start()
    gather_resid(s, mate, 1).start()
    r.all_resid[rows_of(s), :] = r.own_resid[...]
    r.rest[:, 2 * width : 3 * width] = jnp.sum(grad_resid, axis=0, keepdims=True)
    r.rest[:, 3 * width : 4 * width] = jnp.sum(grad_ln2 * r.normed2[...], axis=0, keepdims=True)
    r.rest[:, 4 * width : 5 * width] = jnp.sum(grad_ln2, axis=0, keepdims=True)
    service(0)
    gather_resid(cross, cross, 0).wait_recv()
    gather_resid(cross, mate, 2).start()
    sum_across(*out_args, r.sum_out, r.cross_out)
    gather_resid(mate, mate, 1).wait_recv()
    gather_resid(lax.rem(mate + 2, seq), mate, 2).wait_recv()

    for t in range(seq):
        rows = slice(t * slot, (t + 1) * slot)
        r.gm[rows, :] = dot_t(r.all_resid[rows, :], r.out_mine[...]).astype(BF16)

        @pl.when(s == t)
        def _():
            r.cols_resid[...] = r.all_resid[:, t * cols : (t + 1) * cols]

    tile = 2 * slot
    for h in range(heads):
        lanes = slice(h * HEAD_DIM, (h + 1) * HEAD_DIM)
        key, value = r.keys[h], r.values[h]
        grad_value = jnp.zeros((seq * slot, HEAD_DIM), F32)
        grad_key = jnp.zeros((seq * slot, HEAD_DIM), F32)
        query_sum = jnp.zeros((1, HEAD_DIM), F32)
        for at_row in range(0, seq * slot, tile):
            rows = slice(at_row, at_row + tile)
            query, gm = r.queries[h, rows, :], r.gm[rows, lanes]
            scores = dot_t(query, key) * scale
            scores = jnp.where(r.key_ok[...] > 0, scores, -1e30)
            probs = jnp.exp(scores - r.lse[h, rows, :])
            grad_value += dot_00(probs.astype(BF16), gm)
            delta = jnp.sum(
                gm.astype(F32) * r.mixed_mine[rows, lanes].astype(F32), axis=-1, keepdims=True
            )
            grad_scores = (probs * (dot_t(gm, value) - delta) * scale).astype(BF16)
            grad_query = jnp.dot(grad_scores, key, preferred_element_type=F32)
            grad_key += dot_00(grad_scores, query)
            r.gqkv[rows, lanes] = grad_query.astype(BF16)
            query_sum += jnp.sum(grad_query, axis=0, keepdims=True)
        r.qsum[:, lanes] = query_sum
        r.vsum[:, lanes] = jnp.sum(grad_value, axis=0, keepdims=True)
        for j, grad in ((1, grad_key), (2, grad_value)):
            to = j * cols + h * HEAD_DIM
            r.gqkv[:, to : to + HEAD_DIM] = grad.astype(BF16)
        if h % 2 == 1:
            service(1 + h // 2)

    for t in range(seq):
        rows = slice(t * slot, (t + 1) * slot)
        r.part_ln1[rows, :] = dot_t(r.gqkv[rows, :], r.mat_qkv[...]).astype(BF16)
    sum_start(*ln1_args)
    for m in range(0, width, LANES):
        grad = jnp.concatenate(
            [
                dot_00(r.ln1[:, m : m + LANES], r.gqkv[...])[:, : 3 * cols],
                dot_00(r.mixed[:, m : m + LANES], r.cols_resid[...]),
            ],
            axis=1,
        )
        r.gmix[m : m + LANES, :] = grad.astype(BF16)
    for c in range(first_mix, len(parts) - 1):
        send_side(c)
    sum_across(*ln1_args, r.sum_ln1, r.cross_ln1)
    out_terms = sum_end(*out_args, r.sum_out, r.cross_out)
    r.output[...] = ((r.base[...] + out_terms) * r.rowmask[...]).astype(BF16)
    service(3)
    grad_ln1 = sum_end(*ln1_args, r.sum_ln1, r.cross_ln1)
    normed1 = r.normed1[...]
    r.input_grad[...] = r.resid32[...] + norm_back(grad_ln1, normed1, r.rstd1[...], r.gain1[...])

    r.front[...] = jnp.zeros_like(r.front)
    r.front[:, :width] = jnp.sum(grad_ln1, axis=0, keepdims=True)
    r.rest[:, :width] = jnp.sum(grad_ln1 * normed1, axis=0, keepdims=True)
    for t in range(seq):

        @pl.when(s == t)
        def _():
            lanes = slice(width + t * cols, width + (t + 1) * cols)
            r.front[:, lanes] = r.vsum[...]
            r.rest[:, lanes] = r.qsum[...]

    own_front = 2 * width // plan.devices
    own_rest = plan.shard_vec - own_front
    for g in range(plan.devices):
        row = g // seq * 16 + g % seq
        r.gvec32[row : row + 1, :own_front] = r.front[:, g * own_front : (g + 1) * own_front]
        r.gvec32[row : row + 1, own_front : own_front + own_rest] = r.rest[
            :, g * own_rest : (g + 1) * own_rest
        ]
    r.gvec[...] = r.gvec32[...].astype(BF16)
    send_side(len(parts) - 1)

    for c in range(4, first_mix + 1):
        service(c)
    service(first_mix + 1)
    r.got1[s] = r.cut1[s]
    for k in range(1, seq):
        exchange(0, r.cut1.at[lax.rem(s + k, seq)], r.got1.at[came_from(k)], k).wait()
    r.o1[...] = jnp.zeros_like(r.o1)
    for g in range(plan.devices):
        i, t = g // seq, g % seq
        a, b = plan.first[g], plan.last[g]
        r.o1[:, a:b] += r.got1[t, :sub, i * plan.block : i * plan.block + b - a].astype(F32)
    for c in range(first_mix + 2, len(parts) + 1):
        service(c)
    r.gotm[s] = r.cutm[s]
    r.ov[s] = r.cutv[s]
    for k in range(1, seq):
        exchange(1, r.cutm.at[lax.rem(s + k, seq)], r.gotm.at[came_from(k)], k).wait()
    for t in range(seq):
        for j in range(3):
            to = j * width + t * cols
            r.oq[:, to : to + cols] = r.gotm[t, :sub, j * cols : (j + 1) * cols].astype(F32)
        r.oo[:, t * cols : (t + 1) * cols] = r.gotm[t, :sub, 3 * cols : 4 * cols].astype(F32)
    for k in range(1, seq):
        exchange(2, r.cutv.at[s], r.ov.at[came_from(k)], k).wait()

    gather_resid(s, cross, 0).wait_send()
    gather_resid(s, mate, 1).wait_send()
    gather_resid(cross, mate, 2).wait_send()
    for c in range(len(parts)):
        for dest in range(line):
            to_side(c, dest).wait_send()

            @pl.when(dest > z)
            def _():
                to_up(c, dest).wait_send()

            @pl.when(dest < z)
            def _():
                to_down(c, dest).wait_send()


def backward(plan, slot, heads, args):
    vmem = pl.BlockSpec(memory_space=pltpu.VMEM)
    img, seq, width, line, cols = plan.img, plan.seq, plan.width, plan.line, plan.cols
    dma = pltpu.SemaphoreType.DMA
    shape = jax.ShapeDtypeStruct
    vec_pad = round_up(plan.shard_vec, LANES)
    parts = []
    step = 48
    for q, rows in ((0, plan.block), (1, plan.rows_pad), (2, plan.rows_pad)):
        parts += [(q, a, min(step, rows - a)) for a in range(0, rows, step)]
    parts.append((3, 0, 16))
    n = len(parts)
    mix = 4 * cols
    inner = [
        (plan.block, width),
        (plan.rows_pad, plan.units),
        (plan.rows_pad, mix),
        (16, vec_pad),
    ]
    buffers = [pltpu.VMEM((line, *dims), BF16) for _ in range(4) for dims in inner]
    own16 = pltpu.VMEM((slot, width), BF16)
    all16 = pltpu.VMEM((seq * slot, width), BF16)
    sums = [pltpu.VMEM((2, slot, width), BF16), own16, own16]
    scratch = buffers + [
        pltpu.VMEM(inner[1], F32),
        pltpu.VMEM(inner[2], F32),
        pltpu.VMEM((seq, plan.sub_pad, plan.units), BF16),
        pltpu.VMEM((seq, plan.sub_pad, mix), BF16),
        pltpu.VMEM((seq, 16, vec_pad), BF16),
        pltpu.VMEM((seq, plan.sub_pad, plan.units), BF16),
        pltpu.VMEM((seq, plan.sub_pad, mix), BF16),
        pltpu.VMEM((img * plan.rows_pad, mix), BF16),
        pltpu.VMEM((img * 16, vec_pad), BF16),
        pltpu.VMEM((img * 16, vec_pad), F32),
        pltpu.VMEM((1, 2 * width), F32),
        pltpu.VMEM((1, plan.shard_vec * plan.devices - 2 * width), F32),
        pltpu.VMEM((1, cols), F32),
        pltpu.VMEM((1, cols), F32),
        *sums,
        *sums,
        *sums,
        own16,
        all16,
        pltpu.VMEM((slot, width), F32),
        pltpu.VMEM((seq * slot, cols), BF16),
        pltpu.VMEM((seq * slot, plan.qkv_cols), BF16),
        all16,
        pltpu.VMEM((seq * slot, cols), BF16),
        *[dma((n, line))] * 6,
        *[dma((3, seq))] * 2,
        *[dma((3, 3))] * 2,
        *[dma((3,))] * 2,
    ]
    return pl.pallas_call(
        functools.partial(backward_kernel, plan, parts, heads),
        out_shape=(
            shape((slot, width), BF16),
            shape((slot, width), F32),
            shape((plan.block, width), F32),
            shape((plan.sub, plan.hidden), F32),
            shape((plan.sub, 3 * width), F32),
            shape((plan.sub, width), F32),
            shape((seq, 16, vec_pad), BF16),
        ),
        in_specs=[vmem] * len(BackwardIn._fields),
        out_specs=(vmem,) * len(BackwardOut._fields),
        scratch_shapes=scratch,
        compiler_params=pltpu.CompilerParams(
            collective_id=1, has_side_effects=True, vmem_limit_bytes=VMEM_LIMIT
        ),
        name="backward",
    )(*[args[name] for name in BackwardIn._fields])


def normalize(values):
    mean = jnp.mean(values, axis=-1, keepdims=True)
    centred = values - mean
    rstd = lax.rsqrt(jnp.mean(centred * centred, axis=-1, keepdims=True) + EPS)
    return (centred * rstd, rstd)


def gelu_parts(pre):
    inner = GELU_C * (pre + 0.044715 * pre * pre * pre)
    tanh_v = jnp.tanh(inner)
    value = 0.5 * pre * (1.0 + tanh_v)
    slope = 0.5 * (1.0 + tanh_v) + 0.5 * pre * (1.0 - tanh_v * tanh_v) * GELU_C * (
        1.0 + 3.0 * 0.044715 * pre * pre
    )
    return (value, slope)


def gather(value, axes):
    return lax.all_gather(value, axes, axis=0, tiled=True)


def scatter_sum(value, axes):
    return lax.psum_scatter(value, axes, scatter_dimension=0, tiled=True)


def weight_grad(left, right):
    return lax.dot_general(
        left, right, (((0,), (0,)), ((), ())), preferred_element_type=F32
    ).astype(BF16)


def batched(left, right, over_left, over_right):
    return lax.dot_general(
        left,
        right,
        (((over_left,), (over_right,)), ((0,), (0,))),
        preferred_element_type=F32,
    )


TILE = 2048


def pack(flat):
    padded = round_up(flat.shape[0], TILE)
    return jnp.pad(flat, (0, padded - flat.shape[0])).reshape(-1, LANES)


def unpack_blocks(packed, blocks, length):
    return packed.reshape(blocks, -1)[:, :length].reshape(-1)


def pack_blocks(flat, blocks):
    block = flat.reshape(blocks, -1)
    padded = round_up(block.shape[1], TILE)
    return jnp.pad(block, ((0, 0), (0, padded - block.shape[1]))).reshape(-1, LANES)


def shards_by_rows(tokens, counts, w_qkv, w_out, w_fc1, w_fc2, vectors, cotangent):
    f32 = jnp.float32
    bf16 = jnp.bfloat16
    width = tokens.shape[2]
    slot = tokens.shape[1]
    scale = HEAD_DIM ** (-0.5)
    position = lax.axis_index("seq")
    seq_count = lax.axis_size("seq")
    img_count = lax.axis_size("img")
    device_count = img_count * seq_count
    both = ("img", "seq")
    shard_qkv, shard_out, shard_fc1, shard_fc2, shard_vec = (
        w.shape[0] for w in (w_qkv, w_out, w_fc1, w_fc2, vectors)
    )
    hidden = shard_fc1 * device_count // width
    heads = HEADS // seq_count
    cols = width // seq_count
    units = hidden // seq_count
    rows = width // img_count
    pad_cols = round_up(3 * cols, LANES) - 3 * cols
    pad_units = round_up(units, LANES) - units
    to_quarter = [(c, (c % img_count) * seq_count + c // img_count) for c in range(device_count)]
    to_owner = [(b, a) for a, b in to_quarter]

    slice_counts = counts[0]
    key_valid = (jnp.arange(slot)[None, :] < slice_counts[:, None]).reshape(-1)
    row_valid = lax.dynamic_slice_in_dim(key_valid, position * slot, slot)
    rowmask = row_valid.astype(f32)[:, None]

    def mine(values):
        return lax.dynamic_slice_in_dim(values, position * slot, slot)

    shard_ov = shard_out + shard_vec
    local = gather(pack(jnp.concatenate([w_qkv, w_fc1, w_out, vectors])), "seq")
    local = local.reshape(seq_count, -1)
    x_all16 = gather(tokens[0], "seq")
    qkv_rows = local[:, :shard_qkv].reshape(rows, 3 * width)
    fc1_rows = local[:, shard_qkv : shard_qkv + shard_fc1].reshape(rows, hidden)
    ov_flat = local[:, shard_qkv + shard_fc1 : shard_qkv + shard_fc1 + shard_ov].reshape(-1)
    ov_cols = round_up(-(-ov_flat.shape[0] // rows), LANES)
    ov_part = jnp.pad(ov_flat, (0, rows * ov_cols - ov_flat.shape[0])).reshape(rows, ov_cols)
    qkv_part = jnp.concatenate(
        [
            lax.dynamic_slice_in_dim(qkv_rows, j * width + position * cols, cols, axis=1)
            for j in range(3)
        ]
        + [jnp.zeros((rows, pad_cols), bf16)],
        axis=1,
    )
    fc1_part = jnp.pad(
        lax.dynamic_slice_in_dim(fc1_rows, position * units, units, axis=1),
        ((0, 0), (0, pad_units)),
    )
    fc2_chunk = lax.ppermute(pack(w_fc2), both, to_quarter).reshape(-1)[:shard_fc2]
    fc2_part = jnp.pad(fc2_chunk.reshape(rows, units), ((0, 0), (0, pad_units)))
    weights = gather(jnp.concatenate([qkv_part, fc1_part, fc2_part, ov_part], axis=1), "img")
    end_qkv = 3 * cols + pad_cols
    end_fc1 = end_qkv + units + pad_units
    end_fc2 = end_fc1 + units + pad_units
    mat_qkv = weights[:, :end_qkv]
    mat_fc1 = weights[:, end_qkv:end_fc1]
    mat_fc2 = jnp.pad(
        weights[:, end_fc1 : end_fc1 + units].reshape(units, width), ((0, pad_units), (0, 0))
    )
    out_vec = weights[:, end_fc2:].reshape(img_count, -1)[:, : seq_count * shard_ov]
    cot_all = gather(cotangent[0], "seq")

    blocks_ov = out_vec.reshape(device_count, -1)
    mat_out = blocks_ov[:, :shard_out].reshape(width, width)
    vec = blocks_ov[:, shard_out : shard_out + shard_vec].reshape(-1).astype(f32)
    bias1, v_bias, gain1, q_bias, out_bias, gain2, bias2, fc2_bias = (
        vec[i * width : (i + 1) * width] for i in range(8)
    )
    fc1_bias = vec[8 * width : 8 * width + hidden]

    def my_cols(values):
        return lax.dynamic_slice_in_dim(values, position * cols, cols)

    fc1_bias_mine = jnp.pad(
        lax.dynamic_slice_in_dim(fc1_bias, position * units, units), (0, pad_units)
    )

    x = x_all16.astype(f32)
    normed1, _ = normalize(x)
    ln1 = (normed1 * gain1 + bias1).astype(bf16)
    qkv = jnp.dot(ln1, mat_qkv, preferred_element_type=f32)

    def by_head(values):
        return values.reshape(-1, heads, HEAD_DIM).transpose(1, 0, 2)

    def by_slot(values):
        return values.transpose(1, 0, 2).reshape(-1, cols)

    queries = by_head((qkv[:, :cols] + my_cols(q_bias)).astype(bf16))
    keys = by_head(qkv[:, cols : 2 * cols].astype(bf16))
    values = by_head((qkv[:, 2 * cols : 3 * cols] + my_cols(v_bias)).astype(bf16))
    scores = batched(queries, keys, 2, 2) * scale
    scores = jnp.where(key_valid[None, None, :], scores, -1e30)
    top = jnp.max(scores, axis=-1, keepdims=True)
    lse = top + jnp.log(jnp.sum(jnp.exp(scores - top), axis=-1, keepdims=True))
    probs = jnp.exp(scores - lse).astype(bf16)
    mixed_heads = batched(probs, values, 2, 1)
    mixed_mine = by_slot(mixed_heads).astype(bf16)
    mixed = lax.all_gather(mixed_mine, "seq", axis=0, tiled=True)
    mixed = (
        mixed.reshape(seq_count, -1, cols).transpose(1, 0, 2).reshape(-1, width)
    )
    resid = x + jnp.dot(mixed, mat_out, preferred_element_type=f32) + out_bias
    normed2, rstd2 = normalize(resid)
    ln2 = (normed2 * gain2 + bias2).astype(bf16)
    pre = jnp.dot(ln2, mat_fc1, preferred_element_type=f32) + fc1_bias_mine
    act_f, slope = gelu_parts(pre)
    act = act_f.astype(bf16)

    grad_y16 = jnp.where(key_valid[:, None], cot_all, jnp.zeros((), bf16))
    grad_pre = dot_t(grad_y16, mat_fc2) * slope
    grad_pre16 = grad_pre.astype(bf16)
    grad_ln2 = scatter_sum(dot_t(grad_pre16, mat_fc1).astype(bf16), "seq").astype(f32)
    grad_y = cotangent[0].astype(f32) * rowmask
    normed2_mine = mine(normed2)
    grad_resid = grad_y + norm_back(grad_ln2, normed2_mine, mine(rstd2), gain2)
    grad_resid16 = gather(grad_resid.astype(bf16), "seq")

    part_fc1 = weight_grad(ln2, grad_pre16)
    part_fc2 = pack_blocks(weight_grad(act, grad_y16)[:units].reshape(-1), img_count)
    out_terms = scatter_sum(
        jnp.dot(act, mat_fc2, preferred_element_type=f32).astype(bf16), "seq"
    ).astype(f32)
    output = ((mine(resid) + out_terms + fc2_bias) * rowmask).astype(bf16)

    out_mine = lax.dynamic_slice_in_dim(mat_out, position * cols, cols)
    gm = by_head(dot_t(grad_resid16, out_mine).astype(bf16))
    mixed_back = by_head(mixed_mine)
    delta = jnp.sum(gm.astype(f32) * mixed_back.astype(f32), axis=-1, keepdims=True)
    grad_values = by_slot(batched(probs, gm, 1, 1))
    dots = batched(gm, values, 2, 2)
    grad_scores = (jnp.exp(scores - lse) * (dots - delta) * scale).astype(bf16)
    grad_queries = by_slot(batched(grad_scores, keys, 2, 1))
    grad_keys = by_slot(batched(grad_scores, queries, 1, 1))
    grad_qkv16 = jnp.concatenate(
        [grad_queries.astype(bf16), grad_keys.astype(bf16), grad_values.astype(bf16)]
        + [jnp.zeros((seq_count * slot, pad_cols), bf16)],
        axis=1,
    )
    grad_ln1 = scatter_sum(dot_t(grad_qkv16, mat_qkv).astype(bf16), "seq").astype(f32)
    part_qkv = weight_grad(ln1, grad_qkv16)
    part_out = pack_blocks(weight_grad(mixed_mine, grad_resid16).reshape(-1), img_count)
    normed1_mine, rstd1_mine = normalize(tokens[0].astype(f32))
    input_grad = grad_resid + norm_back(grad_ln1, normed1_mine, rstd1_mine, gain1)

    def spread(part, full):
        return lax.dynamic_update_slice_in_dim(
            jnp.zeros((full,), f32), part, position * part.shape[0], 0
        )

    shard_front = 2 * width // device_count
    unused = shard_vec * device_count - 8 * width - hidden
    g_front = jnp.concatenate(
        [jnp.sum(grad_ln1, axis=0), spread(jnp.sum(grad_values, axis=0), width)]
    )
    g_rest = jnp.concatenate(
        [
            jnp.sum(grad_ln1 * normed1_mine, axis=0),
            spread(jnp.sum(grad_queries, axis=0), width),
            jnp.sum(grad_resid, axis=0),
            jnp.sum(grad_ln2 * normed2_mine, axis=0),
            jnp.sum(grad_ln2, axis=0),
            jnp.sum(grad_y, axis=0),
            spread(jnp.sum(grad_pre, axis=0)[:units], hidden),
            jnp.zeros((unused,), f32),
        ]
    )
    g_vec = jnp.concatenate(
        [g_front.reshape(device_count, -1), g_rest.reshape(device_count, -1)], axis=1
    )
    vec_pad = round_up(shard_vec, 4 * LANES)
    part_vec = jnp.pad(g_vec, ((0, 0), (0, vec_pad - shard_vec))).astype(bf16)

    parts = [
        part.reshape(img_count, -1, LANES)
        for part in (part_qkv, part_fc1, part_vec, part_fc2, part_out)
    ]
    sizes = [part.shape[1] for part in parts]
    summed = scatter_sum(jnp.concatenate(parts, axis=1).reshape(-1, LANES), "img")
    ends = [sum(sizes[: i + 1]) for i in range(5)]
    chunks = lax.ppermute(summed[ends[2] :], both, to_owner)
    grad_fc2 = chunks[: sizes[3]].reshape(-1)[:shard_fc2].astype(f32)
    grad_out = chunks[sizes[3] :].reshape(-1)[:shard_out].astype(f32)
    shared = gather(summed[: ends[2]], "seq").reshape(seq_count, ends[2], LANES)

    def own_block(packed, thirds, used, size):
        blocks = packed.reshape(seq_count, rows, -1)[:, :, : thirds * used]
        whole = blocks.reshape(seq_count, rows, thirds, used).transpose(1, 2, 0, 3)
        return lax.dynamic_slice_in_dim(whole.reshape(-1), position * size, size).astype(f32)

    grad_qkv = own_block(shared[:, : ends[0]], 3, cols, shard_qkv)
    grad_fc1 = own_block(shared[:, ends[0] : ends[1]], 1, units, shard_fc1)
    vec_sums = jnp.sum(shared[:, ends[1] :].astype(f32), axis=0).reshape(seq_count, vec_pad)
    vec_mine = lax.dynamic_slice_in_dim(vec_sums, position, 1).reshape(-1)
    return (
        output[None],
        input_grad[None],
        grad_qkv,
        grad_out,
        grad_fc1,
        grad_fc2,
        vec_mine[shard_front:shard_vec],
        vec_mine[:shard_front],
    )


def shards(tokens, counts, w_qkv, w_out, w_fc1, w_fc2, vectors, cotangent):
    width = tokens.shape[2]
    slot = tokens.shape[1]
    scale = HEAD_DIM ** (-0.5)
    position = lax.axis_index("seq")
    seq_count = lax.axis_size("seq")
    img_count = lax.axis_size("img")
    device_count = img_count * seq_count
    chunk = lax.axis_index("img") * seq_count + position
    shard_vec = vectors.shape[0]
    plan = Plan(img_count, seq_count, width, w_fc1.shape[0], shard_vec)
    hidden, cols, rows, units = plan.hidden, plan.cols, plan.rows, plan.units
    heads = HEADS // seq_count
    shard_fc = plan.shard_fc

    slice_counts = counts[0]
    key_valid = (jnp.arange(slot)[None, :] < slice_counts[:, None]).reshape(-1)
    row_valid = lax.dynamic_slice_in_dim(key_valid, position * slot, slot)
    rowmask = row_valid.astype(F32)[:, None]
    key_ok = key_valid.astype(F32)[None]

    shifts = sorted({g * shard_fc % width for g in range(device_count)})
    shift = lax.rem(chunk * shard_fc, width)
    fc2_flat = jnp.zeros((), BF16)
    for by in shifts:
        placed = jnp.pad(w_fc2, (by, plan.block * width - by - shard_fc))
        fc2_flat = jnp.where(shift == by, placed, fc2_flat)
    ov = jnp.pad(w_out.reshape(plan.sub, width), ((0, plan.sub_pad - plan.sub), (0, 0)))
    vec_in = jnp.pad(vectors[None], ((0, 15), (0, round_up(shard_vec, LANES) - shard_vec)))
    f = forward(
        plan,
        slot,
        heads,
        dict(
            qkv=w_qkv.reshape(plan.sub, 3 * width),
            fc1=w_fc1.reshape(plan.sub, hidden),
            fc2=fc2_flat.reshape(plan.block, width),
            ov=ov,
            vec_in=vec_in,
            x=tokens[0],
            cot=cotangent[0],
            key_ok=key_ok,
        ),
    )
    mat_fc1 = f.wf1.reshape(width, units)
    mat_fc2 = f.wf2.reshape(units, width)
    cot_all = f.cots.reshape(seq_count * slot, width)
    pre = jnp.dot(f.ln2, mat_fc1, preferred_element_type=F32) + f.fc1_bias
    act_f, slope = gelu_parts(pre)
    act = act_f.astype(BF16)
    grad_y16 = jnp.where(key_valid[:, None], cot_all, jnp.zeros((), BF16))
    grad_pre = dot_t(grad_y16, mat_fc2) * slope
    grad_pre16 = grad_pre.astype(BF16)
    ln2_part = dot_t(grad_pre16, mat_fc1).astype(BF16)
    out_part = jnp.dot(act, mat_fc2, preferred_element_type=F32).astype(BF16)
    part_fc1 = weight_grad(f.ln2, grad_pre16)
    part_fc2 = weight_grad(act, grad_y16)

    output, input_grad, grad2, grad1, gradq, grado, gradv = backward(
        plan,
        slot,
        heads,
        dict(
            g2=part_fc2,
            g1=part_fc1,
            ln2_part=ln2_part,
            out_part=out_part,
            grad_y=cotangent[0].astype(F32) * rowmask,
            rowmask=rowmask,
            key_ok=key_ok,
            pre_sums=jnp.sum(grad_pre, axis=0, keepdims=True),
            **{name: getattr(f, name) for name in BackwardIn._fields if name in ForwardOut._fields},
        ),
    )
    grad_fc2 = lax.dynamic_slice_in_dim(grad2.reshape(-1), shift, shard_fc)
    shard_front = 2 * width // device_count
    vec_sums = jnp.sum(gradv.astype(F32), axis=0)
    vec_mine = lax.dynamic_slice_in_dim(vec_sums, position, 1).reshape(-1)
    return (
        output[None],
        input_grad[None],
        gradq.reshape(-1),
        grado.reshape(-1),
        grad1.reshape(-1),
        grad_fc2,
        vec_mine[shard_front:shard_vec],
        vec_mine[:shard_front],
    )


def solution(mesh):
    def layer(*arrays):
        width = arrays[0].shape[2]
        whole_rows = (
            width % mesh.size == 0
            and mesh.shape["seq"] == 4
            and width // mesh.shape["img"] % 16 == 0
        )
        return (shards if whole_rows else shards_by_rows)(*arrays)

    return jax.shard_map(
        layer,
        mesh=mesh,
        in_specs=(
            P("img", "seq", None),
            P("img", None),
            P(("img", "seq")),
            P(("img", "seq")),
            P(("img", "seq")),
            P(("img", "seq")),
            P(("img", "seq")),
            P("img", "seq", None),
        ),
        out_specs=(
            P("img", "seq", None),
            P("img", "seq", None),
            P(("img", "seq")),
            P(("img", "seq")),
            P(("img", "seq")),
            P(("img", "seq")),
            P(("img", "seq")),
            P(("img", "seq")),
        ),
        check_vma=False,
    )
```

```python
import functools
from typing import NamedTuple

import jax
import jax.numpy as jnp
from jax import lax
from jax.experimental import pallas as pl
from jax.experimental.pallas import tpu as pltpu
from jax.sharding import PartitionSpec as P

HEADS = 16
HEAD_DIM = 72
EPS = 1e-06
GELU_C = 0.7978845608028654
LANES = 128
VMEM_LIMIT = 58 * 1024 * 1024
ACROSS = 1
PACE = ((1, 1, 1, 0), (1, 1, 1, 1), (1, 1, 1, 1), (1, 1), (0, 0, 0, 0))
F32 = jnp.float32
BF16 = jnp.bfloat16


def round_up(value, step):
    return -(-value // step) * step


class Plan:
    def __init__(self, img, seq, width, shard_fc, shard_vec):
        self.img, self.seq, self.width = img, seq, width
        self.line = img // 2
        self.devices = img * seq
        self.hidden = shard_fc * self.devices // width
        self.cols = width // seq
        self.rows = width // img
        self.rows_pad = round_up(self.rows, 16)
        self.sub = self.rows // seq
        self.sub_pad = round_up(self.sub, 16)
        self.shard_fc, self.shard_vec = shard_fc, shard_vec
        self.first = [g * shard_fc // width for g in range(self.devices)]
        self.last = [-(-(g + 1) * shard_fc // width) for g in range(self.devices)]
        self.block = round_up(max(b - a for a, b in zip(self.first, self.last)), 16)
        self.units = img * self.block
        self.qkv_cols = round_up(3 * self.cols, LANES)
        self.mix_cols = round_up(4 * self.cols, LANES)


def coords(plan):
    index = lax.axis_index("img")
    return index // 2, lax.rem(index, 2), lax.axis_index("seq")


def remote(src, dst, send, recv, img, seq):
    return pltpu.make_async_remote_copy(
        src_ref=src,
        dst_ref=dst,
        send_sem=send,
        recv_sem=recv,
        device_id=(img, seq),
        device_id_type=pl.DeviceIdType.MESH,
    )


def entry_barrier(plan, z, y, s):
    barrier = pltpu.get_barrier_semaphore()

    def greet(img, seq):
        pl.semaphore_signal(
            barrier, inc=1, device_id=(img, seq), device_id_type=pl.DeviceIdType.MESH
        )

    @pl.when(z > 0)
    def _():
        greet((z - 1) * 2 + y, s)

    @pl.when(z < plan.line - 1)
    def _():
        greet((z + 1) * 2 + y, s)

    greet(z * 2 + 1 - y, s)
    for k in range(1, plan.seq):
        greet(z * 2 + y, lax.rem(s + k, plan.seq))
    peers = plan.seq + jnp.minimum(z, 1) + jnp.minimum(plan.line - 1 - z, 1)
    pl.semaphore_wait(barrier, peers)


class ForwardIn(NamedTuple):
    qkv: jax.Array
    fc1: jax.Array
    fc2: jax.Array
    ov: jax.Array
    vec_in: jax.Array
    x: jax.Array
    cot: jax.Array
    key_ok: jax.Array


class ForwardOut(NamedTuple):
    wf1: jax.Array
    wf2: jax.Array
    cots: jax.Array
    mat_qkv: jax.Array
    queries: jax.Array
    keys: jax.Array
    values: jax.Array
    lse: jax.Array
    mixed_mine: jax.Array
    mixed: jax.Array
    ln1: jax.Array
    ln2: jax.Array
    base: jax.Array
    normed2: jax.Array
    rstd2: jax.Array
    normed1: jax.Array
    rstd1: jax.Array
    out_mine: jax.Array
    gain1: jax.Array
    gain2: jax.Array
    fc1_bias: jax.Array


class ForwardScratch(NamedTuple):
    cq: jax.Array
    cf: jax.Array
    rq: jax.Array
    rf: jax.Array
    mq: jax.Array
    mf: jax.Array
    wo: jax.Array
    vecs: jax.Array
    mat_out: jax.Array
    xs: jax.Array
    vec: jax.Array
    qkv_all: jax.Array
    others: jax.Array
    loc_sem: jax.Array
    up_sem: jax.Array
    down_sem: jax.Array
    side_sem: jax.Array
    got_sem: jax.Array
    seq_send: jax.Array
    seq_recv: jax.Array
    ag_send: jax.Array
    ag_recv: jax.Array


FORWARD = ForwardIn._fields + ForwardOut._fields + ForwardScratch._fields


class Refs:
    def __init__(self, names, refs):
        self.__dict__.update(zip(names, refs))


def forward_kernel(plan, items, heads, *refs):
    r = Refs(FORWARD, refs)
    z, y, s = coords(plan)
    me = z * 2 + y
    line, seq, sub, cols, width = plan.line, plan.seq, plan.sub, plan.cols, plan.width
    slot = r.x.shape[0]
    scale = HEAD_DIM ** (-0.5)
    entry_barrier(plan, z, y, s)
    sources = dict(vec=r.vec_in, ov=r.ov, fc2=r.fc2, wq=r.mq, wf1=r.mf)

    def source(q):
        name, a, n = items[q]
        return sources[name].at[pl.ds(a, n)]

    def target(q, piece):
        name, a, n = items[q]
        if name == "vec":
            return r.vecs.at[s, piece]
        if name == "ov":
            return r.wo.at[s, piece]
        if name == "wq":
            return r.mat_qkv.at[pl.ds(pl.multiple_of(piece * plan.rows_pad + a, 16), n)]
        return {"fc2": r.wf2, "wf1": r.wf1}[name].at[piece, pl.ds(a, n)]

    def hop(q, piece, src, way):
        img = {"up": me + 2, "down": me - 2, "side": z * 2 + 1 - y}[way]
        sem = {"up": r.up_sem, "down": r.down_sem, "side": r.side_sem}[way]
        return remote(src, target(q, piece), sem.at[q, piece], r.got_sem.at[q, piece], img, s)

    def own_copy(q):
        return pltpu.make_async_copy(source(q), target(q, me), r.loc_sem.at[q])

    def own(q):
        own_copy(q).start()
        hop(q, me, source(q), "side").start()

        @pl.when(z < line - 1)
        def _():
            hop(q, me, source(q), "up").start()

        @pl.when(z > 0)
        def _():
            hop(q, me, source(q), "down").start()

    def line_only(q, d):
        for yy in (y, 1 - y):
            low, high = (z - d) * 2 + yy, (z + d) * 2 + yy

            @pl.when(z - d >= 0)
            def _():
                hop(q, low, target(q, low), "up").wait_recv()

                @pl.when(z < line - 1)
                def _():
                    hop(q, low, target(q, low), "up").start()

            @pl.when(z + d < line)
            def _():
                hop(q, high, target(q, high), "down").wait_recv()

                @pl.when(z > 0)
                def _():
                    hop(q, high, target(q, high), "down").start()

    def from_side(q):
        other = z * 2 + 1 - y
        hop(q, other, target(q, other), "side").wait_recv()

        @pl.when(z < line - 1)
        def _():
            hop(q, other, target(q, other), "up").start()

        @pl.when(z > 0)
        def _():
            hop(q, other, target(q, other), "down").start()

    def pass_on(q, d):
        if q in across_first:
            if d == 1:
                from_side(q)
            line_only(q, d)
            return
        low = (z - d) * 2 + y
        high = (z + d) * 2 + y

        @pl.when(z - d >= 0)
        def _():
            hop(q, low, target(q, low), "side").wait_recv()
            hop(q, low, target(q, low), "side").start()

            @pl.when(z < line - 1)
            def _():
                hop(q, low, target(q, low), "up").start()

        @pl.when(z + d < line)
        def _():
            hop(q, high, target(q, high), "side").wait_recv()
            hop(q, high, target(q, high), "side").start()

            @pl.when(z > 0)
            def _():
                hop(q, high, target(q, high), "down").start()

    def wait_side(q):
        for zs in range(line):
            piece = zs * 2 + 1 - y
            if q not in across_first:
                hop(q, piece, target(q, piece), "side").wait_recv()
        own_copy(q).wait()

    def exchange(a, src, dst, k):
        peer = lax.rem(s + k, seq)
        return remote(src, dst, r.seq_send.at[a, k], r.seq_recv.at[a, k], me, peer)

    def came_from(k):
        return lax.rem(s + seq - k, seq)

    core = lax.rem(s, 2)
    mate, cross = s + 1 - 2 * core, lax.rem(s + 2, seq)

    def spread(n, own, part, owner, to, k):
        src = part(owner) if own is None else own
        return remote(src, part(owner), r.ag_send.at[n, k], r.ag_recv.at[n, k], me, to)

    def spread_start(n, own, part):
        spread(n, own, part, s, cross, 0).start()
        spread(n, own, part, s, mate, 1).start()

    def spread_on(n, own, part):
        spread(n, None, part, cross, cross, 0).wait_recv()
        spread(n, None, part, cross, mate, 2).start()

    def spread_end(n, own, part):
        spread(n, None, part, mate, mate, 1).wait_recv()
        spread(n, None, part, lax.rem(mate + 2, seq), mate, 2).wait_recv()

    def spread_sent(n, own, part):
        spread(n, own, part, s, cross, 0).wait_send()
        spread(n, own, part, s, mate, 1).wait_send()
        spread(n, None, part, cross, mate, 2).wait_send()

    def item(name):
        return [q for q in range(len(items)) if items[q][0] == name]

    def rows_of(t):
        return pl.ds(pl.multiple_of(t * slot, slot), slot)

    across_first = item("fc2")[-ACROSS:] if ACROSS else []

    xs = (0, r.x, lambda t: r.xs.at[rows_of(t)])
    cots = (1, r.cot, lambda t: r.cots.at[t])
    vecs = (2, None, lambda t: r.vecs.at[t])
    wos = (3, None, lambda t: r.wo.at[t])
    mixes = (4, r.mixed_mine, lambda t: r.others.at[t])
    own(item("vec")[0])
    own(item("ov")[0])
    early = item("fc2")[:1]
    for q in early:
        own(q)
    x_copy = pltpu.make_async_copy(r.x, r.xs.at[rows_of(s)], r.loc_sem.at[len(items)])
    cot_copy = pltpu.make_async_copy(r.cot, r.cots.at[s], r.loc_sem.at[len(items) + 1])
    r.cq[...] = jnp.zeros_like(r.cq)
    for t in range(seq):
        for j in range(3):
            at = j * width + t * cols
            r.cq[t, :sub, j * cols : (j + 1) * cols] = r.qkv[:, at : at + cols]
    for k in range(1, seq):
        exchange(0, r.cq.at[lax.rem(s + k, seq)], r.rq.at[s], k).start()
    x_copy.start()
    spread_start(*xs)
    r.cf[...] = jnp.zeros_like(r.cf)
    for g in range(plan.devices):
        i, t = g // seq, g % seq
        a, b = plan.first[g], plan.last[g]
        r.cf[t, :sub, i * plan.block : i * plan.block + b - a] = r.fc1[:, a:b]
    for k in range(1, seq):
        exchange(1, r.cf.at[lax.rem(s + k, seq)], r.rf.at[s], k).start()
    wq, late = item("wq"), [q for q in item("fc2") if q not in early]

    def merge(a, sent, got, merged):
        for k in range(1, seq):
            exchange(a, sent.at[lax.rem(s + k, seq)], got.at[came_from(k)], k).wait()
        got[s] = sent[s]
        for t in range(seq):
            merged[t * sub : (t + 1) * sub, :] = got[t, :sub, :]

    def all_on(queue, d):
        for q in queue:
            pass_on(q, d)

    all_on(item("vec"), 1)
    merge(0, r.cq, r.rq, r.mq)
    own(wq[0])
    all_on(item("ov"), 1)
    all_on(item("vec"), 2)
    spread_on(*xs)
    for q in late:
        own(q)
    merge(1, r.cf, r.rf, r.mf)
    all_on(wq, 1)
    for d in range(3, line):
        all_on(item("vec"), d)
    for d in range(2, line):
        all_on(item("ov"), d)
    wait_side(item("vec")[0])
    spread_start(*vecs)
    for q in item("wf1"):
        own(q)
    for d in range(2, line):
        all_on(wq, d)
    all_on(early, 1)
    spread_on(*vecs)
    wait_side(item("ov")[0])
    spread_start(*wos)
    cot_copy.start()
    spread_start(*cots)
    all_on(late, 1)
    for d in range(2, line):
        all_on(early, d)

    rest = [(q, 1) for q in item("wf1")]
    rest += [(q, d) for d in range(2, line) for q in late + item("wf1")]

    def service(n=1):
        for _ in range(n):
            if rest:
                pass_on(*rest.pop(0))

    x_copy.wait()
    spread_end(*xs)
    spread_end(*vecs)
    count = plan.shard_vec
    for g in range(plan.devices):
        i, t = g // seq, g % seq
        r.vec[:, g * count : (g + 1) * count] = r.vecs[t, i, :1, :count].astype(F32)
    bias1, v_bias, gain1, q_bias, out_bias, gain2, bias2, fc2_bias = (
        r.vec[:, n * width : (n + 1) * width] for n in range(8)
    )
    r.gain1[...] = gain1
    r.gain2[...] = gain2
    r.fc1_bias[...] = jnp.zeros_like(r.fc1_bias)
    for t in range(seq):

        @pl.when(s == t)
        def _():
            for i in range(plan.img):
                a, b = plan.first[i * seq + t], plan.last[i * seq + t]
                to = i * plan.block
                r.fc1_bias[:, to : to + b - a] = r.vec[:, 8 * width + a : 8 * width + b]

    for t in range(seq):
        rows = slice(t * slot, (t + 1) * slot)
        normed, rstd = normalize(r.xs[rows, :].astype(F32))
        r.ln1[rows, :] = (normed * gain1 + bias1).astype(BF16)

        @pl.when(s == t)
        def _():
            r.normed1[...] = normed
            r.rstd1[...] = rstd

        service(PACE[0][t])

    for q in item("wq"):
        wait_side(q)
    for t in range(seq):
        rows = slice(t * slot, (t + 1) * slot)
        r.qkv_all[rows, :] = jnp.dot(
            r.ln1[rows, :], r.mat_qkv[...], preferred_element_type=F32
        )
        service(PACE[1][t])
    for t in range(seq):

        @pl.when(s == t)
        def _():
            lanes = slice(t * cols, (t + 1) * cols)
            r.qkv_all[:, :cols] += q_bias[:, lanes]
            r.qkv_all[:, 2 * cols : 3 * cols] += v_bias[:, lanes]

    for h in range(heads):
        for j, out in enumerate((r.queries, r.keys, r.values)):
            at = j * cols + h * HEAD_DIM
            out[h] = r.qkv_all[:, at : at + HEAD_DIM].astype(BF16)
    tile = 2 * slot
    for h in range(heads):
        lanes = slice(h * HEAD_DIM, (h + 1) * HEAD_DIM)
        key, value = r.keys[h], r.values[h]
        for at in range(0, seq * slot, tile):
            rows = slice(at, at + tile)
            scores = dot_t(r.queries[h, rows, :], key) * scale
            scores = jnp.where(r.key_ok[...] > 0, scores, -1e30)
            top = jnp.max(scores, axis=-1, keepdims=True)
            terms = jnp.exp(scores - top)
            total = jnp.sum(terms, axis=-1, keepdims=True)
            r.lse[h, rows, :] = top + jnp.log(total)
            probs = (terms * (1.0 / total)).astype(BF16)
            r.mixed_mine[rows, lanes] = jnp.dot(
                probs, value, preferred_element_type=F32
            ).astype(BF16)
        service(PACE[2][h])
        if h == 0:
            spread_on(*wos)
        if h == heads - 1:
            spread_on(*cots)

    spread_start(*mixes)
    r.others[s] = r.mixed_mine[...]
    spread_end(*wos)
    for g in range(plan.devices):
        i, t = g // seq, g % seq
        r.mat_out[g * sub : (g + 1) * sub, :] = r.wo[t, i, :sub, :]
    for t in range(seq):

        @pl.when(s == t)
        def _():
            r.out_mine[...] = r.mat_out[t * cols : (t + 1) * cols, :]

    service(PACE[3][0])
    spread_on(*mixes)
    service(PACE[3][1])
    spread_end(*mixes)
    for t in range(seq):
        r.mixed[:, t * cols : (t + 1) * cols] = r.others[t]
    for t in range(seq):
        rows = slice(t * slot, (t + 1) * slot)
        resid = (
            r.xs[rows, :].astype(F32)
            + jnp.dot(r.mixed[rows, :], r.mat_out[...], preferred_element_type=F32)
            + out_bias
        )
        normed, rstd = normalize(resid)
        r.ln2[rows, :] = (normed * gain2 + bias2).astype(BF16)

        @pl.when(s == t)
        def _():
            r.base[...] = resid + fc2_bias
            r.normed2[...] = normed
            r.rstd2[...] = rstd

        service(PACE[4][t])
    service(len(rest))
    for q in item("fc2") + item("wf1"):
        wait_side(q)

    def wait_sends(q, piece, zs):
        @pl.when(jnp.logical_and(z < line - 1, zs <= z))
        def _():
            hop(q, piece, target(q, piece), "up").wait_send()

        @pl.when(jnp.logical_and(z > 0, zs >= z))
        def _():
            hop(q, piece, target(q, piece), "down").wait_send()

    for q in range(len(items)):
        if q in across_first:
            hop(q, me, target(q, me), "side").wait_send()
        for zs in range(line):
            wait_sends(q, zs * 2 + y, zs)
            if q in across_first:
                wait_sends(q, zs * 2 + 1 - y, zs)
            else:
                hop(q, zs * 2 + y, target(q, zs * 2 + y), "side").wait_send()

    cot_copy.wait()
    spread_end(*cots)
    for each in (xs, cots, vecs, wos, mixes):
        spread_sent(*each)


def forward(plan, slot, heads, args):
    any_spec = pl.BlockSpec(memory_space=pl.ANY)
    vmem = pl.BlockSpec(memory_space=pltpu.VMEM)
    img, seq, width, cols = plan.img, plan.seq, plan.width, plan.cols
    tokens = seq * slot
    dma = pltpu.SemaphoreType.DMA
    shape = jax.ShapeDtypeStruct
    items = [("vec", 0, 16), ("ov", 0, plan.sub_pad)]
    step = 48
    for name, rows, by in (
        ("fc2", plan.block, step),
        ("wq", plan.rows_pad, plan.rows_pad),
        ("wf1", plan.rows_pad, step),
    ):
        items += [(name, a, min(by, rows - a)) for a in range(0, rows, by)]
    n = len(items)
    head = shape((heads, tokens, HEAD_DIM), BF16)
    all16 = shape((tokens, width), BF16)
    own32 = shape((slot, width), F32)
    column = shape((slot, 1), F32)
    row = shape((1, width), F32)
    outs = (
        shape((img, plan.rows_pad, plan.units), BF16),
        shape((img, plan.block, width), BF16),
        shape((seq, slot, width), BF16),
        shape((img * plan.rows_pad, plan.qkv_cols), BF16),
        head,
        head,
        head,
        shape((heads, tokens, 1), F32),
        shape((tokens, cols), BF16),
        all16,
        all16,
        all16,
        own32,
        own32,
        column,
        own32,
        column,
        shape((cols, width), BF16),
        row,
        row,
        shape((1, plan.units), F32),
    )
    result = pl.pallas_call(
        functools.partial(forward_kernel, plan, items, heads),
        out_shape=outs,
        in_specs=[vmem, vmem, any_spec, any_spec, vmem, vmem, any_spec, vmem],
        out_specs=(any_spec,) * 3 + (vmem,) * (len(outs) - 3),
        scratch_shapes=[
            pltpu.VMEM((seq, plan.sub_pad, plan.qkv_cols), BF16),
            pltpu.VMEM((seq, plan.sub_pad, plan.units), BF16),
            pltpu.VMEM((seq, plan.sub_pad, plan.qkv_cols), BF16),
            pltpu.VMEM((seq, plan.sub_pad, plan.units), BF16),
            pltpu.VMEM((plan.rows_pad, plan.qkv_cols), BF16),
            pltpu.VMEM((plan.rows_pad, plan.units), BF16),
            pltpu.VMEM((seq, img, plan.sub_pad, width), BF16),
            pltpu.VMEM((seq, img, *args["vec_in"].shape), BF16),
            pltpu.VMEM((width, width), BF16),
            pltpu.VMEM((tokens, width), BF16),
            pltpu.VMEM((1, plan.shard_vec * plan.devices), F32),
            pltpu.VMEM((tokens, plan.qkv_cols), F32),
            pltpu.VMEM((seq, tokens, cols), BF16),
            dma((n + 2,)),
            *[dma((n, img))] * 4,
            *[dma((2, seq))] * 2,
            *[dma((5, 3))] * 2,
        ],
        compiler_params=pltpu.CompilerParams(
            collective_id=0, has_side_effects=True, vmem_limit_bytes=VMEM_LIMIT
        ),
        name="forward",
    )(*[args[name] for name in ForwardIn._fields])
    return Refs(ForwardOut._fields, result)


def dot_00(left, right):
    return lax.dot_general(left, right, (((0,), (0,)), ((), ())), preferred_element_type=F32)


def dot_t(left, right):
    return lax.dot_general(left, right, (((1,), (1,)), ((), ())), preferred_element_type=F32)


def norm_back(grad_in, normed, rstd, gain):
    scaled = grad_in * gain
    return rstd * (
        scaled
        - jnp.mean(scaled, axis=-1, keepdims=True)
        - normed * jnp.mean(scaled * normed, axis=-1, keepdims=True)
    )


class BackwardIn(NamedTuple):
    g2: jax.Array
    g1: jax.Array
    ln2_part: jax.Array
    out_part: jax.Array
    normed2: jax.Array
    rstd2: jax.Array
    gain2: jax.Array
    grad_y: jax.Array
    base: jax.Array
    rowmask: jax.Array
    queries: jax.Array
    keys: jax.Array
    values: jax.Array
    lse: jax.Array
    key_ok: jax.Array
    mixed_mine: jax.Array
    mixed: jax.Array
    ln1: jax.Array
    mat_qkv: jax.Array
    out_mine: jax.Array
    normed1: jax.Array
    rstd1: jax.Array
    gain1: jax.Array
    pre_sums: jax.Array


class BackwardOut(NamedTuple):
    output: jax.Array
    input_grad: jax.Array
    o2: jax.Array
    o1: jax.Array
    oq: jax.Array
    oo: jax.Array
    ov: jax.Array


class BackwardScratch(NamedTuple):
    side2: jax.Array
    side1: jax.Array
    sidem: jax.Array
    sidev: jax.Array
    low2: jax.Array
    low1: jax.Array
    lowm: jax.Array
    lowv: jax.Array
    high2: jax.Array
    high1: jax.Array
    highm: jax.Array
    highv: jax.Array
    acc2: jax.Array
    acc1: jax.Array
    accm: jax.Array
    accv: jax.Array
    fin1: jax.Array
    finm: jax.Array
    cut1: jax.Array
    cutm: jax.Array
    cutv: jax.Array
    got1: jax.Array
    gotm: jax.Array
    gmix: jax.Array
    gvec: jax.Array
    gvec32: jax.Array
    front: jax.Array
    rest: jax.Array
    qsum: jax.Array
    vsum: jax.Array
    pair_ln2: jax.Array
    cross_ln2: jax.Array
    sum_ln2: jax.Array
    pair_out: jax.Array
    cross_out: jax.Array
    sum_out: jax.Array
    pair_ln1: jax.Array
    cross_ln1: jax.Array
    sum_ln1: jax.Array
    own_resid: jax.Array
    all_resid: jax.Array
    resid32: jax.Array
    gm: jax.Array
    gqkv: jax.Array
    part_ln1: jax.Array
    cols_resid: jax.Array
    side_send: jax.Array
    side_recv: jax.Array
    low_send: jax.Array
    low_recv: jax.Array
    high_send: jax.Array
    high_recv: jax.Array
    seq_send: jax.Array
    seq_recv: jax.Array
    rs_send: jax.Array
    rs_recv: jax.Array
    ag_send: jax.Array
    ag_recv: jax.Array


BACKWARD = BackwardIn._fields + BackwardOut._fields + BackwardScratch._fields


def backward_kernel(plan, parts, heads, *refs):
    r = Refs(BACKWARD, refs)
    z, y, s = coords(plan)
    me = z * 2 + y
    line, seq, sub, cols = plan.line, plan.seq, plan.sub, plan.cols
    width = plan.width
    slot = r.output.shape[0]
    scale = HEAD_DIM ** (-0.5)
    entry_barrier(plan, z, y, s)
    grads = [r.g2, r.g1, r.gmix, r.gvec]
    tall = [plan.block, plan.rows_pad, plan.rows_pad, 16]
    sides = [r.side2, r.side1, r.sidem, r.sidev]
    lows = [r.low2, r.low1, r.lowm, r.lowv]
    highs = [r.high2, r.high1, r.highm, r.highv]
    accs = [r.acc2, r.acc1, r.accm, r.accv]

    def at(c):
        q, a, n = parts[c]
        return q, pl.ds(a, n)

    def piece(c, img):
        q, a, n = parts[c]
        return grads[q].at[pl.ds(pl.multiple_of(img * tall[q] + a, 16), n)]

    def to_side(c, dest):
        q, w = at(c)
        return remote(
            piece(c, dest * 2 + 1 - y),
            sides[q].at[dest, w],
            r.side_send.at[c, dest],
            r.side_recv.at[c, dest],
            z * 2 + 1 - y,
            s,
        )

    def to_up(c, dest):
        q, w = at(c)
        return remote(
            accs[q].at[dest, w],
            lows[q].at[dest, w],
            r.low_send.at[c, dest],
            r.low_recv.at[c, dest],
            me + 2,
            s,
        )

    def to_down(c, dest):
        q, w = at(c)
        return remote(
            accs[q].at[dest, w],
            highs[q].at[dest, w],
            r.high_send.at[c, dest],
            r.high_recv.at[c, dest],
            me - 2,
            s,
        )

    def send_side(c):
        for d in range(line - 1, -1, -1):

            @pl.when(z + d < line)
            def _():
                to_side(c, z + d).start()

            if d:

                @pl.when(z - d >= 0)
                def _():
                    to_side(c, z - d).start()

    def both(c, dest):
        q, w = at(c)
        to_side(c, dest).wait_recv()
        return piece(c, dest * 2 + y)[...].astype(F32) + sides[q][dest, w, :].astype(F32)

    def pass_on(c):
        q, w = at(c)
        for d in range(line - 1, 0, -1):

            @pl.when(z + d < line)
            def _():
                dest = z + d
                total = both(c, dest)

                @pl.when(z > 0)
                def _():
                    to_up(c, dest).wait_recv()
                    accs[q][dest, w, :] = (total + lows[q][dest, w, :].astype(F32)).astype(BF16)

                @pl.when(z == 0)
                def _():
                    accs[q][dest, w, :] = total.astype(BF16)

                to_up(c, dest).start()

            @pl.when(z - d >= 0)
            def _():
                dest = z - d
                total = both(c, dest)

                @pl.when(z < line - 1)
                def _():
                    to_down(c, dest).wait_recv()
                    accs[q][dest, w, :] = (total + highs[q][dest, w, :].astype(F32)).astype(BF16)

                @pl.when(z == line - 1)
                def _():
                    accs[q][dest, w, :] = total.astype(BF16)

                to_down(c, dest).start()

    outs = [r.o2, r.fin1, r.finm, None]

    def finish(c):
        q, w = at(c)
        total = both(c, z)

        def store(value):
            if q == 3:
                r.cutv[s, w, :] = value.astype(BF16)
            else:
                outs[q][w, :] = value

        @pl.when(z == 0)
        def _():
            to_down(c, z).wait_recv()
            store(total + highs[q][z, w, :].astype(F32))

        @pl.when(z == line - 1)
        def _():
            to_up(c, z).wait_recv()
            store(total + lows[q][z, w, :].astype(F32))

        @pl.when(jnp.logical_and(z > 0, z < line - 1))
        def _():
            to_down(c, z).wait_recv()
            to_up(c, z).wait_recv()
            store(total + lows[q][z, w, :].astype(F32) + highs[q][z, w, :].astype(F32))

    def exchange(a, src, dst, k):
        peer = lax.rem(s + k, seq)
        return remote(src, dst, r.seq_send.at[a, k], r.seq_recv.at[a, k], me, peer)

    def came_from(k):
        return lax.rem(s + seq - k, seq)

    ends = {max(c for c in range(len(parts)) if parts[c][0] == q): q for q in (1, 2, 3)}

    def after(c):
        if c not in ends:
            return
        q = ends[c]
        if q == 3:
            for k in range(1, seq):
                exchange(2, r.cutv.at[s], r.ov.at[s], k).start()
            return
        fin, cut, got = ((r.fin1, r.cut1, r.got1), (r.finm, r.cutm, r.gotm))[q - 1]
        for t in range(seq):
            cut[t, :sub, :] = fin[t * sub : (t + 1) * sub, :].astype(BF16)
        for k in range(1, seq):
            exchange(q - 1, cut.at[lax.rem(s + k, seq)], got.at[s], k).start()

    def service(c):
        if c < len(parts):
            pass_on(c)
        if c >= 1:
            finish(c - 1)
            after(c - 1)

    core, far = lax.rem(s, 2), s // 2
    mate, cross = s + 1 - 2 * core, lax.rem(s + 2, seq)

    def rows_of(t):
        return pl.ds(pl.multiple_of(t * slot, slot), slot)

    def to_mate(n, part, pair, h):
        return remote(
            part.at[rows_of(h * 2 + 1 - core)],
            pair.at[h],
            r.rs_send.at[n, h],
            r.rs_recv.at[n, h],
            me,
            mate,
        )

    def to_cross(n, summed, got):
        return remote(summed, got, r.rs_send.at[n, 2], r.rs_recv.at[n, 2], me, cross)

    def sum_start(n, part, pair):
        to_mate(n, part, pair, 1 - far).start()
        to_mate(n, part, pair, far).start()

    def sum_across(n, part, pair, summed, got):
        to_mate(n, part, pair, 1 - far).wait_recv()
        summed[...] = (
            part[rows_of(cross), :].astype(F32) + pair[1 - far].astype(F32)
        ).astype(BF16)
        to_cross(n, summed, got).start()

    def sum_end(n, part, pair, summed, got):
        to_mate(n, part, pair, far).wait_recv()
        to_cross(n, summed, got).wait_recv()
        to_mate(n, part, pair, far).wait_send()
        to_mate(n, part, pair, 1 - far).wait_send()
        to_cross(n, summed, got).wait_send()
        return part[rows_of(s), :].astype(F32) + pair[far].astype(F32) + got[...].astype(F32)

    ln2_args = (0, r.ln2_part, r.pair_ln2)
    out_args = (1, r.out_part, r.pair_out)
    ln1_args = (2, r.part_ln1, r.pair_ln1)

    sum_start(*ln2_args)
    first_mix = min(c for c in range(len(parts)) if parts[c][0] == 2)
    for c in range(first_mix):
        send_side(c)
    r.rest[...] = jnp.zeros_like(r.rest)
    r.rest[:, 5 * width : 6 * width] = jnp.sum(r.grad_y[...], axis=0, keepdims=True)
    for t in range(seq):

        @pl.when(s == t)
        def _():
            for i in range(plan.img):
                a, b = plan.first[i * seq + t], plan.last[i * seq + t]
                at = i * plan.block
                r.rest[:, 6 * width + a : 6 * width + b] += r.pre_sums[:, at : at + b - a]

    r.gqkv[...] = jnp.zeros_like(r.gqkv)
    r.gvec32[...] = jnp.zeros_like(r.gvec32)
    sum_across(*ln2_args, r.sum_ln2, r.cross_ln2)
    sum_start(*out_args)
    grad_ln2 = sum_end(*ln2_args, r.sum_ln2, r.cross_ln2)
    grad_resid = r.grad_y[...] + norm_back(grad_ln2, r.normed2[...], r.rstd2[...], r.gain2[...])
    r.own_resid[...] = grad_resid.astype(BF16)
    r.resid32[...] = grad_resid

    def gather_resid(part, to, n):
        rows = r.all_resid.at[rows_of(part)]
        src = r.own_resid if n < 2 else rows
        return remote(src, rows, r.ag_send.at[n], r.ag_recv.at[n], me, to)

    gather_resid(s, cross, 0).start()
    gather_resid(s, mate, 1).start()
    r.all_resid[rows_of(s), :] = r.own_resid[...]
    r.rest[:, 2 * width : 3 * width] = jnp.sum(grad_resid, axis=0, keepdims=True)
    r.rest[:, 3 * width : 4 * width] = jnp.sum(grad_ln2 * r.normed2[...], axis=0, keepdims=True)
    r.rest[:, 4 * width : 5 * width] = jnp.sum(grad_ln2, axis=0, keepdims=True)
    service(0)
    gather_resid(cross, cross, 0).wait_recv()
    gather_resid(cross, mate, 2).start()
    sum_across(*out_args, r.sum_out, r.cross_out)
    gather_resid(mate, mate, 1).wait_recv()
    gather_resid(lax.rem(mate + 2, seq), mate, 2).wait_recv()

    for t in range(seq):
        rows = slice(t * slot, (t + 1) * slot)
        r.gm[rows, :] = dot_t(r.all_resid[rows, :], r.out_mine[...]).astype(BF16)

        @pl.when(s == t)
        def _():
            r.cols_resid[...] = r.all_resid[:, t * cols : (t + 1) * cols]

    tile = 2 * slot
    for h in range(heads):
        lanes = slice(h * HEAD_DIM, (h + 1) * HEAD_DIM)
        key, value = r.keys[h], r.values[h]
        grad_value = jnp.zeros((seq * slot, HEAD_DIM), F32)
        grad_key = jnp.zeros((seq * slot, HEAD_DIM), F32)
        query_sum = jnp.zeros((1, HEAD_DIM), F32)
        for at_row in range(0, seq * slot, tile):
            rows = slice(at_row, at_row + tile)
            query, gm = r.queries[h, rows, :], r.gm[rows, lanes]
            scores = dot_t(query, key) * scale
            scores = jnp.where(r.key_ok[...] > 0, scores, -1e30)
            probs = jnp.exp(scores - r.lse[h, rows, :])
            grad_value += dot_00(probs.astype(BF16), gm)
            delta = jnp.sum(
                gm.astype(F32) * r.mixed_mine[rows, lanes].astype(F32), axis=-1, keepdims=True
            )
            grad_scores = (probs * (dot_t(gm, value) - delta) * scale).astype(BF16)
            grad_query = jnp.dot(grad_scores, key, preferred_element_type=F32)
            grad_key += dot_00(grad_scores, query)
            r.gqkv[rows, lanes] = grad_query.astype(BF16)
            query_sum += jnp.sum(grad_query, axis=0, keepdims=True)
        r.qsum[:, lanes] = query_sum
        r.vsum[:, lanes] = jnp.sum(grad_value, axis=0, keepdims=True)
        for j, grad in ((1, grad_key), (2, grad_value)):
            to = j * cols + h * HEAD_DIM
            r.gqkv[:, to : to + HEAD_DIM] = grad.astype(BF16)
        if h % 2 == 1:
            service(1 + h // 2)

    for t in range(seq):
        rows = slice(t * slot, (t + 1) * slot)
        r.part_ln1[rows, :] = dot_t(r.gqkv[rows, :], r.mat_qkv[...]).astype(BF16)
    sum_start(*ln1_args)
    for m in range(0, width, LANES):
        grad = jnp.concatenate(
            [
                dot_00(r.ln1[:, m : m + LANES], r.gqkv[...])[:, : 3 * cols],
                dot_00(r.mixed[:, m : m + LANES], r.cols_resid[...]),
            ],
            axis=1,
        )
        r.gmix[m : m + LANES, :] = grad.astype(BF16)
    for c in range(first_mix, len(parts) - 2):
        send_side(c)
    sum_across(*ln1_args, r.sum_ln1, r.cross_ln1)
    out_terms = sum_end(*out_args, r.sum_out, r.cross_out)
    r.output[...] = ((r.base[...] + out_terms) * r.rowmask[...]).astype(BF16)
    service(3)
    grad_ln1 = sum_end(*ln1_args, r.sum_ln1, r.cross_ln1)
    normed1 = r.normed1[...]
    r.input_grad[...] = r.resid32[...] + norm_back(grad_ln1, normed1, r.rstd1[...], r.gain1[...])

    r.front[...] = jnp.zeros_like(r.front)
    r.front[:, :width] = jnp.sum(grad_ln1, axis=0, keepdims=True)
    r.rest[:, :width] = jnp.sum(grad_ln1 * normed1, axis=0, keepdims=True)
    for t in range(seq):

        @pl.when(s == t)
        def _():
            lanes = slice(width + t * cols, width + (t + 1) * cols)
            r.front[:, lanes] = r.vsum[...]
            r.rest[:, lanes] = r.qsum[...]

    own_front = 2 * width // plan.devices
    own_rest = plan.shard_vec - own_front
    for g in range(plan.devices):
        row = g // seq * 16 + g % seq
        r.gvec32[row : row + 1, :own_front] = r.front[:, g * own_front : (g + 1) * own_front]
        r.gvec32[row : row + 1, own_front : own_front + own_rest] = r.rest[
            :, g * own_rest : (g + 1) * own_rest
        ]
    r.gvec[...] = r.gvec32[...].astype(BF16)
    send_side(len(parts) - 2)
    send_side(len(parts) - 1)

    for c in range(4, first_mix + 1):
        service(c)
    service(first_mix + 1)
    r.got1[s] = r.cut1[s]
    for k in range(1, seq):
        exchange(0, r.cut1.at[lax.rem(s + k, seq)], r.got1.at[came_from(k)], k).wait()
    r.o1[...] = jnp.zeros_like(r.o1)
    for g in range(plan.devices):
        i, t = g // seq, g % seq
        a, b = plan.first[g], plan.last[g]
        r.o1[:, a:b] += r.got1[t, :sub, i * plan.block : i * plan.block + b - a].astype(F32)
    for c in range(first_mix + 2, len(parts) + 1):
        service(c)
    r.gotm[s] = r.cutm[s]
    r.ov[s] = r.cutv[s]
    for k in range(1, seq):
        exchange(1, r.cutm.at[lax.rem(s + k, seq)], r.gotm.at[came_from(k)], k).wait()
    for t in range(seq):
        for j in range(3):
            to = j * width + t * cols
            r.oq[:, to : to + cols] = r.gotm[t, :sub, j * cols : (j + 1) * cols].astype(F32)
        r.oo[:, t * cols : (t + 1) * cols] = r.gotm[t, :sub, 3 * cols : 4 * cols].astype(F32)
    for k in range(1, seq):
        exchange(2, r.cutv.at[s], r.ov.at[came_from(k)], k).wait()

    gather_resid(s, cross, 0).wait_send()
    gather_resid(s, mate, 1).wait_send()
    gather_resid(cross, mate, 2).wait_send()
    for c in range(len(parts)):
        for dest in range(line):
            to_side(c, dest).wait_send()

            @pl.when(dest > z)
            def _():
                to_up(c, dest).wait_send()

            @pl.when(dest < z)
            def _():
                to_down(c, dest).wait_send()


def backward(plan, slot, heads, args):
    vmem = pl.BlockSpec(memory_space=pltpu.VMEM)
    img, seq, width, line, cols = plan.img, plan.seq, plan.width, plan.line, plan.cols
    dma = pltpu.SemaphoreType.DMA
    shape = jax.ShapeDtypeStruct
    vec_pad = round_up(plan.shard_vec, LANES)
    parts = []
    step = 48
    for q, rows in ((0, plan.block), (1, plan.rows_pad), (2, plan.rows_pad)):
        parts += [(q, a, min(step, rows - a)) for a in range(0, rows, step)]
    parts.insert(len(parts) - 1, (3, 0, 16))
    n = len(parts)
    mix = 4 * cols
    inner = [
        (plan.block, width),
        (plan.rows_pad, plan.units),
        (plan.rows_pad, mix),
        (16, vec_pad),
    ]
    buffers = [pltpu.VMEM((line, *dims), BF16) for _ in range(4) for dims in inner]
    own16 = pltpu.VMEM((slot, width), BF16)
    all16 = pltpu.VMEM((seq * slot, width), BF16)
    sums = [pltpu.VMEM((2, slot, width), BF16), own16, own16]
    scratch = buffers + [
        pltpu.VMEM(inner[1], F32),
        pltpu.VMEM(inner[2], F32),
        pltpu.VMEM((seq, plan.sub_pad, plan.units), BF16),
        pltpu.VMEM((seq, plan.sub_pad, mix), BF16),
        pltpu.VMEM((seq, 16, vec_pad), BF16),
        pltpu.VMEM((seq, plan.sub_pad, plan.units), BF16),
        pltpu.VMEM((seq, plan.sub_pad, mix), BF16),
        pltpu.VMEM((img * plan.rows_pad, mix), BF16),
        pltpu.VMEM((img * 16, vec_pad), BF16),
        pltpu.VMEM((img * 16, vec_pad), F32),
        pltpu.VMEM((1, 2 * width), F32),
        pltpu.VMEM((1, plan.shard_vec * plan.devices - 2 * width), F32),
        pltpu.VMEM((1, cols), F32),
        pltpu.VMEM((1, cols), F32),
        *sums,
        *sums,
        *sums,
        own16,
        all16,
        pltpu.VMEM((slot, width), F32),
        pltpu.VMEM((seq * slot, cols), BF16),
        pltpu.VMEM((seq * slot, plan.qkv_cols), BF16),
        all16,
        pltpu.VMEM((seq * slot, cols), BF16),
        *[dma((n, line))] * 6,
        *[dma((3, seq))] * 2,
        *[dma((3, 3))] * 2,
        *[dma((3,))] * 2,
    ]
    return pl.pallas_call(
        functools.partial(backward_kernel, plan, parts, heads),
        out_shape=(
            shape((slot, width), BF16),
            shape((slot, width), F32),
            shape((plan.block, width), F32),
            shape((plan.sub, plan.hidden), F32),
            shape((plan.sub, 3 * width), F32),
            shape((plan.sub, width), F32),
            shape((seq, 16, vec_pad), BF16),
        ),
        in_specs=[vmem] * len(BackwardIn._fields),
        out_specs=(vmem,) * len(BackwardOut._fields),
        scratch_shapes=scratch,
        compiler_params=pltpu.CompilerParams(
            collective_id=1, has_side_effects=True, vmem_limit_bytes=VMEM_LIMIT
        ),
        name="backward",
    )(*[args[name] for name in BackwardIn._fields])


def ffn_kernel(
    ln2, fc1, bias, fc2, cot, ok, g2, g1, ln2_part, out_part, sums, grad_y, acc_ln2, acc_out
):
    step = pl.program_id(0)

    @pl.when(step == 0)
    def _():
        grad_y[...] = jnp.where(ok[...] > 0, cot[...].astype(F32), 0.0).astype(BF16)
        acc_ln2[...] = jnp.zeros_like(acc_ln2)
        acc_out[...] = jnp.zeros_like(acc_out)

    pre = jnp.dot(ln2[...], fc1[...], preferred_element_type=F32) + bias[...]
    value, slope = gelu_parts(pre)
    act = value.astype(BF16)
    grad_pre = dot_t(grad_y[...], fc2[...]) * slope
    grad_pre16 = grad_pre.astype(BF16)
    sums[...] = jnp.sum(grad_pre, axis=0, keepdims=True)
    acc_out[...] += jnp.dot(act, fc2[...], preferred_element_type=F32)
    acc_ln2[...] += dot_t(grad_pre16, fc1[...])
    g2[...] = dot_00(act, grad_y[...]).astype(BF16)
    g1[...] = dot_00(ln2[...], grad_pre16).astype(BF16)

    @pl.when(step == pl.num_programs(0) - 1)
    def _():
        ln2_part[...] = acc_ln2[...].astype(BF16)
        out_part[...] = acc_out[...].astype(BF16)


def feed_forward(ln2, fc1, bias, fc2, cot, ok):
    tokens, width = ln2.shape
    units = fc2.shape[0]
    by = 3 * LANES if units % (3 * LANES) == 0 else LANES
    shape = jax.ShapeDtypeStruct

    def whole(*dims):
        return pl.BlockSpec(dims, lambda i: (0, 0))

    columns = pl.BlockSpec((width, by), lambda i: (0, i))
    rows = pl.BlockSpec((by, width), lambda i: (i, 0))
    row = pl.BlockSpec((1, by), lambda i: (0, i))
    return pl.pallas_call(
        ffn_kernel,
        grid=(units // by,),
        out_shape=(
            shape((units, width), BF16),
            shape((width, units), BF16),
            shape((tokens, width), BF16),
            shape((tokens, width), BF16),
            shape((1, units), F32),
        ),
        in_specs=[
            whole(tokens, width),
            columns,
            row,
            rows,
            whole(tokens, width),
            whole(tokens, 1),
        ],
        out_specs=(rows, columns, whole(tokens, width), whole(tokens, width), row),
        scratch_shapes=[
            pltpu.VMEM((tokens, width), BF16),
            pltpu.VMEM((tokens, width), F32),
            pltpu.VMEM((tokens, width), F32),
        ],
        compiler_params=pltpu.CompilerParams(
            dimension_semantics=("arbitrary",), vmem_limit_bytes=VMEM_LIMIT
        ),
        name="feed_forward",
    )(ln2, fc1, bias, fc2, cot, ok)


def normalize(values):
    mean = jnp.mean(values, axis=-1, keepdims=True)
    centred = values - mean
    rstd = lax.rsqrt(jnp.mean(centred * centred, axis=-1, keepdims=True) + EPS)
    return (centred * rstd, rstd)


def gelu_parts(pre):
    inner = GELU_C * (pre + 0.044715 * pre * pre * pre)
    tanh_v = jnp.tanh(inner)
    value = 0.5 * pre * (1.0 + tanh_v)
    slope = 0.5 * (1.0 + tanh_v) + 0.5 * pre * (1.0 - tanh_v * tanh_v) * GELU_C * (
        1.0 + 3.0 * 0.044715 * pre * pre
    )
    return (value, slope)


def gather(value, axes):
    return lax.all_gather(value, axes, axis=0, tiled=True)


def scatter_sum(value, axes):
    return lax.psum_scatter(value, axes, scatter_dimension=0, tiled=True)


def weight_grad(left, right):
    return lax.dot_general(
        left, right, (((0,), (0,)), ((), ())), preferred_element_type=F32
    ).astype(BF16)


def batched(left, right, over_left, over_right):
    return lax.dot_general(
        left,
        right,
        (((over_left,), (over_right,)), ((0,), (0,))),
        preferred_element_type=F32,
    )


TILE = 2048


def pack(flat):
    padded = round_up(flat.shape[0], TILE)
    return jnp.pad(flat, (0, padded - flat.shape[0])).reshape(-1, LANES)


def unpack_blocks(packed, blocks, length):
    return packed.reshape(blocks, -1)[:, :length].reshape(-1)


def pack_blocks(flat, blocks):
    block = flat.reshape(blocks, -1)
    padded = round_up(block.shape[1], TILE)
    return jnp.pad(block, ((0, 0), (0, padded - block.shape[1]))).reshape(-1, LANES)


def shards_by_rows(tokens, counts, w_qkv, w_out, w_fc1, w_fc2, vectors, cotangent):
    f32 = jnp.float32
    bf16 = jnp.bfloat16
    width = tokens.shape[2]
    slot = tokens.shape[1]
    scale = HEAD_DIM ** (-0.5)
    position = lax.axis_index("seq")
    seq_count = lax.axis_size("seq")
    img_count = lax.axis_size("img")
    device_count = img_count * seq_count
    both = ("img", "seq")
    shard_qkv, shard_out, shard_fc1, shard_fc2, shard_vec = (
        w.shape[0] for w in (w_qkv, w_out, w_fc1, w_fc2, vectors)
    )
    hidden = shard_fc1 * device_count // width
    heads = HEADS // seq_count
    cols = width // seq_count
    units = hidden // seq_count
    rows = width // img_count
    pad_cols = round_up(3 * cols, LANES) - 3 * cols
    pad_units = round_up(units, LANES) - units
    to_quarter = [(c, (c % img_count) * seq_count + c // img_count) for c in range(device_count)]
    to_owner = [(b, a) for a, b in to_quarter]

    slice_counts = counts[0]
    key_valid = (jnp.arange(slot)[None, :] < slice_counts[:, None]).reshape(-1)
    row_valid = lax.dynamic_slice_in_dim(key_valid, position * slot, slot)
    rowmask = row_valid.astype(f32)[:, None]

    def mine(values):
        return lax.dynamic_slice_in_dim(values, position * slot, slot)

    shard_ov = shard_out + shard_vec
    local = gather(pack(jnp.concatenate([w_qkv, w_fc1, w_out, vectors])), "seq")
    local = local.reshape(seq_count, -1)
    x_all16 = gather(tokens[0], "seq")
    qkv_rows = local[:, :shard_qkv].reshape(rows, 3 * width)
    fc1_rows = local[:, shard_qkv : shard_qkv + shard_fc1].reshape(rows, hidden)
    ov_flat = local[:, shard_qkv + shard_fc1 : shard_qkv + shard_fc1 + shard_ov].reshape(-1)
    ov_cols = round_up(-(-ov_flat.shape[0] // rows), LANES)
    ov_part = jnp.pad(ov_flat, (0, rows * ov_cols - ov_flat.shape[0])).reshape(rows, ov_cols)
    qkv_part = jnp.concatenate(
        [
            lax.dynamic_slice_in_dim(qkv_rows, j * width + position * cols, cols, axis=1)
            for j in range(3)
        ]
        + [jnp.zeros((rows, pad_cols), bf16)],
        axis=1,
    )
    fc1_part = jnp.pad(
        lax.dynamic_slice_in_dim(fc1_rows, position * units, units, axis=1),
        ((0, 0), (0, pad_units)),
    )
    fc2_chunk = lax.ppermute(pack(w_fc2), both, to_quarter).reshape(-1)[:shard_fc2]
    fc2_part = jnp.pad(fc2_chunk.reshape(rows, units), ((0, 0), (0, pad_units)))
    weights = gather(jnp.concatenate([qkv_part, fc1_part, fc2_part, ov_part], axis=1), "img")
    end_qkv = 3 * cols + pad_cols
    end_fc1 = end_qkv + units + pad_units
    end_fc2 = end_fc1 + units + pad_units
    mat_qkv = weights[:, :end_qkv]
    mat_fc1 = weights[:, end_qkv:end_fc1]
    mat_fc2 = jnp.pad(
        weights[:, end_fc1 : end_fc1 + units].reshape(units, width), ((0, pad_units), (0, 0))
    )
    out_vec = weights[:, end_fc2:].reshape(img_count, -1)[:, : seq_count * shard_ov]
    cot_all = gather(cotangent[0], "seq")

    blocks_ov = out_vec.reshape(device_count, -1)
    mat_out = blocks_ov[:, :shard_out].reshape(width, width)
    vec = blocks_ov[:, shard_out : shard_out + shard_vec].reshape(-1).astype(f32)
    bias1, v_bias, gain1, q_bias, out_bias, gain2, bias2, fc2_bias = (
        vec[i * width : (i + 1) * width] for i in range(8)
    )
    fc1_bias = vec[8 * width : 8 * width + hidden]

    def my_cols(values):
        return lax.dynamic_slice_in_dim(values, position * cols, cols)

    fc1_bias_mine = jnp.pad(
        lax.dynamic_slice_in_dim(fc1_bias, position * units, units), (0, pad_units)
    )

    x = x_all16.astype(f32)
    normed1, _ = normalize(x)
    ln1 = (normed1 * gain1 + bias1).astype(bf16)
    qkv = jnp.dot(ln1, mat_qkv, preferred_element_type=f32)

    def by_head(values):
        return values.reshape(-1, heads, HEAD_DIM).transpose(1, 0, 2)

    def by_slot(values):
        return values.transpose(1, 0, 2).reshape(-1, cols)

    queries = by_head((qkv[:, :cols] + my_cols(q_bias)).astype(bf16))
    keys = by_head(qkv[:, cols : 2 * cols].astype(bf16))
    values = by_head((qkv[:, 2 * cols : 3 * cols] + my_cols(v_bias)).astype(bf16))
    scores = batched(queries, keys, 2, 2) * scale
    scores = jnp.where(key_valid[None, None, :], scores, -1e30)
    top = jnp.max(scores, axis=-1, keepdims=True)
    lse = top + jnp.log(jnp.sum(jnp.exp(scores - top), axis=-1, keepdims=True))
    probs = jnp.exp(scores - lse).astype(bf16)
    mixed_heads = batched(probs, values, 2, 1)
    mixed_mine = by_slot(mixed_heads).astype(bf16)
    mixed = lax.all_gather(mixed_mine, "seq", axis=0, tiled=True)
    mixed = (
        mixed.reshape(seq_count, -1, cols).transpose(1, 0, 2).reshape(-1, width)
    )
    resid = x + jnp.dot(mixed, mat_out, preferred_element_type=f32) + out_bias
    normed2, rstd2 = normalize(resid)
    ln2 = (normed2 * gain2 + bias2).astype(bf16)
    pre = jnp.dot(ln2, mat_fc1, preferred_element_type=f32) + fc1_bias_mine
    act_f, slope = gelu_parts(pre)
    act = act_f.astype(bf16)

    grad_y16 = jnp.where(key_valid[:, None], cot_all, jnp.zeros((), bf16))
    grad_pre = dot_t(grad_y16, mat_fc2) * slope
    grad_pre16 = grad_pre.astype(bf16)
    grad_ln2 = scatter_sum(dot_t(grad_pre16, mat_fc1).astype(bf16), "seq").astype(f32)
    grad_y = cotangent[0].astype(f32) * rowmask
    normed2_mine = mine(normed2)
    grad_resid = grad_y + norm_back(grad_ln2, normed2_mine, mine(rstd2), gain2)
    grad_resid16 = gather(grad_resid.astype(bf16), "seq")

    part_fc1 = weight_grad(ln2, grad_pre16)
    part_fc2 = pack_blocks(weight_grad(act, grad_y16)[:units].reshape(-1), img_count)
    out_terms = scatter_sum(
        jnp.dot(act, mat_fc2, preferred_element_type=f32).astype(bf16), "seq"
    ).astype(f32)
    output = ((mine(resid) + out_terms + fc2_bias) * rowmask).astype(bf16)

    out_mine = lax.dynamic_slice_in_dim(mat_out, position * cols, cols)
    gm = by_head(dot_t(grad_resid16, out_mine).astype(bf16))
    mixed_back = by_head(mixed_mine)
    delta = jnp.sum(gm.astype(f32) * mixed_back.astype(f32), axis=-1, keepdims=True)
    grad_values = by_slot(batched(probs, gm, 1, 1))
    dots = batched(gm, values, 2, 2)
    grad_scores = (jnp.exp(scores - lse) * (dots - delta) * scale).astype(bf16)
    grad_queries = by_slot(batched(grad_scores, keys, 2, 1))
    grad_keys = by_slot(batched(grad_scores, queries, 1, 1))
    grad_qkv16 = jnp.concatenate(
        [grad_queries.astype(bf16), grad_keys.astype(bf16), grad_values.astype(bf16)]
        + [jnp.zeros((seq_count * slot, pad_cols), bf16)],
        axis=1,
    )
    grad_ln1 = scatter_sum(dot_t(grad_qkv16, mat_qkv).astype(bf16), "seq").astype(f32)
    part_qkv = weight_grad(ln1, grad_qkv16)
    part_out = pack_blocks(weight_grad(mixed_mine, grad_resid16).reshape(-1), img_count)
    normed1_mine, rstd1_mine = normalize(tokens[0].astype(f32))
    input_grad = grad_resid + norm_back(grad_ln1, normed1_mine, rstd1_mine, gain1)

    def spread(part, full):
        return lax.dynamic_update_slice_in_dim(
            jnp.zeros((full,), f32), part, position * part.shape[0], 0
        )

    shard_front = 2 * width // device_count
    unused = shard_vec * device_count - 8 * width - hidden
    g_front = jnp.concatenate(
        [jnp.sum(grad_ln1, axis=0), spread(jnp.sum(grad_values, axis=0), width)]
    )
    g_rest = jnp.concatenate(
        [
            jnp.sum(grad_ln1 * normed1_mine, axis=0),
            spread(jnp.sum(grad_queries, axis=0), width),
            jnp.sum(grad_resid, axis=0),
            jnp.sum(grad_ln2 * normed2_mine, axis=0),
            jnp.sum(grad_ln2, axis=0),
            jnp.sum(grad_y, axis=0),
            spread(jnp.sum(grad_pre, axis=0)[:units], hidden),
            jnp.zeros((unused,), f32),
        ]
    )
    g_vec = jnp.concatenate(
        [g_front.reshape(device_count, -1), g_rest.reshape(device_count, -1)], axis=1
    )
    vec_pad = round_up(shard_vec, 4 * LANES)
    part_vec = jnp.pad(g_vec, ((0, 0), (0, vec_pad - shard_vec))).astype(bf16)

    parts = [
        part.reshape(img_count, -1, LANES)
        for part in (part_qkv, part_fc1, part_vec, part_fc2, part_out)
    ]
    sizes = [part.shape[1] for part in parts]
    summed = scatter_sum(jnp.concatenate(parts, axis=1).reshape(-1, LANES), "img")
    ends = [sum(sizes[: i + 1]) for i in range(5)]
    chunks = lax.ppermute(summed[ends[2] :], both, to_owner)
    grad_fc2 = chunks[: sizes[3]].reshape(-1)[:shard_fc2].astype(f32)
    grad_out = chunks[sizes[3] :].reshape(-1)[:shard_out].astype(f32)
    shared = gather(summed[: ends[2]], "seq").reshape(seq_count, ends[2], LANES)

    def own_block(packed, thirds, used, size):
        blocks = packed.reshape(seq_count, rows, -1)[:, :, : thirds * used]
        whole = blocks.reshape(seq_count, rows, thirds, used).transpose(1, 2, 0, 3)
        return lax.dynamic_slice_in_dim(whole.reshape(-1), position * size, size).astype(f32)

    grad_qkv = own_block(shared[:, : ends[0]], 3, cols, shard_qkv)
    grad_fc1 = own_block(shared[:, ends[0] : ends[1]], 1, units, shard_fc1)
    vec_sums = jnp.sum(shared[:, ends[1] :].astype(f32), axis=0).reshape(seq_count, vec_pad)
    vec_mine = lax.dynamic_slice_in_dim(vec_sums, position, 1).reshape(-1)
    return (
        output[None],
        input_grad[None],
        grad_qkv,
        grad_out,
        grad_fc1,
        grad_fc2,
        vec_mine[shard_front:shard_vec],
        vec_mine[:shard_front],
    )


def shards(tokens, counts, w_qkv, w_out, w_fc1, w_fc2, vectors, cotangent):
    width = tokens.shape[2]
    slot = tokens.shape[1]
    scale = HEAD_DIM ** (-0.5)
    position = lax.axis_index("seq")
    seq_count = lax.axis_size("seq")
    img_count = lax.axis_size("img")
    device_count = img_count * seq_count
    chunk = lax.axis_index("img") * seq_count + position
    shard_vec = vectors.shape[0]
    plan = Plan(img_count, seq_count, width, w_fc1.shape[0], shard_vec)
    hidden, cols, rows, units = plan.hidden, plan.cols, plan.rows, plan.units
    heads = HEADS // seq_count
    shard_fc = plan.shard_fc

    slice_counts = counts[0]
    key_valid = (jnp.arange(slot)[None, :] < slice_counts[:, None]).reshape(-1)
    row_valid = lax.dynamic_slice_in_dim(key_valid, position * slot, slot)
    rowmask = row_valid.astype(F32)[:, None]
    key_ok = key_valid.astype(F32)[None]

    shifts = sorted({g * shard_fc % width for g in range(device_count)})
    shift = lax.rem(chunk * shard_fc, width)
    fc2_flat = jnp.zeros((), BF16)
    for by in shifts:
        placed = jnp.pad(w_fc2, (by, plan.block * width - by - shard_fc))
        fc2_flat = jnp.where(shift == by, placed, fc2_flat)
    ov = jnp.pad(w_out.reshape(plan.sub, width), ((0, plan.sub_pad - plan.sub), (0, 0)))
    vec_in = jnp.pad(vectors[None], ((0, 15), (0, round_up(shard_vec, LANES) - shard_vec)))
    f = forward(
        plan,
        slot,
        heads,
        dict(
            qkv=w_qkv.reshape(plan.sub, 3 * width),
            fc1=w_fc1.reshape(plan.sub, hidden),
            fc2=fc2_flat.reshape(plan.block, width),
            ov=ov,
            vec_in=vec_in,
            x=tokens[0],
            cot=cotangent[0],
            key_ok=key_ok,
        ),
    )
    mat_fc1 = f.wf1.reshape(width, units)
    mat_fc2 = f.wf2.reshape(units, width)
    cot_all = f.cots.reshape(seq_count * slot, width)
    part_fc2, part_fc1, ln2_part, out_part, pre_sums = feed_forward(
        f.ln2, mat_fc1, f.fc1_bias, mat_fc2, cot_all, key_valid.astype(F32)[:, None]
    )
    output, input_grad, grad2, grad1, gradq, grado, gradv = backward(
        plan,
        slot,
        heads,
        dict(
            g2=part_fc2,
            g1=part_fc1,
            ln2_part=ln2_part,
            out_part=out_part,
            grad_y=cotangent[0].astype(F32) * rowmask,
            rowmask=rowmask,
            key_ok=key_ok,
            pre_sums=pre_sums,
            **{name: getattr(f, name) for name in BackwardIn._fields if name in ForwardOut._fields},
        ),
    )
    grad_fc2 = lax.dynamic_slice_in_dim(grad2.reshape(-1), shift, shard_fc)
    shard_front = 2 * width // device_count
    vec_sums = jnp.sum(gradv.astype(F32), axis=0)
    vec_mine = lax.dynamic_slice_in_dim(vec_sums, position, 1).reshape(-1)
    return (
        output[None],
        input_grad[None],
        gradq.reshape(-1),
        grado.reshape(-1),
        grad1.reshape(-1),
        grad_fc2,
        vec_mine[shard_front:shard_vec],
        vec_mine[:shard_front],
    )


def solution(mesh):
    def layer(*arrays):
        width = arrays[0].shape[2]
        whole_rows = (
            width % mesh.size == 0
            and mesh.shape["seq"] == 4
            and width // mesh.shape["img"] % 16 == 0
        )
        return (shards if whole_rows else shards_by_rows)(*arrays)

    return jax.shard_map(
        layer,
        mesh=mesh,
        in_specs=(
            P("img", "seq", None),
            P("img", None),
            P(("img", "seq")),
            P(("img", "seq")),
            P(("img", "seq")),
            P(("img", "seq")),
            P(("img", "seq")),
            P("img", "seq", None),
        ),
        out_specs=(
            P("img", "seq", None),
            P("img", "seq", None),
            P(("img", "seq")),
            P(("img", "seq")),
            P(("img", "seq")),
            P(("img", "seq")),
            P(("img", "seq")),
            P(("img", "seq")),
        ),
        check_vma=False,
    )
```

```python
import functools
from typing import NamedTuple

import jax
import jax.numpy as jnp
from jax import lax
from jax.experimental import pallas as pl
from jax.experimental.pallas import tpu as pltpu
from jax.sharding import PartitionSpec as P

HEADS = 16
HEAD_DIM = 72
EPS = 1e-06
GELU_C = 0.7978845608028654
LANES = 128
VMEM_LIMIT = 58 * 1024 * 1024
ACROSS = 1
PACE = ((1, 1, 1, 0), (1, 1, 1, 1), (1, 1, 1, 1), (1, 1), (0, 0, 0, 0))
F32 = jnp.float32
BF16 = jnp.bfloat16


def round_up(value, step):
    return -(-value // step) * step


class Plan:
    def __init__(self, img, seq, width, shard_fc, shard_vec):
        self.img, self.seq, self.width = img, seq, width
        self.line = img // 2
        self.devices = img * seq
        self.hidden = shard_fc * self.devices // width
        self.cols = width // seq
        self.rows = width // img
        self.rows_pad = round_up(self.rows, 16)
        self.sub = self.rows // seq
        self.sub_pad = round_up(self.sub, 16)
        self.shard_fc, self.shard_vec = shard_fc, shard_vec
        self.first = [g * shard_fc // width for g in range(self.devices)]
        self.last = [-(-(g + 1) * shard_fc // width) for g in range(self.devices)]
        self.block = round_up(max(b - a for a, b in zip(self.first, self.last)), 16)
        self.units = img * self.block
        self.qkv_cols = round_up(3 * self.cols, LANES)
        self.mix_cols = round_up(4 * self.cols, LANES)


def coords(plan):
    index = lax.axis_index("img")
    return index // 2, lax.rem(index, 2), lax.axis_index("seq")


def remote(src, dst, send, recv, img, seq):
    return pltpu.make_async_remote_copy(
        src_ref=src,
        dst_ref=dst,
        send_sem=send,
        recv_sem=recv,
        device_id=(img, seq),
        device_id_type=pl.DeviceIdType.MESH,
    )


def entry_barrier(plan, z, y, s):
    barrier = pltpu.get_barrier_semaphore()

    def greet(img, seq):
        pl.semaphore_signal(
            barrier, inc=1, device_id=(img, seq), device_id_type=pl.DeviceIdType.MESH
        )

    @pl.when(z > 0)
    def _():
        greet((z - 1) * 2 + y, s)

    @pl.when(z < plan.line - 1)
    def _():
        greet((z + 1) * 2 + y, s)

    greet(z * 2 + 1 - y, s)
    for k in range(1, plan.seq):
        greet(z * 2 + y, lax.rem(s + k, plan.seq))
    peers = plan.seq + jnp.minimum(z, 1) + jnp.minimum(plan.line - 1 - z, 1)
    pl.semaphore_wait(barrier, peers)


class ForwardIn(NamedTuple):
    qkv: jax.Array
    fc1: jax.Array
    fc2: jax.Array
    ov: jax.Array
    vec_in: jax.Array
    x: jax.Array
    cot: jax.Array
    key_ok: jax.Array


class ForwardOut(NamedTuple):
    wf1: jax.Array
    wf2: jax.Array
    cots: jax.Array
    mat_qkv: jax.Array
    queries: jax.Array
    keys: jax.Array
    values: jax.Array
    lse: jax.Array
    mixed_mine: jax.Array
    mixed: jax.Array
    ln1: jax.Array
    ln2: jax.Array
    base: jax.Array
    normed2: jax.Array
    rstd2: jax.Array
    normed1: jax.Array
    rstd1: jax.Array
    out_mine: jax.Array
    gain1: jax.Array
    gain2: jax.Array
    fc1_bias: jax.Array


class ForwardScratch(NamedTuple):
    cq: jax.Array
    cf: jax.Array
    rq: jax.Array
    rf: jax.Array
    mq: jax.Array
    mf: jax.Array
    wo: jax.Array
    vecs: jax.Array
    mat_out: jax.Array
    xs: jax.Array
    vec: jax.Array
    qkv_all: jax.Array
    others: jax.Array
    loc_sem: jax.Array
    up_sem: jax.Array
    down_sem: jax.Array
    side_sem: jax.Array
    got_sem: jax.Array
    seq_send: jax.Array
    seq_recv: jax.Array
    ag_send: jax.Array
    ag_recv: jax.Array


FORWARD = ForwardIn._fields + ForwardOut._fields + ForwardScratch._fields


class Refs:
    def __init__(self, names, refs):
        self.__dict__.update(zip(names, refs))


def forward_kernel(plan, items, heads, *refs):
    r = Refs(FORWARD, refs)
    z, y, s = coords(plan)
    me = z * 2 + y
    line, seq, sub, cols, width = plan.line, plan.seq, plan.sub, plan.cols, plan.width
    slot = r.x.shape[0]
    scale = HEAD_DIM ** (-0.5)
    entry_barrier(plan, z, y, s)
    sources = dict(vec=r.vec_in, ov=r.ov, fc2=r.fc2, wq=r.mq, wf1=r.mf)

    def source(q):
        name, a, n = items[q]
        return sources[name].at[pl.ds(a, n)]

    def target(q, piece):
        name, a, n = items[q]
        if name == "vec":
            return r.vecs.at[s, piece]
        if name == "ov":
            return r.wo.at[s, piece]
        if name == "wq":
            return r.mat_qkv.at[pl.ds(pl.multiple_of(piece * plan.rows_pad + a, 16), n)]
        return {"fc2": r.wf2, "wf1": r.wf1}[name].at[piece, pl.ds(a, n)]

    def hop(q, piece, src, way):
        img = {"up": me + 2, "down": me - 2, "side": z * 2 + 1 - y}[way]
        sem = {"up": r.up_sem, "down": r.down_sem, "side": r.side_sem}[way]
        return remote(src, target(q, piece), sem.at[q, piece], r.got_sem.at[q, piece], img, s)

    def own_copy(q):
        return pltpu.make_async_copy(source(q), target(q, me), r.loc_sem.at[q])

    def own(q):
        own_copy(q).start()
        hop(q, me, source(q), "side").start()

        @pl.when(z < line - 1)
        def _():
            hop(q, me, source(q), "up").start()

        @pl.when(z > 0)
        def _():
            hop(q, me, source(q), "down").start()

    def line_only(q, d):
        for yy in (y, 1 - y):
            low, high = (z - d) * 2 + yy, (z + d) * 2 + yy

            @pl.when(z - d >= 0)
            def _():
                hop(q, low, target(q, low), "up").wait_recv()

                @pl.when(z < line - 1)
                def _():
                    hop(q, low, target(q, low), "up").start()

            @pl.when(z + d < line)
            def _():
                hop(q, high, target(q, high), "down").wait_recv()

                @pl.when(z > 0)
                def _():
                    hop(q, high, target(q, high), "down").start()

    def from_side(q):
        other = z * 2 + 1 - y
        hop(q, other, target(q, other), "side").wait_recv()

        @pl.when(z < line - 1)
        def _():
            hop(q, other, target(q, other), "up").start()

        @pl.when(z > 0)
        def _():
            hop(q, other, target(q, other), "down").start()

    def pass_on(q, d):
        if q in across_first:
            if d == 1:
                from_side(q)
            line_only(q, d)
            return
        low = (z - d) * 2 + y
        high = (z + d) * 2 + y

        @pl.when(z - d >= 0)
        def _():
            hop(q, low, target(q, low), "side").wait_recv()
            hop(q, low, target(q, low), "side").start()

            @pl.when(z < line - 1)
            def _():
                hop(q, low, target(q, low), "up").start()

        @pl.when(z + d < line)
        def _():
            hop(q, high, target(q, high), "side").wait_recv()
            hop(q, high, target(q, high), "side").start()

            @pl.when(z > 0)
            def _():
                hop(q, high, target(q, high), "down").start()

    def wait_side(q):
        for zs in range(line):
            piece = zs * 2 + 1 - y
            if q not in across_first:
                hop(q, piece, target(q, piece), "side").wait_recv()
        own_copy(q).wait()

    def exchange(a, src, dst, k):
        peer = lax.rem(s + k, seq)
        return remote(src, dst, r.seq_send.at[a, k], r.seq_recv.at[a, k], me, peer)

    def came_from(k):
        return lax.rem(s + seq - k, seq)

    core = lax.rem(s, 2)
    mate, cross = s + 1 - 2 * core, lax.rem(s + 2, seq)

    def spread(n, own, part, owner, to, k):
        src = part(owner) if own is None else own
        return remote(src, part(owner), r.ag_send.at[n, k], r.ag_recv.at[n, k], me, to)

    def spread_start(n, own, part):
        spread(n, own, part, s, cross, 0).start()
        spread(n, own, part, s, mate, 1).start()

    def spread_on(n, own, part):
        spread(n, None, part, cross, cross, 0).wait_recv()
        spread(n, None, part, cross, mate, 2).start()

    def spread_end(n, own, part):
        spread(n, None, part, mate, mate, 1).wait_recv()
        spread(n, None, part, lax.rem(mate + 2, seq), mate, 2).wait_recv()

    def spread_sent(n, own, part):
        spread(n, own, part, s, cross, 0).wait_send()
        spread(n, own, part, s, mate, 1).wait_send()
        spread(n, None, part, cross, mate, 2).wait_send()

    def item(name):
        return [q for q in range(len(items)) if items[q][0] == name]

    def rows_of(t):
        return pl.ds(pl.multiple_of(t * slot, slot), slot)

    across_first = item("fc2")[-ACROSS:] if ACROSS else []

    xs = (0, r.x, lambda t: r.xs.at[rows_of(t)])
    cots = (1, r.cot, lambda t: r.cots.at[t])
    vecs = (2, None, lambda t: r.vecs.at[t])
    wos = (3, None, lambda t: r.wo.at[t])
    mixes = (4, r.mixed_mine, lambda t: r.others.at[t])
    own(item("vec")[0])
    own(item("ov")[0])
    early = item("fc2")[:1]
    for q in early:
        own(q)
    x_copy = pltpu.make_async_copy(r.x, r.xs.at[rows_of(s)], r.loc_sem.at[len(items)])
    cot_copy = pltpu.make_async_copy(r.cot, r.cots.at[s], r.loc_sem.at[len(items) + 1])
    r.cq[...] = jnp.zeros_like(r.cq)
    for t in range(seq):
        for j in range(3):
            at = j * width + t * cols
            r.cq[t, :sub, j * cols : (j + 1) * cols] = r.qkv[:, at : at + cols]
    for k in range(1, seq):
        exchange(0, r.cq.at[lax.rem(s + k, seq)], r.rq.at[s], k).start()
    x_copy.start()
    spread_start(*xs)
    r.cf[...] = jnp.zeros_like(r.cf)
    for g in range(plan.devices):
        i, t = g // seq, g % seq
        a, b = plan.first[g], plan.last[g]
        r.cf[t, :sub, i * plan.block : i * plan.block + b - a] = r.fc1[:, a:b]
    for k in range(1, seq):
        exchange(1, r.cf.at[lax.rem(s + k, seq)], r.rf.at[s], k).start()
    wq, late = item("wq"), [q for q in item("fc2") if q not in early]

    def merge(a, sent, got, merged):
        for k in range(1, seq):
            exchange(a, sent.at[lax.rem(s + k, seq)], got.at[came_from(k)], k).wait()
        got[s] = sent[s]
        for t in range(seq):
            merged[t * sub : (t + 1) * sub, :] = got[t, :sub, :]

    def all_on(queue, d):
        for q in queue:
            pass_on(q, d)

    all_on(item("vec"), 1)
    merge(0, r.cq, r.rq, r.mq)
    own(wq[0])
    all_on(item("ov"), 1)
    all_on(item("vec"), 2)
    spread_on(*xs)
    for q in late:
        own(q)
    merge(1, r.cf, r.rf, r.mf)
    all_on(wq, 1)
    for d in range(3, line):
        all_on(item("vec"), d)
    for d in range(2, line):
        all_on(item("ov"), d)
    wait_side(item("vec")[0])
    spread_start(*vecs)
    for q in item("wf1"):
        own(q)
    for d in range(2, line):
        all_on(wq, d)
    all_on(early, 1)
    spread_on(*vecs)
    wait_side(item("ov")[0])
    spread_start(*wos)
    cot_copy.start()
    spread_start(*cots)
    all_on(late, 1)
    for d in range(2, line):
        all_on(early, d)

    rest = [(q, 1) for q in item("wf1")]
    rest += [(q, d) for d in range(2, line) for q in late + item("wf1")]

    def service(n=1):
        for _ in range(n):
            if rest:
                pass_on(*rest.pop(0))

    x_copy.wait()
    spread_end(*xs)
    spread_end(*vecs)
    count = plan.shard_vec
    for g in range(plan.devices):
        i, t = g // seq, g % seq
        r.vec[:, g * count : (g + 1) * count] = r.vecs[t, i, :1, :count].astype(F32)
    bias1, v_bias, gain1, q_bias, out_bias, gain2, bias2, fc2_bias = (
        r.vec[:, n * width : (n + 1) * width] for n in range(8)
    )
    r.gain1[...] = gain1
    r.gain2[...] = gain2
    r.fc1_bias[...] = jnp.zeros_like(r.fc1_bias)
    for t in range(seq):

        @pl.when(s == t)
        def _():
            for i in range(plan.img):
                a, b = plan.first[i * seq + t], plan.last[i * seq + t]
                to = i * plan.block
                r.fc1_bias[:, to : to + b - a] = r.vec[:, 8 * width + a : 8 * width + b]

    for t in range(seq):
        rows = slice(t * slot, (t + 1) * slot)
        normed, rstd = normalize(r.xs[rows, :].astype(F32))
        r.ln1[rows, :] = (normed * gain1 + bias1).astype(BF16)

        @pl.when(s == t)
        def _():
            r.normed1[...] = normed
            r.rstd1[...] = rstd

        service(PACE[0][t])

    for q in item("wq"):
        wait_side(q)
    for t in range(seq):
        rows = slice(t * slot, (t + 1) * slot)
        r.qkv_all[rows, :] = jnp.dot(
            r.ln1[rows, :], r.mat_qkv[...], preferred_element_type=F32
        )
        service(PACE[1][t])
    for t in range(seq):

        @pl.when(s == t)
        def _():
            lanes = slice(t * cols, (t + 1) * cols)
            r.qkv_all[:, :cols] += q_bias[:, lanes]
            r.qkv_all[:, 2 * cols : 3 * cols] += v_bias[:, lanes]

    for h in range(heads):
        for j, out in enumerate((r.queries, r.keys, r.values)):
            at = j * cols + h * HEAD_DIM
            out[h] = r.qkv_all[:, at : at + HEAD_DIM].astype(BF16)
    tile = 2 * slot
    for h in range(heads):
        lanes = slice(h * HEAD_DIM, (h + 1) * HEAD_DIM)
        key, value = r.keys[h], r.values[h]
        for at in range(0, seq * slot, tile):
            rows = slice(at, at + tile)
            scores = dot_t(r.queries[h, rows, :], key) * scale
            scores = jnp.where(r.key_ok[...] > 0, scores, -1e30)
            top = jnp.max(scores, axis=-1, keepdims=True)
            terms = jnp.exp(scores - top)
            total = jnp.sum(terms, axis=-1, keepdims=True)
            r.lse[h, rows, :] = top + jnp.log(total)
            probs = (terms * (1.0 / total)).astype(BF16)
            r.mixed_mine[rows, lanes] = jnp.dot(
                probs, value, preferred_element_type=F32
            ).astype(BF16)
        service(PACE[2][h])
        if h == 0:
            spread_on(*wos)
        if h == heads - 1:
            spread_on(*cots)

    spread_start(*mixes)
    r.others[s] = r.mixed_mine[...]
    spread_end(*wos)
    for g in range(plan.devices):
        i, t = g // seq, g % seq
        r.mat_out[g * sub : (g + 1) * sub, :] = r.wo[t, i, :sub, :]
    for t in range(seq):

        @pl.when(s == t)
        def _():
            r.out_mine[...] = r.mat_out[t * cols : (t + 1) * cols, :]

    service(PACE[3][0])
    spread_on(*mixes)
    service(PACE[3][1])
    spread_end(*mixes)
    for t in range(seq):
        r.mixed[:, t * cols : (t + 1) * cols] = r.others[t]
    for t in range(seq):
        rows = slice(t * slot, (t + 1) * slot)
        resid = (
            r.xs[rows, :].astype(F32)
            + jnp.dot(r.mixed[rows, :], r.mat_out[...], preferred_element_type=F32)
            + out_bias
        )
        normed, rstd = normalize(resid)
        r.ln2[rows, :] = (normed * gain2 + bias2).astype(BF16)

        @pl.when(s == t)
        def _():
            r.base[...] = resid + fc2_bias
            r.normed2[...] = normed
            r.rstd2[...] = rstd

        service(PACE[4][t])
    service(len(rest))
    for q in item("fc2") + item("wf1"):
        wait_side(q)

    def wait_sends(q, piece, zs):
        @pl.when(jnp.logical_and(z < line - 1, zs <= z))
        def _():
            hop(q, piece, target(q, piece), "up").wait_send()

        @pl.when(jnp.logical_and(z > 0, zs >= z))
        def _():
            hop(q, piece, target(q, piece), "down").wait_send()

    for q in range(len(items)):
        if q in across_first:
            hop(q, me, target(q, me), "side").wait_send()
        for zs in range(line):
            wait_sends(q, zs * 2 + y, zs)
            if q in across_first:
                wait_sends(q, zs * 2 + 1 - y, zs)
            else:
                hop(q, zs * 2 + y, target(q, zs * 2 + y), "side").wait_send()

    cot_copy.wait()
    spread_end(*cots)
    for each in (xs, cots, vecs, wos, mixes):
        spread_sent(*each)


def forward(plan, slot, heads, args):
    any_spec = pl.BlockSpec(memory_space=pl.ANY)
    vmem = pl.BlockSpec(memory_space=pltpu.VMEM)
    img, seq, width, cols = plan.img, plan.seq, plan.width, plan.cols
    tokens = seq * slot
    dma = pltpu.SemaphoreType.DMA
    shape = jax.ShapeDtypeStruct
    items = [("vec", 0, 16), ("ov", 0, plan.sub_pad)]
    step = 48
    for name, rows, by in (
        ("fc2", plan.block, step),
        ("wq", plan.rows_pad, plan.rows_pad),
        ("wf1", plan.rows_pad, step),
    ):
        items += [(name, a, min(by, rows - a)) for a in range(0, rows, by)]
    n = len(items)
    head = shape((heads, tokens, HEAD_DIM), BF16)
    all16 = shape((tokens, width), BF16)
    own32 = shape((slot, width), F32)
    column = shape((slot, 1), F32)
    row = shape((1, width), F32)
    outs = (
        shape((img, plan.rows_pad, plan.units), BF16),
        shape((img, plan.block, width), BF16),
        shape((seq, slot, width), BF16),
        shape((img * plan.rows_pad, plan.qkv_cols), BF16),
        head,
        head,
        head,
        shape((heads, tokens, 1), F32),
        shape((tokens, cols), BF16),
        all16,
        all16,
        all16,
        own32,
        own32,
        column,
        own32,
        column,
        shape((cols, width), BF16),
        row,
        row,
        shape((1, plan.units), F32),
    )
    result = pl.pallas_call(
        functools.partial(forward_kernel, plan, items, heads),
        out_shape=outs,
        in_specs=[vmem, vmem, any_spec, any_spec, vmem, vmem, any_spec, vmem],
        out_specs=(any_spec,) * 3 + (vmem,) * (len(outs) - 3),
        scratch_shapes=[
            pltpu.VMEM((seq, plan.sub_pad, plan.qkv_cols), BF16),
            pltpu.VMEM((seq, plan.sub_pad, plan.units), BF16),
            pltpu.VMEM((seq, plan.sub_pad, plan.qkv_cols), BF16),
            pltpu.VMEM((seq, plan.sub_pad, plan.units), BF16),
            pltpu.VMEM((plan.rows_pad, plan.qkv_cols), BF16),
            pltpu.VMEM((plan.rows_pad, plan.units), BF16),
            pltpu.VMEM((seq, img, plan.sub_pad, width), BF16),
            pltpu.VMEM((seq, img, *args["vec_in"].shape), BF16),
            pltpu.VMEM((width, width), BF16),
            pltpu.VMEM((tokens, width), BF16),
            pltpu.VMEM((1, plan.shard_vec * plan.devices), F32),
            pltpu.VMEM((tokens, plan.qkv_cols), F32),
            pltpu.VMEM((seq, tokens, cols), BF16),
            dma((n + 2,)),
            *[dma((n, img))] * 4,
            *[dma((2, seq))] * 2,
            *[dma((5, 3))] * 2,
        ],
        compiler_params=pltpu.CompilerParams(
            collective_id=0, has_side_effects=True, vmem_limit_bytes=VMEM_LIMIT
        ),
        name="forward",
    )(*[args[name] for name in ForwardIn._fields])
    return Refs(ForwardOut._fields, result)


def dot_00(left, right):
    return lax.dot_general(left, right, (((0,), (0,)), ((), ())), preferred_element_type=F32)


def dot_t(left, right):
    return lax.dot_general(left, right, (((1,), (1,)), ((), ())), preferred_element_type=F32)


def norm_back(grad_in, normed, rstd, gain):
    scaled = grad_in * gain
    return rstd * (
        scaled
        - jnp.mean(scaled, axis=-1, keepdims=True)
        - normed * jnp.mean(scaled * normed, axis=-1, keepdims=True)
    )


class BackwardIn(NamedTuple):
    g2: jax.Array
    g1: jax.Array
    ln2_part: jax.Array
    out_part: jax.Array
    normed2: jax.Array
    rstd2: jax.Array
    gain2: jax.Array
    grad_y: jax.Array
    base: jax.Array
    rowmask: jax.Array
    queries: jax.Array
    keys: jax.Array
    values: jax.Array
    lse: jax.Array
    key_ok: jax.Array
    mixed_mine: jax.Array
    mixed: jax.Array
    ln1: jax.Array
    mat_qkv: jax.Array
    out_mine: jax.Array
    normed1: jax.Array
    rstd1: jax.Array
    gain1: jax.Array
    pre_sums: jax.Array


class BackwardOut(NamedTuple):
    output: jax.Array
    input_grad: jax.Array
    o2: jax.Array
    o1: jax.Array
    oq: jax.Array
    oo: jax.Array
    ov: jax.Array


class BackwardScratch(NamedTuple):
    side2: jax.Array
    side1: jax.Array
    sidem: jax.Array
    sidev: jax.Array
    low2: jax.Array
    low1: jax.Array
    lowm: jax.Array
    lowv: jax.Array
    high2: jax.Array
    high1: jax.Array
    highm: jax.Array
    highv: jax.Array
    acc2: jax.Array
    acc1: jax.Array
    accm: jax.Array
    accv: jax.Array
    fin1: jax.Array
    finm: jax.Array
    cut1: jax.Array
    cutm: jax.Array
    cutv: jax.Array
    got1: jax.Array
    gotm: jax.Array
    gmix: jax.Array
    gvec: jax.Array
    gvec32: jax.Array
    front: jax.Array
    rest: jax.Array
    qsum: jax.Array
    vsum: jax.Array
    pair_ln2: jax.Array
    cross_ln2: jax.Array
    sum_ln2: jax.Array
    pair_out: jax.Array
    cross_out: jax.Array
    sum_out: jax.Array
    pair_ln1: jax.Array
    cross_ln1: jax.Array
    sum_ln1: jax.Array
    own_resid: jax.Array
    all_resid: jax.Array
    resid32: jax.Array
    gm: jax.Array
    gqkv: jax.Array
    part_ln1: jax.Array
    cols_resid: jax.Array
    side_send: jax.Array
    side_recv: jax.Array
    low_send: jax.Array
    low_recv: jax.Array
    high_send: jax.Array
    high_recv: jax.Array
    seq_send: jax.Array
    seq_recv: jax.Array
    rs_send: jax.Array
    rs_recv: jax.Array
    ag_send: jax.Array
    ag_recv: jax.Array


BACKWARD = BackwardIn._fields + BackwardOut._fields + BackwardScratch._fields


def backward_kernel(plan, parts, heads, *refs):
    r = Refs(BACKWARD, refs)
    z, y, s = coords(plan)
    me = z * 2 + y
    line, seq, sub, cols = plan.line, plan.seq, plan.sub, plan.cols
    width = plan.width
    slot = r.output.shape[0]
    scale = HEAD_DIM ** (-0.5)
    entry_barrier(plan, z, y, s)
    grads = [r.g2, r.g1, r.gmix, r.gvec]
    tall = [plan.block, plan.rows_pad, plan.rows_pad, 16]
    sides = [r.side2, r.side1, r.sidem, r.sidev]
    lows = [r.low2, r.low1, r.lowm, r.lowv]
    highs = [r.high2, r.high1, r.highm, r.highv]
    accs = [r.acc2, r.acc1, r.accm, r.accv]

    def at(c):
        q, a, n = parts[c]
        return q, pl.ds(a, n)

    def piece(c, img):
        q, a, n = parts[c]
        return grads[q].at[pl.ds(pl.multiple_of(img * tall[q] + a, 16), n)]

    def to_side(c, dest):
        q, w = at(c)
        return remote(
            piece(c, dest * 2 + 1 - y),
            sides[q].at[dest, w],
            r.side_send.at[c, dest],
            r.side_recv.at[c, dest],
            z * 2 + 1 - y,
            s,
        )

    def to_up(c, dest):
        q, w = at(c)
        return remote(
            accs[q].at[dest, w],
            lows[q].at[dest, w],
            r.low_send.at[c, dest],
            r.low_recv.at[c, dest],
            me + 2,
            s,
        )

    def to_down(c, dest):
        q, w = at(c)
        return remote(
            accs[q].at[dest, w],
            highs[q].at[dest, w],
            r.high_send.at[c, dest],
            r.high_recv.at[c, dest],
            me - 2,
            s,
        )

    def send_side(c):
        for d in range(line - 1, -1, -1):

            @pl.when(z + d < line)
            def _():
                to_side(c, z + d).start()

            if d:

                @pl.when(z - d >= 0)
                def _():
                    to_side(c, z - d).start()

    def both(c, dest):
        q, w = at(c)
        to_side(c, dest).wait_recv()
        return piece(c, dest * 2 + y)[...].astype(F32) + sides[q][dest, w, :].astype(F32)

    def pass_on(c):
        q, w = at(c)
        for d in range(line - 1, 0, -1):

            @pl.when(z + d < line)
            def _():
                dest = z + d
                total = both(c, dest)

                @pl.when(z > 0)
                def _():
                    to_up(c, dest).wait_recv()
                    accs[q][dest, w, :] = (total + lows[q][dest, w, :].astype(F32)).astype(BF16)

                @pl.when(z == 0)
                def _():
                    accs[q][dest, w, :] = total.astype(BF16)

                to_up(c, dest).start()

            @pl.when(z - d >= 0)
            def _():
                dest = z - d
                total = both(c, dest)

                @pl.when(z < line - 1)
                def _():
                    to_down(c, dest).wait_recv()
                    accs[q][dest, w, :] = (total + highs[q][dest, w, :].astype(F32)).astype(BF16)

                @pl.when(z == line - 1)
                def _():
                    accs[q][dest, w, :] = total.astype(BF16)

                to_down(c, dest).start()

    outs = [r.o2, r.fin1, r.finm, None]

    def finish(c):
        q, w = at(c)
        total = both(c, z)

        def store(value):
            if q == 3:
                r.cutv[s, w, :] = value.astype(BF16)
            else:
                outs[q][w, :] = value

        @pl.when(z == 0)
        def _():
            to_down(c, z).wait_recv()
            store(total + highs[q][z, w, :].astype(F32))

        @pl.when(z == line - 1)
        def _():
            to_up(c, z).wait_recv()
            store(total + lows[q][z, w, :].astype(F32))

        @pl.when(jnp.logical_and(z > 0, z < line - 1))
        def _():
            to_down(c, z).wait_recv()
            to_up(c, z).wait_recv()
            store(total + lows[q][z, w, :].astype(F32) + highs[q][z, w, :].astype(F32))

    def exchange(a, src, dst, k):
        peer = lax.rem(s + k, seq)
        return remote(src, dst, r.seq_send.at[a, k], r.seq_recv.at[a, k], me, peer)

    def came_from(k):
        return lax.rem(s + seq - k, seq)

    ends = {max(c for c in range(len(parts)) if parts[c][0] == q): q for q in (1, 2, 3)}

    def after(c):
        if c not in ends:
            return
        q = ends[c]
        if q == 3:
            for k in range(1, seq):
                exchange(2, r.cutv.at[s], r.ov.at[s], k).start()
            return
        fin, cut, got = ((r.fin1, r.cut1, r.got1), (r.finm, r.cutm, r.gotm))[q - 1]
        for t in range(seq):
            cut[t, :sub, :] = fin[t * sub : (t + 1) * sub, :].astype(BF16)
        for k in range(1, seq):
            exchange(q - 1, cut.at[lax.rem(s + k, seq)], got.at[s], k).start()

    def service(c):
        if c < len(parts):
            pass_on(c)
        if c >= 1:
            finish(c - 1)
            after(c - 1)

    core, far = lax.rem(s, 2), s // 2
    mate, cross = s + 1 - 2 * core, lax.rem(s + 2, seq)

    def rows_of(t):
        return pl.ds(pl.multiple_of(t * slot, slot), slot)

    def to_mate(n, part, pair, h):
        return remote(
            part.at[rows_of(h * 2 + 1 - core)],
            pair.at[h],
            r.rs_send.at[n, h],
            r.rs_recv.at[n, h],
            me,
            mate,
        )

    def to_cross(n, summed, got):
        return remote(summed, got, r.rs_send.at[n, 2], r.rs_recv.at[n, 2], me, cross)

    def sum_start(n, part, pair):
        to_mate(n, part, pair, 1 - far).start()
        to_mate(n, part, pair, far).start()

    def sum_across(n, part, pair, summed, got):
        to_mate(n, part, pair, 1 - far).wait_recv()
        summed[...] = (
            part[rows_of(cross), :].astype(F32) + pair[1 - far].astype(F32)
        ).astype(BF16)
        to_cross(n, summed, got).start()

    def sum_end(n, part, pair, summed, got):
        to_mate(n, part, pair, far).wait_recv()
        to_cross(n, summed, got).wait_recv()
        to_mate(n, part, pair, far).wait_send()
        to_mate(n, part, pair, 1 - far).wait_send()
        to_cross(n, summed, got).wait_send()
        return part[rows_of(s), :].astype(F32) + pair[far].astype(F32) + got[...].astype(F32)

    ln2_args = (0, r.ln2_part, r.pair_ln2)
    out_args = (1, r.out_part, r.pair_out)
    ln1_args = (2, r.part_ln1, r.pair_ln1)

    sum_start(*ln2_args)
    first_mix = min(c for c in range(len(parts)) if parts[c][0] == 2)
    for c in range(first_mix):
        send_side(c)
    r.rest[...] = jnp.zeros_like(r.rest)
    r.rest[:, 5 * width : 6 * width] = jnp.sum(r.grad_y[...], axis=0, keepdims=True)
    for t in range(seq):

        @pl.when(s == t)
        def _():
            for i in range(plan.img):
                a, b = plan.first[i * seq + t], plan.last[i * seq + t]
                at = i * plan.block
                r.rest[:, 6 * width + a : 6 * width + b] += r.pre_sums[:, at : at + b - a]

    r.gqkv[...] = jnp.zeros_like(r.gqkv)
    r.gvec32[...] = jnp.zeros_like(r.gvec32)
    sum_across(*ln2_args, r.sum_ln2, r.cross_ln2)
    sum_start(*out_args)
    grad_ln2 = sum_end(*ln2_args, r.sum_ln2, r.cross_ln2)
    grad_resid = r.grad_y[...] + norm_back(grad_ln2, r.normed2[...], r.rstd2[...], r.gain2[...])
    r.own_resid[...] = grad_resid.astype(BF16)
    r.resid32[...] = grad_resid

    def gather_resid(part, to, n):
        rows = r.all_resid.at[rows_of(part)]
        src = r.own_resid if n < 2 else rows
        return remote(src, rows, r.ag_send.at[n], r.ag_recv.at[n], me, to)

    gather_resid(s, cross, 0).start()
    gather_resid(s, mate, 1).start()
    r.all_resid[rows_of(s), :] = r.own_resid[...]
    r.rest[:, 2 * width : 3 * width] = jnp.sum(grad_resid, axis=0, keepdims=True)
    r.rest[:, 3 * width : 4 * width] = jnp.sum(grad_ln2 * r.normed2[...], axis=0, keepdims=True)
    r.rest[:, 4 * width : 5 * width] = jnp.sum(grad_ln2, axis=0, keepdims=True)
    service(0)
    gather_resid(cross, cross, 0).wait_recv()
    gather_resid(cross, mate, 2).start()
    sum_across(*out_args, r.sum_out, r.cross_out)
    gather_resid(mate, mate, 1).wait_recv()
    gather_resid(lax.rem(mate + 2, seq), mate, 2).wait_recv()

    for t in range(seq):
        rows = slice(t * slot, (t + 1) * slot)
        r.gm[rows, :] = dot_t(r.all_resid[rows, :], r.out_mine[...]).astype(BF16)

        @pl.when(s == t)
        def _():
            r.cols_resid[...] = r.all_resid[:, t * cols : (t + 1) * cols]

    tile = 2 * slot
    for h in range(heads):
        lanes = slice(h * HEAD_DIM, (h + 1) * HEAD_DIM)
        key, value = r.keys[h], r.values[h]
        grad_value = jnp.zeros((seq * slot, HEAD_DIM), F32)
        grad_key = jnp.zeros((seq * slot, HEAD_DIM), F32)
        query_sum = jnp.zeros((1, HEAD_DIM), F32)
        for at_row in range(0, seq * slot, tile):
            rows = slice(at_row, at_row + tile)
            query, gm = r.queries[h, rows, :], r.gm[rows, lanes]
            scores = dot_t(query, key) * scale
            scores = jnp.where(r.key_ok[...] > 0, scores, -1e30)
            probs = jnp.exp(scores - r.lse[h, rows, :])
            grad_value += dot_00(probs.astype(BF16), gm)
            delta = jnp.sum(
                gm.astype(F32) * r.mixed_mine[rows, lanes].astype(F32), axis=-1, keepdims=True
            )
            grad_scores = (probs * (dot_t(gm, value) - delta) * scale).astype(BF16)
            grad_query = jnp.dot(grad_scores, key, preferred_element_type=F32)
            grad_key += dot_00(grad_scores, query)
            r.gqkv[rows, lanes] = grad_query.astype(BF16)
            query_sum += jnp.sum(grad_query, axis=0, keepdims=True)
        r.qsum[:, lanes] = query_sum
        r.vsum[:, lanes] = jnp.sum(grad_value, axis=0, keepdims=True)
        for j, grad in ((1, grad_key), (2, grad_value)):
            to = j * cols + h * HEAD_DIM
            r.gqkv[:, to : to + HEAD_DIM] = grad.astype(BF16)
        if h % 2 == 1:
            service(1 + h // 2)

    for t in range(seq):
        rows = slice(t * slot, (t + 1) * slot)
        r.part_ln1[rows, :] = dot_t(r.gqkv[rows, :], r.mat_qkv[...]).astype(BF16)
    sum_start(*ln1_args)
    for m in range(0, width, LANES):
        grad = jnp.concatenate(
            [
                dot_00(r.ln1[:, m : m + LANES], r.gqkv[...])[:, : 3 * cols],
                dot_00(r.mixed[:, m : m + LANES], r.cols_resid[...]),
            ],
            axis=1,
        )
        r.gmix[m : m + LANES, :] = grad.astype(BF16)
    for c in range(first_mix, len(parts) - 2):
        send_side(c)
    sum_across(*ln1_args, r.sum_ln1, r.cross_ln1)
    out_terms = sum_end(*out_args, r.sum_out, r.cross_out)
    r.output[...] = ((r.base[...] + out_terms) * r.rowmask[...]).astype(BF16)
    service(3)
    grad_ln1 = sum_end(*ln1_args, r.sum_ln1, r.cross_ln1)
    normed1 = r.normed1[...]
    r.input_grad[...] = r.resid32[...] + norm_back(grad_ln1, normed1, r.rstd1[...], r.gain1[...])

    r.front[...] = jnp.zeros_like(r.front)
    r.front[:, :width] = jnp.sum(grad_ln1, axis=0, keepdims=True)
    r.rest[:, :width] = jnp.sum(grad_ln1 * normed1, axis=0, keepdims=True)
    for t in range(seq):

        @pl.when(s == t)
        def _():
            lanes = slice(width + t * cols, width + (t + 1) * cols)
            r.front[:, lanes] = r.vsum[...]
            r.rest[:, lanes] = r.qsum[...]

    own_front = 2 * width // plan.devices
    own_rest = plan.shard_vec - own_front
    for g in range(plan.devices):
        row = g // seq * 16 + g % seq
        r.gvec32[row : row + 1, :own_front] = r.front[:, g * own_front : (g + 1) * own_front]
        r.gvec32[row : row + 1, own_front : own_front + own_rest] = r.rest[
            :, g * own_rest : (g + 1) * own_rest
        ]
    r.gvec[...] = r.gvec32[...].astype(BF16)
    send_side(len(parts) - 2)
    send_side(len(parts) - 1)

    for c in range(4, first_mix + 1):
        service(c)
    service(first_mix + 1)
    r.got1[s] = r.cut1[s]
    for k in range(1, seq):
        exchange(0, r.cut1.at[lax.rem(s + k, seq)], r.got1.at[came_from(k)], k).wait()
    r.o1[...] = jnp.zeros_like(r.o1)
    for g in range(plan.devices):
        i, t = g // seq, g % seq
        a, b = plan.first[g], plan.last[g]
        r.o1[:, a:b] += r.got1[t, :sub, i * plan.block : i * plan.block + b - a].astype(F32)
    for c in range(first_mix + 2, len(parts) + 1):
        service(c)
    r.gotm[s] = r.cutm[s]
    r.ov[s] = r.cutv[s]
    for k in range(1, seq):
        exchange(1, r.cutm.at[lax.rem(s + k, seq)], r.gotm.at[came_from(k)], k).wait()
    for t in range(seq):
        for j in range(3):
            to = j * width + t * cols
            r.oq[:, to : to + cols] = r.gotm[t, :sub, j * cols : (j + 1) * cols].astype(F32)
        r.oo[:, t * cols : (t + 1) * cols] = r.gotm[t, :sub, 3 * cols : 4 * cols].astype(F32)
    for k in range(1, seq):
        exchange(2, r.cutv.at[s], r.ov.at[came_from(k)], k).wait()

    gather_resid(s, cross, 0).wait_send()
    gather_resid(s, mate, 1).wait_send()
    gather_resid(cross, mate, 2).wait_send()
    for c in range(len(parts)):
        for dest in range(line):
            to_side(c, dest).wait_send()

            @pl.when(dest > z)
            def _():
                to_up(c, dest).wait_send()

            @pl.when(dest < z)
            def _():
                to_down(c, dest).wait_send()


def backward(plan, slot, heads, args):
    vmem = pl.BlockSpec(memory_space=pltpu.VMEM)
    img, seq, width, line, cols = plan.img, plan.seq, plan.width, plan.line, plan.cols
    dma = pltpu.SemaphoreType.DMA
    shape = jax.ShapeDtypeStruct
    vec_pad = round_up(plan.shard_vec, LANES)
    parts = []
    step = 80
    for q, rows in ((0, plan.block), (1, plan.rows_pad), (2, plan.rows_pad)):
        parts += [(q, a, min(step, rows - a)) for a in range(0, rows, step)]
    parts.insert(len(parts) - 1, (3, 0, 16))
    n = len(parts)
    mix = 4 * cols
    inner = [
        (plan.block, width),
        (plan.rows_pad, plan.units),
        (plan.rows_pad, mix),
        (16, vec_pad),
    ]
    buffers = [pltpu.VMEM((line, *dims), BF16) for _ in range(4) for dims in inner]
    own16 = pltpu.VMEM((slot, width), BF16)
    all16 = pltpu.VMEM((seq * slot, width), BF16)
    sums = [pltpu.VMEM((2, slot, width), BF16), own16, own16]
    scratch = buffers + [
        pltpu.VMEM(inner[1], F32),
        pltpu.VMEM(inner[2], F32),
        pltpu.VMEM((seq, plan.sub_pad, plan.units), BF16),
        pltpu.VMEM((seq, plan.sub_pad, mix), BF16),
        pltpu.VMEM((seq, 16, vec_pad), BF16),
        pltpu.VMEM((seq, plan.sub_pad, plan.units), BF16),
        pltpu.VMEM((seq, plan.sub_pad, mix), BF16),
        pltpu.VMEM((img * plan.rows_pad, mix), BF16),
        pltpu.VMEM((img * 16, vec_pad), BF16),
        pltpu.VMEM((img * 16, vec_pad), F32),
        pltpu.VMEM((1, 2 * width), F32),
        pltpu.VMEM((1, plan.shard_vec * plan.devices - 2 * width), F32),
        pltpu.VMEM((1, cols), F32),
        pltpu.VMEM((1, cols), F32),
        *sums,
        *sums,
        *sums,
        own16,
        all16,
        pltpu.VMEM((slot, width), F32),
        pltpu.VMEM((seq * slot, cols), BF16),
        pltpu.VMEM((seq * slot, plan.qkv_cols), BF16),
        all16,
        pltpu.VMEM((seq * slot, cols), BF16),
        *[dma((n, line))] * 6,
        *[dma((3, seq))] * 2,
        *[dma((3, 3))] * 2,
        *[dma((3,))] * 2,
    ]
    return pl.pallas_call(
        functools.partial(backward_kernel, plan, parts, heads),
        out_shape=(
            shape((slot, width), BF16),
            shape((slot, width), F32),
            shape((plan.block, width), F32),
            shape((plan.sub, plan.hidden), F32),
            shape((plan.sub, 3 * width), F32),
            shape((plan.sub, width), F32),
            shape((seq, 16, vec_pad), BF16),
        ),
        in_specs=[vmem] * len(BackwardIn._fields),
        out_specs=(vmem,) * len(BackwardOut._fields),
        scratch_shapes=scratch,
        compiler_params=pltpu.CompilerParams(
            collective_id=1, has_side_effects=True, vmem_limit_bytes=VMEM_LIMIT
        ),
        name="backward",
    )(*[args[name] for name in BackwardIn._fields])


def ffn_kernel(
    ln2, fc1, bias, fc2, cot, ok, g2, g1, ln2_part, out_part, sums, grad_y, acc_ln2, acc_out
):
    step = pl.program_id(0)

    @pl.when(step == 0)
    def _():
        grad_y[...] = jnp.where(ok[...] > 0, cot[...].astype(F32), 0.0).astype(BF16)
        acc_ln2[...] = jnp.zeros_like(acc_ln2)
        acc_out[...] = jnp.zeros_like(acc_out)

    pre = jnp.dot(ln2[...], fc1[...], preferred_element_type=F32) + bias[...]
    value, slope = gelu_parts(pre)
    act = value.astype(BF16)
    grad_pre = dot_t(grad_y[...], fc2[...]) * slope
    grad_pre16 = grad_pre.astype(BF16)
    sums[...] = jnp.sum(grad_pre, axis=0, keepdims=True)
    acc_out[...] += jnp.dot(act, fc2[...], preferred_element_type=F32)
    acc_ln2[...] += dot_t(grad_pre16, fc1[...])
    g2[...] = dot_00(act, grad_y[...]).astype(BF16)
    g1[...] = dot_00(ln2[...], grad_pre16).astype(BF16)

    @pl.when(step == pl.num_programs(0) - 1)
    def _():
        ln2_part[...] = acc_ln2[...].astype(BF16)
        out_part[...] = acc_out[...].astype(BF16)


def feed_forward(ln2, fc1, bias, fc2, cot, ok):
    tokens, width = ln2.shape
    units = fc2.shape[0]
    by = 3 * LANES if units % (3 * LANES) == 0 else LANES
    shape = jax.ShapeDtypeStruct

    def whole(*dims):
        return pl.BlockSpec(dims, lambda i: (0, 0))

    columns = pl.BlockSpec((width, by), lambda i: (0, i))
    rows = pl.BlockSpec((by, width), lambda i: (i, 0))
    row = pl.BlockSpec((1, by), lambda i: (0, i))
    return pl.pallas_call(
        ffn_kernel,
        grid=(units // by,),
        out_shape=(
            shape((units, width), BF16),
            shape((width, units), BF16),
            shape((tokens, width), BF16),
            shape((tokens, width), BF16),
            shape((1, units), F32),
        ),
        in_specs=[
            whole(tokens, width),
            columns,
            row,
            rows,
            whole(tokens, width),
            whole(tokens, 1),
        ],
        out_specs=(rows, columns, whole(tokens, width), whole(tokens, width), row),
        scratch_shapes=[
            pltpu.VMEM((tokens, width), BF16),
            pltpu.VMEM((tokens, width), F32),
            pltpu.VMEM((tokens, width), F32),
        ],
        compiler_params=pltpu.CompilerParams(
            dimension_semantics=("arbitrary",), vmem_limit_bytes=VMEM_LIMIT
        ),
        name="feed_forward",
    )(ln2, fc1, bias, fc2, cot, ok)


def normalize(values):
    mean = jnp.mean(values, axis=-1, keepdims=True)
    centred = values - mean
    rstd = lax.rsqrt(jnp.mean(centred * centred, axis=-1, keepdims=True) + EPS)
    return (centred * rstd, rstd)


def gelu_parts(pre):
    inner = GELU_C * (pre + 0.044715 * pre * pre * pre)
    tanh_v = jnp.tanh(inner)
    value = 0.5 * pre * (1.0 + tanh_v)
    slope = 0.5 * (1.0 + tanh_v) + 0.5 * pre * (1.0 - tanh_v * tanh_v) * GELU_C * (
        1.0 + 3.0 * 0.044715 * pre * pre
    )
    return (value, slope)


def gather(value, axes):
    return lax.all_gather(value, axes, axis=0, tiled=True)


def scatter_sum(value, axes):
    return lax.psum_scatter(value, axes, scatter_dimension=0, tiled=True)


def weight_grad(left, right):
    return lax.dot_general(
        left, right, (((0,), (0,)), ((), ())), preferred_element_type=F32
    ).astype(BF16)


def batched(left, right, over_left, over_right):
    return lax.dot_general(
        left,
        right,
        (((over_left,), (over_right,)), ((0,), (0,))),
        preferred_element_type=F32,
    )


TILE = 2048


def pack(flat):
    padded = round_up(flat.shape[0], TILE)
    return jnp.pad(flat, (0, padded - flat.shape[0])).reshape(-1, LANES)


def unpack_blocks(packed, blocks, length):
    return packed.reshape(blocks, -1)[:, :length].reshape(-1)


def pack_blocks(flat, blocks):
    block = flat.reshape(blocks, -1)
    padded = round_up(block.shape[1], TILE)
    return jnp.pad(block, ((0, 0), (0, padded - block.shape[1]))).reshape(-1, LANES)


def shards_by_rows(tokens, counts, w_qkv, w_out, w_fc1, w_fc2, vectors, cotangent):
    f32 = jnp.float32
    bf16 = jnp.bfloat16
    width = tokens.shape[2]
    slot = tokens.shape[1]
    scale = HEAD_DIM ** (-0.5)
    position = lax.axis_index("seq")
    seq_count = lax.axis_size("seq")
    img_count = lax.axis_size("img")
    device_count = img_count * seq_count
    both = ("img", "seq")
    shard_qkv, shard_out, shard_fc1, shard_fc2, shard_vec = (
        w.shape[0] for w in (w_qkv, w_out, w_fc1, w_fc2, vectors)
    )
    hidden = shard_fc1 * device_count // width
    heads = HEADS // seq_count
    cols = width // seq_count
    units = hidden // seq_count
    rows = width // img_count
    pad_cols = round_up(3 * cols, LANES) - 3 * cols
    pad_units = round_up(units, LANES) - units
    to_quarter = [(c, (c % img_count) * seq_count + c // img_count) for c in range(device_count)]
    to_owner = [(b, a) for a, b in to_quarter]

    slice_counts = counts[0]
    key_valid = (jnp.arange(slot)[None, :] < slice_counts[:, None]).reshape(-1)
    row_valid = lax.dynamic_slice_in_dim(key_valid, position * slot, slot)
    rowmask = row_valid.astype(f32)[:, None]

    def mine(values):
        return lax.dynamic_slice_in_dim(values, position * slot, slot)

    shard_ov = shard_out + shard_vec
    local = gather(pack(jnp.concatenate([w_qkv, w_fc1, w_out, vectors])), "seq")
    local = local.reshape(seq_count, -1)
    x_all16 = gather(tokens[0], "seq")
    qkv_rows = local[:, :shard_qkv].reshape(rows, 3 * width)
    fc1_rows = local[:, shard_qkv : shard_qkv + shard_fc1].reshape(rows, hidden)
    ov_flat = local[:, shard_qkv + shard_fc1 : shard_qkv + shard_fc1 + shard_ov].reshape(-1)
    ov_cols = round_up(-(-ov_flat.shape[0] // rows), LANES)
    ov_part = jnp.pad(ov_flat, (0, rows * ov_cols - ov_flat.shape[0])).reshape(rows, ov_cols)
    qkv_part = jnp.concatenate(
        [
            lax.dynamic_slice_in_dim(qkv_rows, j * width + position * cols, cols, axis=1)
            for j in range(3)
        ]
        + [jnp.zeros((rows, pad_cols), bf16)],
        axis=1,
    )
    fc1_part = jnp.pad(
        lax.dynamic_slice_in_dim(fc1_rows, position * units, units, axis=1),
        ((0, 0), (0, pad_units)),
    )
    fc2_chunk = lax.ppermute(pack(w_fc2), both, to_quarter).reshape(-1)[:shard_fc2]
    fc2_part = jnp.pad(fc2_chunk.reshape(rows, units), ((0, 0), (0, pad_units)))
    weights = gather(jnp.concatenate([qkv_part, fc1_part, fc2_part, ov_part], axis=1), "img")
    end_qkv = 3 * cols + pad_cols
    end_fc1 = end_qkv + units + pad_units
    end_fc2 = end_fc1 + units + pad_units
    mat_qkv = weights[:, :end_qkv]
    mat_fc1 = weights[:, end_qkv:end_fc1]
    mat_fc2 = jnp.pad(
        weights[:, end_fc1 : end_fc1 + units].reshape(units, width), ((0, pad_units), (0, 0))
    )
    out_vec = weights[:, end_fc2:].reshape(img_count, -1)[:, : seq_count * shard_ov]
    cot_all = gather(cotangent[0], "seq")

    blocks_ov = out_vec.reshape(device_count, -1)
    mat_out = blocks_ov[:, :shard_out].reshape(width, width)
    vec = blocks_ov[:, shard_out : shard_out + shard_vec].reshape(-1).astype(f32)
    bias1, v_bias, gain1, q_bias, out_bias, gain2, bias2, fc2_bias = (
        vec[i * width : (i + 1) * width] for i in range(8)
    )
    fc1_bias = vec[8 * width : 8 * width + hidden]

    def my_cols(values):
        return lax.dynamic_slice_in_dim(values, position * cols, cols)

    fc1_bias_mine = jnp.pad(
        lax.dynamic_slice_in_dim(fc1_bias, position * units, units), (0, pad_units)
    )

    x = x_all16.astype(f32)
    normed1, _ = normalize(x)
    ln1 = (normed1 * gain1 + bias1).astype(bf16)
    qkv = jnp.dot(ln1, mat_qkv, preferred_element_type=f32)

    def by_head(values):
        return values.reshape(-1, heads, HEAD_DIM).transpose(1, 0, 2)

    def by_slot(values):
        return values.transpose(1, 0, 2).reshape(-1, cols)

    queries = by_head((qkv[:, :cols] + my_cols(q_bias)).astype(bf16))
    keys = by_head(qkv[:, cols : 2 * cols].astype(bf16))
    values = by_head((qkv[:, 2 * cols : 3 * cols] + my_cols(v_bias)).astype(bf16))
    scores = batched(queries, keys, 2, 2) * scale
    scores = jnp.where(key_valid[None, None, :], scores, -1e30)
    top = jnp.max(scores, axis=-1, keepdims=True)
    lse = top + jnp.log(jnp.sum(jnp.exp(scores - top), axis=-1, keepdims=True))
    probs = jnp.exp(scores - lse).astype(bf16)
    mixed_heads = batched(probs, values, 2, 1)
    mixed_mine = by_slot(mixed_heads).astype(bf16)
    mixed = lax.all_gather(mixed_mine, "seq", axis=0, tiled=True)
    mixed = (
        mixed.reshape(seq_count, -1, cols).transpose(1, 0, 2).reshape(-1, width)
    )
    resid = x + jnp.dot(mixed, mat_out, preferred_element_type=f32) + out_bias
    normed2, rstd2 = normalize(resid)
    ln2 = (normed2 * gain2 + bias2).astype(bf16)
    pre = jnp.dot(ln2, mat_fc1, preferred_element_type=f32) + fc1_bias_mine
    act_f, slope = gelu_parts(pre)
    act = act_f.astype(bf16)

    grad_y16 = jnp.where(key_valid[:, None], cot_all, jnp.zeros((), bf16))
    grad_pre = dot_t(grad_y16, mat_fc2) * slope
    grad_pre16 = grad_pre.astype(bf16)
    grad_ln2 = scatter_sum(dot_t(grad_pre16, mat_fc1).astype(bf16), "seq").astype(f32)
    grad_y = cotangent[0].astype(f32) * rowmask
    normed2_mine = mine(normed2)
    grad_resid = grad_y + norm_back(grad_ln2, normed2_mine, mine(rstd2), gain2)
    grad_resid16 = gather(grad_resid.astype(bf16), "seq")

    part_fc1 = weight_grad(ln2, grad_pre16)
    part_fc2 = pack_blocks(weight_grad(act, grad_y16)[:units].reshape(-1), img_count)
    out_terms = scatter_sum(
        jnp.dot(act, mat_fc2, preferred_element_type=f32).astype(bf16), "seq"
    ).astype(f32)
    output = ((mine(resid) + out_terms + fc2_bias) * rowmask).astype(bf16)

    out_mine = lax.dynamic_slice_in_dim(mat_out, position * cols, cols)
    gm = by_head(dot_t(grad_resid16, out_mine).astype(bf16))
    mixed_back = by_head(mixed_mine)
    delta = jnp.sum(gm.astype(f32) * mixed_back.astype(f32), axis=-1, keepdims=True)
    grad_values = by_slot(batched(probs, gm, 1, 1))
    dots = batched(gm, values, 2, 2)
    grad_scores = (jnp.exp(scores - lse) * (dots - delta) * scale).astype(bf16)
    grad_queries = by_slot(batched(grad_scores, keys, 2, 1))
    grad_keys = by_slot(batched(grad_scores, queries, 1, 1))
    grad_qkv16 = jnp.concatenate(
        [grad_queries.astype(bf16), grad_keys.astype(bf16), grad_values.astype(bf16)]
        + [jnp.zeros((seq_count * slot, pad_cols), bf16)],
        axis=1,
    )
    grad_ln1 = scatter_sum(dot_t(grad_qkv16, mat_qkv).astype(bf16), "seq").astype(f32)
    part_qkv = weight_grad(ln1, grad_qkv16)
    part_out = pack_blocks(weight_grad(mixed_mine, grad_resid16).reshape(-1), img_count)
    normed1_mine, rstd1_mine = normalize(tokens[0].astype(f32))
    input_grad = grad_resid + norm_back(grad_ln1, normed1_mine, rstd1_mine, gain1)

    def spread(part, full):
        return lax.dynamic_update_slice_in_dim(
            jnp.zeros((full,), f32), part, position * part.shape[0], 0
        )

    shard_front = 2 * width // device_count
    unused = shard_vec * device_count - 8 * width - hidden
    g_front = jnp.concatenate(
        [jnp.sum(grad_ln1, axis=0), spread(jnp.sum(grad_values, axis=0), width)]
    )
    g_rest = jnp.concatenate(
        [
            jnp.sum(grad_ln1 * normed1_mine, axis=0),
            spread(jnp.sum(grad_queries, axis=0), width),
            jnp.sum(grad_resid, axis=0),
            jnp.sum(grad_ln2 * normed2_mine, axis=0),
            jnp.sum(grad_ln2, axis=0),
            jnp.sum(grad_y, axis=0),
            spread(jnp.sum(grad_pre, axis=0)[:units], hidden),
            jnp.zeros((unused,), f32),
        ]
    )
    g_vec = jnp.concatenate(
        [g_front.reshape(device_count, -1), g_rest.reshape(device_count, -1)], axis=1
    )
    vec_pad = round_up(shard_vec, 4 * LANES)
    part_vec = jnp.pad(g_vec, ((0, 0), (0, vec_pad - shard_vec))).astype(bf16)

    parts = [
        part.reshape(img_count, -1, LANES)
        for part in (part_qkv, part_fc1, part_vec, part_fc2, part_out)
    ]
    sizes = [part.shape[1] for part in parts]
    summed = scatter_sum(jnp.concatenate(parts, axis=1).reshape(-1, LANES), "img")
    ends = [sum(sizes[: i + 1]) for i in range(5)]
    chunks = lax.ppermute(summed[ends[2] :], both, to_owner)
    grad_fc2 = chunks[: sizes[3]].reshape(-1)[:shard_fc2].astype(f32)
    grad_out = chunks[sizes[3] :].reshape(-1)[:shard_out].astype(f32)
    shared = gather(summed[: ends[2]], "seq").reshape(seq_count, ends[2], LANES)

    def own_block(packed, thirds, used, size):
        blocks = packed.reshape(seq_count, rows, -1)[:, :, : thirds * used]
        whole = blocks.reshape(seq_count, rows, thirds, used).transpose(1, 2, 0, 3)
        return lax.dynamic_slice_in_dim(whole.reshape(-1), position * size, size).astype(f32)

    grad_qkv = own_block(shared[:, : ends[0]], 3, cols, shard_qkv)
    grad_fc1 = own_block(shared[:, ends[0] : ends[1]], 1, units, shard_fc1)
    vec_sums = jnp.sum(shared[:, ends[1] :].astype(f32), axis=0).reshape(seq_count, vec_pad)
    vec_mine = lax.dynamic_slice_in_dim(vec_sums, position, 1).reshape(-1)
    return (
        output[None],
        input_grad[None],
        grad_qkv,
        grad_out,
        grad_fc1,
        grad_fc2,
        vec_mine[shard_front:shard_vec],
        vec_mine[:shard_front],
    )


def shards(tokens, counts, w_qkv, w_out, w_fc1, w_fc2, vectors, cotangent):
    width = tokens.shape[2]
    slot = tokens.shape[1]
    scale = HEAD_DIM ** (-0.5)
    position = lax.axis_index("seq")
    seq_count = lax.axis_size("seq")
    img_count = lax.axis_size("img")
    device_count = img_count * seq_count
    chunk = lax.axis_index("img") * seq_count + position
    shard_vec = vectors.shape[0]
    plan = Plan(img_count, seq_count, width, w_fc1.shape[0], shard_vec)
    hidden, cols, rows, units = plan.hidden, plan.cols, plan.rows, plan.units
    heads = HEADS // seq_count
    shard_fc = plan.shard_fc

    slice_counts = counts[0]
    key_valid = (jnp.arange(slot)[None, :] < slice_counts[:, None]).reshape(-1)
    row_valid = lax.dynamic_slice_in_dim(key_valid, position * slot, slot)
    rowmask = row_valid.astype(F32)[:, None]
    key_ok = key_valid.astype(F32)[None]

    shifts = sorted({g * shard_fc % width for g in range(device_count)})
    shift = lax.rem(chunk * shard_fc, width)
    fc2_flat = jnp.zeros((), BF16)
    for by in shifts:
        placed = jnp.pad(w_fc2, (by, plan.block * width - by - shard_fc))
        fc2_flat = jnp.where(shift == by, placed, fc2_flat)
    ov = jnp.pad(w_out.reshape(plan.sub, width), ((0, plan.sub_pad - plan.sub), (0, 0)))
    vec_in = jnp.pad(vectors[None], ((0, 15), (0, round_up(shard_vec, LANES) - shard_vec)))
    f = forward(
        plan,
        slot,
        heads,
        dict(
            qkv=w_qkv.reshape(plan.sub, 3 * width),
            fc1=w_fc1.reshape(plan.sub, hidden),
            fc2=fc2_flat.reshape(plan.block, width),
            ov=ov,
            vec_in=vec_in,
            x=tokens[0],
            cot=cotangent[0],
            key_ok=key_ok,
        ),
    )
    mat_fc1 = f.wf1.reshape(width, units)
    mat_fc2 = f.wf2.reshape(units, width)
    cot_all = f.cots.reshape(seq_count * slot, width)
    part_fc2, part_fc1, ln2_part, out_part, pre_sums = feed_forward(
        f.ln2, mat_fc1, f.fc1_bias, mat_fc2, cot_all, key_valid.astype(F32)[:, None]
    )
    output, input_grad, grad2, grad1, gradq, grado, gradv = backward(
        plan,
        slot,
        heads,
        dict(
            g2=part_fc2,
            g1=part_fc1,
            ln2_part=ln2_part,
            out_part=out_part,
            grad_y=cotangent[0].astype(F32) * rowmask,
            rowmask=rowmask,
            key_ok=key_ok,
            pre_sums=pre_sums,
            **{name: getattr(f, name) for name in BackwardIn._fields if name in ForwardOut._fields},
        ),
    )
    grad_fc2 = lax.dynamic_slice_in_dim(grad2.reshape(-1), shift, shard_fc)
    shard_front = 2 * width // device_count
    vec_sums = jnp.sum(gradv.astype(F32), axis=0)
    vec_mine = lax.dynamic_slice_in_dim(vec_sums, position, 1).reshape(-1)
    return (
        output[None],
        input_grad[None],
        gradq.reshape(-1),
        grado.reshape(-1),
        grad1.reshape(-1),
        grad_fc2,
        vec_mine[shard_front:shard_vec],
        vec_mine[:shard_front],
    )


def solution(mesh):
    def layer(*arrays):
        width = arrays[0].shape[2]
        whole_rows = (
            width % mesh.size == 0
            and mesh.shape["seq"] == 4
            and width // mesh.shape["img"] % 16 == 0
        )
        return (shards if whole_rows else shards_by_rows)(*arrays)

    return jax.shard_map(
        layer,
        mesh=mesh,
        in_specs=(
            P("img", "seq", None),
            P("img", None),
            P(("img", "seq")),
            P(("img", "seq")),
            P(("img", "seq")),
            P(("img", "seq")),
            P(("img", "seq")),
            P("img", "seq", None),
        ),
        out_specs=(
            P("img", "seq", None),
            P("img", "seq", None),
            P(("img", "seq")),
            P(("img", "seq")),
            P(("img", "seq")),
            P(("img", "seq")),
            P(("img", "seq")),
            P(("img", "seq")),
        ),
        check_vma=False,
    )
```
